32 devices in a mesh: parts: 2 (over y), replica: 4 (over x, core), tensor: 4 (over z).
Axes of the slice: x: 2, y: 2, z: 4, core: 2. Of those that a mesh axis runs over, the one named last changes fastest.
Arguments:
- prompt_owner: int32 [8], P('parts'), parts along dimension 0, may hold values from 0 to 3, each once
- fork_map: int32 [1024], P(('parts', 'replica')), parts along dimension 0, may hold values from 0 to 3
- page_table: int32 [24], P('parts'), parts along dimension 0, may hold values from 0 to 11, each once
- prompt_length: int32 [8], P('parts'), parts along dimension 0, may hold values from 1 to 384
- span_states: bfloat16 [1024, 8192], P(('parts', 'replica'), 'tensor'), parts along dimension 0, may hold values from -6 to 6
- decode_states: bfloat16 [1024, 4, 8192], P(('parts', 'replica'), None, 'tensor'), parts along dimension 0, may hold values from -6 to 6
- decode_queries: bfloat16 [1024, 4, 4096], P(('parts', 'replica'), None, 'tensor'), parts along dimension 0, may hold values from -64 to 64
- key_weight: bfloat16 [8192, 512], P('tensor'), may hold values from -0.0625 to 0.0625
- value_weight: bfloat16 [8192, 512], P('tensor'), may hold values from -0.0625 to 0.0625
- out_weight: bfloat16 [4096, 8192], P(None, 'tensor'), may hold values from -0.09375 to 0.09375
- page_pool: bfloat16 [4, 24, 128, 256], P('tensor', 'parts'), parts along dimension 1, may hold values from -6 to 60, as said below
Outputs:
- decoded: bfloat16 [1024, 4, 8192], P(('parts', 'replica'), None, 'tensor'), parts along dimension 0
The draws below stay inside these ranges and needn't reach their ends.
There are 2 independent parts, one for each index of `parts`. The reference program is written for one: setup_inputs(seed, part) draws one part's arguments, and reference() takes and returns one part's arrays. A program takes and returns all parts, laid end to end along the dimension named above; an argument that names none is the same for every part. Nothing has to cross between parts.
Inputs may be any that keep to these rules, and one draw needn't show every extreme that they name: Replica r prefills prompt prompt_owner[r]; every prompt has exactly one such replica. The cache pages of prompt p are page_table[p * 3 + c] for c below 3; every pool page belongs to exactly one prompt. page_pool[t] holds the cache of key-value head t; devices that read the same head hold equal copies.
All inputs are finite; a program needn't handle non-finite values.
Results may differ from the reference program's by a relative error of at most 0.009.
Values may be sent and summed in bfloat16 or wider, within the bound.
No kernel may reach another device: no remote copies, remote signals or barrier semaphores. Data moves between devices by JAX's collectives and lax.ppermute only.
A program may use at most 64 MiB of HBM per device.

```python
import jax
import jax.numpy as jnp
from jax import lax

D = 8192
HD = 128
HEADS = 32
KVH = 4
SPAN = 128
STEPS = 4
PAGE = 128
CPAGES = 3
ROWS = 128
SHARE = 1
POOL = 12
ALL_ROWS = 512
ALL_SPAN = 512
N_REPLICA = 4


def draw_page_pool(key, part):
    base = jnp.clip(jax.random.normal(key, (KVH, POOL, PAGE, 2 * HD), jnp.float32), -6.0, 6.0)
    return jnp.repeat(base, SHARE, axis=0).astype(jnp.bfloat16)


def draw_decode_queries(key, part):
    base = jnp.clip(jax.random.normal(key, (ALL_ROWS, STEPS, HEADS, HD), jnp.float32), -6.0, 6.0)
    return base.reshape(ALL_ROWS, STEPS, HEADS * HD).astype(jnp.bfloat16)


def set_ends(drawn, key, smallest, high):
    index_at = [jax.random.randint(jax.random.fold_in(key, axis), (), 0, length) for axis, length in enumerate(drawn.shape)]
    main_axis = drawn.shape.index(max(drawn.shape))
    next_to = index_at[:main_axis] + [(index_at[main_axis] + 1) % drawn.shape[main_axis]] + index_at[main_axis + 1:]
    return drawn.at[tuple(index_at)].set(smallest).at[tuple(next_to)].set(high)


def steps_of(rng, extent, cuts, low, top_value):
    def one(axis_at, shards_of):
        heights = jax.random.uniform(jax.random.fold_in(jax.random.fold_in(rng, 6), axis_at), (shards_of,), jnp.float32, low / len(cuts), top_value / len(cuts))
        return jnp.repeat(jnp.exp(heights), extent[axis_at] // shards_of).reshape((-1,) + (1,) * (len(extent) - axis_at - 1))

    loudness = one(*cuts[0])
    for cut in cuts[1:]:
        loudness = loudness * one(*cut)
    return loudness


def normal_values(key, shape, spread, bound, cuts=(), kind=jnp.bfloat16):
    values = spread * jax.random.normal(key, shape, jnp.float32)
    if cuts:
        values = values * steps_of(key, shape, cuts, -0.22, 0.18)
    return jnp.clip(values, -bound, bound).astype(kind)


def setup_inputs(seed: int = 0, part: int = 0) -> dict:
    key_list = jax.random.split(jax.random.key(seed), 12)
    part_splits = jax.random.split(jax.random.fold_in(key_list[11], part), 12)
    prompt_owner = jax.random.permutation(part_splits[0], N_REPLICA).astype(jnp.int32)
    fork_map = set_ends(jax.random.randint(part_splits[1], (ALL_ROWS,), 0, N_REPLICA), jax.random.fold_in(part_splits[1], 1), 0, N_REPLICA - 1).astype(jnp.int32)
    page_table = jax.random.permutation(part_splits[2], POOL).astype(jnp.int32)
    prompt_length = set_ends(jax.random.randint(part_splits[3], (N_REPLICA,), 1, CPAGES * PAGE + 1), jax.random.fold_in(part_splits[3], 1), 1, CPAGES * PAGE).astype(jnp.int32)
    span_states = normal_values(part_splits[4], (ALL_SPAN, D), 1.0, 6.0, ((0, 4), (1, 4)))
    decode_states = normal_values(part_splits[5], (ALL_ROWS, STEPS, D), 1.0, 6.0, ((0, 4), (2, 4)))
    decode_queries = draw_decode_queries(jax.random.fold_in(jax.random.fold_in(key_list[11], part), 71), part)
    key_weight = normal_values(key_list[7], (D, KVH * HD), D ** -0.5, 0.0625, ((0, 4),))
    value_weight = normal_values(key_list[8], (D, KVH * HD), D ** -0.5, 0.0625, ((0, 4),))
    out_weight = normal_values(key_list[9], (HEADS * HD, D), (HEADS * HD) ** -0.5, 0.09375, ((1, 4),))
    page_pool = draw_page_pool(jax.random.fold_in(jax.random.fold_in(key_list[11], part), 71), part)
    return dict(prompt_owner=prompt_owner, fork_map=fork_map, page_table=page_table, prompt_length=prompt_length, span_states=span_states, decode_states=decode_states, decode_queries=decode_queries, key_weight=key_weight, value_weight=value_weight, out_weight=out_weight, page_pool=page_pool)


rope_base = 1000000.0


def rotary(vectors, places):
    half = vectors.shape[-1] // 2
    freq = rope_base ** (-(2.0 / vectors.shape[-1]) * jnp.arange(half, dtype=jnp.float32))
    angle = places.astype(jnp.float32)[..., None, None] * freq
    cosine = jnp.cos(angle)
    sine = jnp.sin(angle)
    first = vectors[..., :half]
    second = vectors[..., half:]
    return jnp.concatenate([first * cosine - second * sine, second * cosine + first * sine], -1)


def reference(prompt_owner, fork_map, page_table, prompt_length, span_states, decode_states, decode_queries, key_weight, value_weight, out_weight, page_pool):
    weights = jnp.concatenate([key_weight, value_weight], 1)
    tokens = jnp.concatenate([span_states, decode_states.reshape(ALL_ROWS * STEPS, D)], 0)
    projected = jnp.dot(tokens, weights, preferred_element_type=jnp.float32)
    span_places = prompt_length[prompt_owner][:, None] + jnp.arange(SPAN, dtype=jnp.int32)[None, :]
    tail_places = prompt_length[fork_map][:, None] + SPAN + jnp.arange(STEPS, dtype=jnp.int32)[None, :]
    positions = jnp.concatenate([span_places.reshape(-1), tail_places.reshape(-1)]).astype(jnp.int32)
    number = positions.shape[0]
    new_keys = rotary(projected[:, :KVH * HD].reshape(number, KVH, HD), positions).astype(jnp.bfloat16)
    new_values = projected[:, KVH * HD:].reshape(number, KVH, HD).astype(jnp.bfloat16)
    span_keys = new_keys[:ALL_SPAN]
    span_values = new_values[:ALL_SPAN]
    tail_keys = new_keys[ALL_SPAN:].reshape(N_REPLICA, ROWS, STEPS, KVH, HD)
    tail_values = new_values[ALL_SPAN:].reshape(N_REPLICA, ROWS, STEPS, KVH, HD)
    entries = jnp.arange(POOL, dtype=jnp.int32)
    page_prompt = jnp.zeros((POOL,), jnp.int32).at[page_table].set(entries // CPAGES)
    page_slot = jnp.zeros((POOL,), jnp.int32).at[page_table].set(entries % CPAGES)
    cached_places = page_slot[:, None] * PAGE + jnp.arange(PAGE, dtype=jnp.int32)[None, :]
    visible = cached_places < prompt_length[page_prompt][:, None]
    pool_prompt = jnp.where(visible, page_prompt[:, None], -1).reshape(-1)
    key_prompt = jnp.concatenate([pool_prompt, jnp.repeat(prompt_owner, SPAN)]).astype(jnp.int32)
    group = HEADS // KVH
    scale = HD ** -0.5
    causal = jnp.arange(STEPS)[None, :] <= jnp.arange(STEPS)[:, None]
    queries = decode_queries.reshape(N_REPLICA, ROWS, STEPS, HEADS, HD)
    row_prompts = fork_map.reshape(N_REPLICA, ROWS)

    def one_replica(items):
        query, prompt, own_keys, own_values = items
        pieces = []
        for head_group in range(KVH):
            cache = page_pool[head_group * SHARE].reshape(POOL * PAGE, 2 * HD)
            key_table = jnp.concatenate([cache[:, :HD], span_keys[:, head_group]], 0).astype(jnp.float32)
            value_table = jnp.concatenate([cache[:, HD:], span_values[:, head_group]], 0).astype(jnp.float32)
            local = query[:, :, head_group * group:(head_group + 1) * group].astype(jnp.float32)
            scores = jnp.einsum("rshd,kd->rshk", local, key_table) * scale
            allowed = (key_prompt[None, :] == prompt[:, None])[:, None, None, :]
            scores = jnp.where(allowed, scores, -jnp.inf)
            tail_key = own_keys[:, :, head_group].astype(jnp.float32)
            tail_value = own_values[:, :, head_group].astype(jnp.float32)
            tail = jnp.einsum("rshd,rtd->rsht", local, tail_key) * scale
            tail = jnp.where(causal[None, :, None, :], tail, -jnp.inf)
            highest = jnp.maximum(jnp.max(scores, -1), jnp.max(tail, -1))
            weight = jnp.exp(scores - highest[..., None])
            tail_weight = jnp.exp(tail - highest[..., None])
            total = jnp.sum(weight, -1) + jnp.sum(tail_weight, -1)
            mixed = jnp.einsum("rshk,kd->rshd", weight.astype(jnp.bfloat16).astype(jnp.float32), value_table)
            mixed = mixed + jnp.einsum("rsht,rtd->rshd", tail_weight.astype(jnp.bfloat16).astype(jnp.float32), tail_value)
            pieces.append((mixed / total[..., None]).astype(jnp.bfloat16))
        return jnp.concatenate(pieces, 2)

    attended = lax.map(one_replica, (queries, row_prompts, tail_keys, tail_values))
    flat = attended.reshape(ALL_ROWS * STEPS, HEADS * HD)
    decoded = jnp.dot(flat, out_weight, preferred_element_type=jnp.float32).astype(jnp.bfloat16)
    return decoded.reshape(ALL_ROWS, STEPS, D)
```

```python
import functools
import math

import jax
import jax.numpy as jnp
from jax import lax
from jax.experimental import pallas as pl
from jax.experimental.pallas import tpu as pltpu
from jax.sharding import PartitionSpec as P

HD = 128
rope_base = 1000000.0
LOG2E = math.log2(math.e)
HIDDEN = -1e30


def rotary(vectors, places):
    half = vectors.shape[-1] // 2
    freq = rope_base ** (-(2.0 / vectors.shape[-1]) * jnp.arange(half, dtype=jnp.float32))
    angle = places.astype(jnp.float32)[..., None, None] * freq
    cosine = jnp.cos(angle)
    sine = jnp.sin(angle)
    first = vectors[..., :half]
    second = vectors[..., half:]
    return jnp.concatenate([first * cosine - second * sine, second * cosine + first * sine], -1)


def rotate_round(summed, places, kv_heads):
    number = summed.shape[0]
    turned = rotary(summed[:, : kv_heads * HD].reshape(number, kv_heads, HD), places)
    turned = turned.astype(jnp.bfloat16).reshape(number, kv_heads * HD)
    return jnp.concatenate([turned, summed[:, kv_heads * HD :].astype(jnp.bfloat16)], 1)


def own_pair(packed, head_group, kv_heads):
    key_part = lax.dynamic_slice_in_dim(packed, head_group * HD, HD, 1)
    value_part = lax.dynamic_slice_in_dim(packed, (kv_heads + head_group) * HD, HD, 1)
    return jnp.concatenate([key_part, value_part], 1)


def attend_kernel(heads, steps, scale2, q_ref, prompt_ref, keyp_ref, pool_ref, span_ref, tail_ref, o_ref):
    m = q_ref.shape[0]
    shared = keyp_ref.shape[1]
    cached = pool_ref.shape[0]
    bias = jnp.where(prompt_ref[...] == keyp_ref[...], 0.0, HIDDEN)
    row = lax.broadcasted_iota(jnp.int32, (m, m), 0)
    col = lax.broadcasted_iota(jnp.int32, (m, m), 1)
    own = (row // steps == col // steps) & (col <= row)
    tail_bias = jnp.where(own, 0.0, HIDDEN)
    nt = (((1,), (1,)), ((), ()))
    parts = (
        (pool_ref, bias[:, :cached]),
        (span_ref, bias[:, cached:shared]),
        (tail_ref, tail_bias),
    )
    for h in range(heads):
        q = q_ref[:, h * HD : (h + 1) * HD]
        scores = [
            lax.dot_general(q, ref[:, :HD], nt, preferred_element_type=jnp.float32) * scale2 + b
            for ref, b in parts
        ]
        top = functools.reduce(jnp.maximum, [jnp.max(s, 1, keepdims=True) for s in scores])
        weights = [jnp.exp2(s - top) for s in scores]
        total = sum(jnp.sum(w, 1, keepdims=True) for w in weights)
        mixed = sum(
            jnp.dot(w.astype(jnp.bfloat16), ref[:, HD:], preferred_element_type=jnp.float32)
            for w, (ref, _) in zip(weights, parts)
        )
        o_ref[:, h * HD : (h + 1) * HD] = (mixed / total).astype(jnp.bfloat16)


def attend(q, row_prompt, key_prompt, pool, span_pairs, tail_pairs, block, steps):
    rows, width = q.shape
    shared = key_prompt.shape[1]
    whole = lambda shape: pl.BlockSpec(shape, lambda i: (0, 0))
    kernel = functools.partial(attend_kernel, width // HD, steps, LOG2E / math.sqrt(HD))
    return pl.pallas_call(
        kernel,
        grid=(rows // block,),
        in_specs=[
            pl.BlockSpec((block, width), lambda i: (i, 0)),
            pl.BlockSpec((block, 1), lambda i: (i, 0)),
            whole((1, shared)),
            whole(pool.shape),
            whole(span_pairs.shape),
            pl.BlockSpec((block, 2 * HD), lambda i: (i, 0)),
        ],
        out_specs=pl.BlockSpec((block, width), lambda i: (i, 0)),
        out_shape=jax.ShapeDtypeStruct((rows, width), jnp.bfloat16),
        name="attend",
    )(q, row_prompt, key_prompt, pool, span_pairs, tail_pairs)


def project_kernel(rank_ref, x_ref, k_ref, v_ref, keep_ref, send_ref):
    j = pl.program_id(0)
    x = x_ref[...]
    unit = jnp.concatenate(
        [
            jnp.dot(x, k_ref[...], preferred_element_type=jnp.float32),
            jnp.dot(x, v_ref[...], preferred_element_type=jnp.float32),
        ],
        1,
    )

    @pl.when(j < 2)
    def _():
        send_ref[0] = unit.astype(jnp.bfloat16)

    @pl.when(j >= 2)
    def _():
        keep_ref[0] = unit


def project(rank, x, key_weight, value_weight):
    rows, width = x.shape
    def head(j, r):
        rel = 2 * (j % 2) + (1 - j // 2)
        return (0, r[0] ^ rel)

    spec = pl.BlockSpec((width, HD), head)
    return pl.pallas_call(
        project_kernel,
        grid_spec=pltpu.PrefetchScalarGridSpec(
            num_scalar_prefetch=1,
            grid=(4,),
            in_specs=[pl.BlockSpec((rows, width), lambda j, r: (0, 0)), spec, spec],
            out_specs=[
                pl.BlockSpec((1, rows, 2 * HD), lambda j, r: (jnp.maximum(j - 2, 0), 0, 0)),
                pl.BlockSpec((1, rows, 2 * HD), lambda j, r: (jnp.minimum(j, 1), 0, 0)),
            ],
        ),
        out_shape=[
            jax.ShapeDtypeStruct((2, rows, 2 * HD), jnp.float32),
            jax.ShapeDtypeStruct((2, rows, 2 * HD), jnp.bfloat16),
        ],
        name="project",
    )(rank, x, key_weight, value_weight)


def out_kernel(n, rank_ref, *refs):
    o_ref = refs[-1]
    total = None
    for a_ref, w_ref in zip(refs[:n], refs[n:-1]):
        one = jnp.dot(a_ref[...], w_ref[...], preferred_element_type=jnp.float32)
        total = one if total is None else total + one
    o_ref[...] = total.astype(jnp.bfloat16)


def out_project(rank, pieces, out_weight, tile):
    rows, width = pieces[0].shape
    n = len(pieces)
    columns = out_weight.shape[1]
    in_specs = [pl.BlockSpec((rows, width), lambda i, r: (0, 0)) for _ in pieces]
    for j in range(n):
        in_specs.append(pl.BlockSpec((width, tile), lambda i, r, j=j: (r[0] ^ j, i)))
    return pl.pallas_call(
        functools.partial(out_kernel, n),
        grid_spec=pltpu.PrefetchScalarGridSpec(
            num_scalar_prefetch=1,
            grid=(columns // tile,),
            in_specs=in_specs,
            out_specs=pl.BlockSpec((rows, tile), lambda i, r: (0, i)),
        ),
        out_shape=jax.ShapeDtypeStruct((rows, columns), jnp.bfloat16),
        name="out_project",
    )(rank, *pieces, *([out_weight] * n))


def swap(x, axis, bit):
    return lax.ppermute(x, axis, [(i, i ^ bit) for i in range(lax.axis_size(axis))])


def scatter_sum(keep, send, places):
    got = swap(send, "tensor", 1).astype(jnp.float32)
    half = keep + got
    last = swap(half[1].astype(jnp.bfloat16), "tensor", 2).astype(jnp.float32)
    return rotate_round(half[0] + last, places, 1)


def mask_tables(prompt_owner, page_table, prompt_length, page_size, span, order):
    n_replica = order.shape[0]
    prompts = jnp.arange(n_replica, dtype=jnp.int32)
    pool_pages = page_table.shape[0]
    cpages = pool_pages // n_replica
    entries = jnp.arange(pool_pages, dtype=jnp.int32)
    page_hits = page_table[None, :] == entries[:, None]
    page_prompt = jnp.sum(jnp.where(page_hits, entries[None, :] // cpages, 0), 1)
    page_slot = jnp.sum(jnp.where(page_hits, entries[None, :] % cpages, 0), 1)
    page_length = jnp.sum(
        jnp.where(page_prompt[:, None] == prompts[None, :], prompt_length[None, :], 0), 1
    )
    visible = (
        page_slot[:, None] * page_size + jnp.arange(page_size, dtype=jnp.int32)[None, :]
        < page_length[:, None]
    )
    pool_prompt = jnp.where(visible, page_prompt[:, None], -1).reshape(-1)
    owners = jnp.sum(jnp.where(order[:, None] == prompts[None, :], prompt_owner[None, :], 0), 1)
    return jnp.concatenate([pool_prompt, jnp.repeat(owners, span)])[None, :]


def gather_heads(own):
    rank = lax.axis_index("tensor")
    far = swap(own, "tensor", 2)
    near = swap(own, "tensor", 1)
    across = lax.ppermute(own, "tensor", [(1, 2), (2, 1)])
    passed = lax.ppermute(far, "tensor", [(1, 0), (2, 3)])
    inner = (rank == 1) | (rank == 2)
    return [own, near, far, jnp.where(inner, across, passed)]


def on_device(
    prompt_owner,
    fork_map,
    page_table,
    prompt_length,
    span_states,
    decode_states,
    decode_queries,
    key_weight,
    value_weight,
    out_weight,
    page_pool,
):
    replica = lax.axis_index("replica")
    device_rank = lax.axis_index("tensor")
    n_replica = lax.axis_size("replica")
    n_tensor = lax.axis_size("tensor")
    span = span_states.shape[0]
    rows, steps, width = decode_states.shape
    heads_dev = decode_queries.shape[2] // HD
    kv_heads = key_weight.shape[1] // HD
    sharing = n_tensor // kv_heads
    prompts = jnp.arange(n_replica, dtype=jnp.int32)
    own_prompt = jnp.sum(jnp.where(prompts == replica, prompt_owner, 0))
    own_length = jnp.sum(jnp.where(prompts == own_prompt, prompt_length, 0))
    row_hits = fork_map[:, None] == prompts[None, :]
    row_length = jnp.sum(jnp.where(row_hits, prompt_length[None, :], 0), 1)
    span_places = own_length + jnp.arange(span, dtype=jnp.int32)
    tail_places = (
        row_length[:, None] + span + jnp.arange(steps, dtype=jnp.int32)[None, :]
    ).reshape(-1)
    row_prompt = jnp.repeat(fork_map, steps)[:, None]
    pool = page_pool.reshape(-1, 2 * HD)
    queries = decode_queries.reshape(rows * steps, heads_dev * HD)
    short_line = n_tensor == kv_heads == 4 and n_replica == 4

    if short_line:
        rank = device_rank.reshape(1).astype(jnp.int32)
        span_keep, span_send = project(rank, span_states, key_weight, value_weight)
        tail_keep, tail_send = project(
            rank, decode_states.reshape(rows * steps, width), key_weight, value_weight
        )
        own_span = scatter_sum(span_keep, span_send, span_places)
        arrived = jnp.concatenate(
            [own_span] + [swap(own_span, "replica", j) for j in range(1, n_replica)], 0
        )
        order = replica ^ jnp.arange(n_replica, dtype=jnp.int32)
        tail_pairs = scatter_sum(tail_keep, tail_send, tail_places)
    else:
        positions = jnp.concatenate([span_places, tail_places])
        tokens = jnp.concatenate([span_states, decode_states.reshape(rows * steps, width)], 0)
        projected = jnp.dot(
            tokens,
            jnp.concatenate([key_weight, value_weight], 1),
            preferred_element_type=jnp.float32,
        )
        share = lax.psum_scatter(projected, "tensor", scatter_dimension=0, tiled=True)
        number = share.shape[0]
        places = lax.dynamic_slice_in_dim(positions, device_rank * number, number)
        turned = rotate_round(share, places, kv_heads)
        groups = jnp.stack([own_pair(turned, g, kv_heads) for g in range(kv_heads)], 0)
        outgoing = jnp.repeat(groups, sharing, axis=0)
        paired = lax.all_to_all(
            outgoing, "tensor", split_axis=0, concat_axis=1, tiled=True
        ).reshape(-1, 2 * HD)
        arrived = lax.all_gather(paired[:span], "replica", axis=0, tiled=True)
        order = jnp.arange(n_replica, dtype=jnp.int32)
        tail_pairs = paired[span:]

    key_prompt = mask_tables(
        prompt_owner, page_table, prompt_length, page_pool.shape[2], span, order
    )
    block = min(rows, 32) * steps
    chunks = rows * steps // block
    outs = []
    for c in range(chunks):
        part = slice(c * block, (c + 1) * block)
        own = attend(
            queries[part], row_prompt[part], key_prompt, pool, arrived, tail_pairs[part], block, steps
        )
        if short_line:
            outs.append(out_project(rank, gather_heads(own), out_weight, 512))
        else:
            outs.append(
                jnp.dot(
                    lax.all_gather(own, "tensor", axis=1, tiled=True),
                    out_weight,
                    preferred_element_type=jnp.float32,
                ).astype(jnp.bfloat16)
            )
    return jnp.concatenate(outs, 0).reshape(rows, steps, width)


def solution(mesh):
    in_specs = (
        P("parts"),
        P(("parts", "replica")),
        P("parts"),
        P("parts"),
        P(("parts", "replica"), "tensor"),
        P(("parts", "replica"), None, "tensor"),
        P(("parts", "replica"), None, "tensor"),
        P("tensor", None),
        P("tensor", None),
        P(None, "tensor"),
        P("tensor", "parts", None, None),
    )
    out_specs = P(("parts", "replica"), None, "tensor")
    return jax.shard_map(
        on_device, mesh=mesh, in_specs=in_specs, out_specs=out_specs, check_vma=False
    )
```

```python
import functools
import math

import jax
import jax.numpy as jnp
from jax import lax
from jax.experimental import pallas as pl
from jax.experimental.pallas import tpu as pltpu
from jax.sharding import PartitionSpec as P


HD = 128
rope_base = 1000000.0
LOG2E = math.log2(math.e)
HIDDEN = -1e30


def rotary(vectors, places):
    half = vectors.shape[-1] // 2
    freq = rope_base ** (-(2.0 / vectors.shape[-1]) * jnp.arange(half, dtype=jnp.float32))
    angle = places.astype(jnp.float32)[..., None, None] * freq
    cosine = jnp.cos(angle)
    sine = jnp.sin(angle)
    first = vectors[..., :half]
    second = vectors[..., half:]
    return jnp.concatenate([first * cosine - second * sine, second * cosine + first * sine], -1)


def rotate_round(summed, places, kv_heads):
    number = summed.shape[0]
    turned = rotary(summed[:, : kv_heads * HD].reshape(number, kv_heads, HD), places)
    turned = turned.astype(jnp.bfloat16).reshape(number, kv_heads * HD)
    return jnp.concatenate([turned, summed[:, kv_heads * HD :].astype(jnp.bfloat16)], 1)


def own_pair(packed, head_group, kv_heads):
    key_part = lax.dynamic_slice_in_dim(packed, head_group * HD, HD, 1)
    value_part = lax.dynamic_slice_in_dim(packed, (kv_heads + head_group) * HD, HD, 1)
    return jnp.concatenate([key_part, value_part], 1)


NT = (((1,), (1,)), ((), ()))
SMALL = pltpu.CompilerParams(vmem_limit_bytes=24 << 20)
LARGE = pltpu.CompilerParams(vmem_limit_bytes=36 << 20)
SET_ROWS = 32


def in_hbm(x):
    return pltpu.with_memory_space_constraint(x, pltpu.HBM)


def lane_tiles(combine, x):
    out = x[..., :HD]
    for i in range(1, x.shape[-1] // HD):
        out = combine(out, x[..., i * HD : (i + 1) * HD])
    return out


def stacked_heads(q_ref, heads):
    m = q_ref.shape[0] * q_ref.shape[1]
    q = q_ref[...].reshape(m, heads * HD)
    return jnp.concatenate([q[:, h * HD : (h + 1) * HD] for h in range(heads)], 0)


def softmax_parts(qs, heads, parts, scale2, s_ref):
    m = qs.shape[0] // heads
    top = None
    at = 0
    for ref, bias in parts:
        n = ref.shape[0]
        s = lax.dot_general(qs, ref[:, :HD], NT, preferred_element_type=jnp.float32)
        s = s.reshape(heads, m, n) * scale2 + bias()[None]
        s_ref[:, :, at : at + n] = s
        most = lane_tiles(jnp.maximum, s)
        top = most if top is None else jnp.maximum(top, most)
        at += n
    top = jnp.max(top, -1, keepdims=True)
    total = mixed = None
    at = 0
    for ref, _ in parts:
        n = ref.shape[0]
        w = jnp.exp2(s_ref[:, :, at : at + n] - top)
        summed = lane_tiles(jnp.add, w)
        one = jnp.dot(
            w.astype(jnp.bfloat16).reshape(heads * m, n),
            ref[:, HD:],
            preferred_element_type=jnp.float32,
        ).reshape(heads, m, HD)
        total = summed if total is None else total + summed
        mixed = one if mixed is None else mixed + one
        at += n
    return top, jnp.sum(total, -1, keepdims=True), mixed


def hidden_unless(prompt, keys):
    return jnp.where(prompt == keys, 0.0, HIDDEN)


def cached_kernel(heads, scale2, q_ref, prompt_ref, keyp_ref, pool_ref, mixed_ref, stat_ref, s_ref):
    qs = stacked_heads(q_ref, heads)
    parts = ((pool_ref, lambda: hidden_unless(prompt_ref[...], keyp_ref[...])),)
    top, total, mixed = softmax_parts(qs, heads, parts, scale2, s_ref)
    mixed_ref[...] = mixed
    lane = lax.broadcasted_iota(jnp.int32, mixed.shape, 2)
    stat_ref[...] = jnp.where(lane < HD // 2, top, total)


def new_kernel(
    heads, steps, scale2, q_ref, prompt_ref, keyp_ref, span_ref, tail_ref, mixed_ref, stat_ref, o_ref, s_ref
):
    qs = stacked_heads(q_ref, heads)
    m = qs.shape[0] // heads

    def causal():
        row = lax.broadcasted_iota(jnp.int32, (m, m), 0)
        col = lax.broadcasted_iota(jnp.int32, (m, m), 1)
        return jnp.where((row // steps == col // steps) & (col <= row), 0.0, HIDDEN)

    parts = (
        (span_ref, lambda: hidden_unless(prompt_ref[...], keyp_ref[...])),
        (tail_ref, causal),
    )
    top, total, mixed = softmax_parts(qs, heads, parts, scale2, s_ref)
    old_top = stat_ref[:, :, :1]
    old_total = stat_ref[:, :, HD // 2 : HD // 2 + 1]
    both = jnp.maximum(top, old_top)
    new_share = jnp.exp2(top - both)
    old_share = jnp.exp2(old_top - both)
    total = total * new_share + old_total * old_share
    mixed = mixed * new_share + mixed_ref[...] * old_share
    out = (mixed / total).astype(jnp.bfloat16)
    for h in range(heads):
        o_ref[:, h * HD : (h + 1) * HD] = out[h]


def attend_cached(q, row_prompt, key_prompt, pool, start, count):
    steps, width = q.shape[1:]
    heads = width // HD
    block = min(SET_ROWS, q.shape[0])
    m = block * steps
    cached = pool.shape[0]
    return pl.pallas_call(
        functools.partial(cached_kernel, heads, LOG2E / math.sqrt(HD)),
        grid=(count,),
        in_specs=[
            pl.BlockSpec((block, steps, width), lambda i: (i + start, 0, 0)),
            pl.BlockSpec((m, 1), lambda i: (i + start, 0)),
            pl.BlockSpec((1, cached), lambda i: (0, 0)),
            pl.BlockSpec((cached, 2 * HD), lambda i: (0, 0)),
        ],
        out_specs=[pl.BlockSpec((heads, m, HD), lambda i: (0, i, 0))] * 2,
        out_shape=[jax.ShapeDtypeStruct((heads, m * count, HD), jnp.float32)] * 2,
        scratch_shapes=[pltpu.VMEM((heads, m, cached), jnp.float32)],
        cost_estimate=pl.CostEstimate(
            flops=4 * count * heads * m * cached * HD,
            transcendentals=count * heads * m * cached,
            bytes_accessed=8 * count * heads * m * HD,
        ),
        compiler_params=SMALL,
        name="attend_cached",
    )(q, row_prompt, key_prompt, pool)


def attend_new(q, row_prompt, key_prompt, span_pairs, tail_pairs, mixed, stat, start, count):
    steps, width = q.shape[1:]
    heads = width // HD
    block = min(SET_ROWS, q.shape[0])
    m = block * steps
    keys = span_pairs.shape[0]
    part = pl.BlockSpec((heads, m, HD), lambda i: (0, i, 0))
    return pl.pallas_call(
        functools.partial(new_kernel, heads, steps, LOG2E / math.sqrt(HD)),
        grid=(count,),
        in_specs=[
            pl.BlockSpec((block, steps, width), lambda i: (i + start, 0, 0)),
            pl.BlockSpec((m, 1), lambda i: (i + start, 0)),
            pl.BlockSpec((1, keys), lambda i: (0, 0)),
            pl.BlockSpec((keys, 2 * HD), lambda i: (0, 0)),
            pl.BlockSpec((m, 2 * HD), lambda i: (i, 0)),
            part,
            part,
        ],
        out_specs=pl.BlockSpec((m, width), lambda i: (i, 0)),
        out_shape=jax.ShapeDtypeStruct((m * count, width), jnp.bfloat16),
        scratch_shapes=[pltpu.VMEM((heads, m, keys + m), jnp.float32)],
        cost_estimate=pl.CostEstimate(
            flops=4 * count * heads * m * (keys + m) * HD,
            transcendentals=count * heads * m * (keys + m),
            bytes_accessed=10 * count * heads * m * HD,
        ),
        compiler_params=SMALL,
        name="attend_new",
    )(q, row_prompt, key_prompt, span_pairs, tail_pairs, mixed, stat)


def project_kernel(split, kept, sent, rank_ref, x_ref, *refs):
    keep_ref, send_ref, acc = refs[-3:]
    s = pl.program_id(0)
    x = x_ref[...].reshape(-1, x_ref.shape[-1])
    w = jnp.concatenate(
        [jnp.concatenate([refs[2 * i][...], refs[2 * i + 1][...]], 1) for i in range(split)], 0
    )
    one = jnp.dot(x, w, preferred_element_type=jnp.float32)

    @pl.when(s == 0)
    def _():
        acc[...] = one

    @pl.when(s > 0)
    def _():
        acc[...] += one

    @pl.when(s == pl.num_programs(0) - 1)
    def _():
        keys = acc.shape[1] // 2
        for ref, rels in ((send_ref, sent), (keep_ref, kept)):
            for i, rel in enumerate(rels):
                at = pl.multiple_of((rank_ref[0] ^ rel) * HD, HD)
                ref[i, :, :HD] = acc[:, pl.ds(at, HD)].astype(ref.dtype)
                ref[i, :, HD:] = acc[:, pl.ds(pl.multiple_of(at + keys, HD), HD)].astype(ref.dtype)


def project(rank, x, start, rows, key_weight, value_weight, kept, sent):
    width, columns = key_weight.shape
    depth, split = width // 2, 2
    lead = (rows,) + x.shape[1:-1]
    n = math.prod(lead)
    zeros = (0,) * (len(lead) - 1)
    in_specs = [
        pl.BlockSpec(
            tuple(pl.Element(d) for d in lead + (depth,)),
            lambda s, r: (start,) + zeros + (s * depth,),
        )
    ]
    for i in range(split):
        piece = pl.BlockSpec((depth // split, columns), lambda s, r, i=i: (s * split + i, 0))
        in_specs += [piece, piece]
    return pl.pallas_call(
        functools.partial(project_kernel, split, kept, sent),
        grid_spec=pltpu.PrefetchScalarGridSpec(
            num_scalar_prefetch=1,
            grid=(width // depth,),
            in_specs=in_specs,
            out_specs=[
                pl.BlockSpec((len(rels), n, 2 * HD), lambda s, r: (0, 0, 0)) for rels in (kept, sent)
            ],
            scratch_shapes=[pltpu.VMEM((n, 2 * columns), jnp.float32)],
        ),
        out_shape=[
            jax.ShapeDtypeStruct((len(kept), n, 2 * HD), jnp.float32),
            jax.ShapeDtypeStruct((len(sent), n, 2 * HD), jnp.bfloat16),
        ],
        cost_estimate=pl.CostEstimate(
            flops=4 * n * width * columns, transcendentals=0, bytes_accessed=4 * width * columns
        ),
        compiler_params=SMALL,
        name="project",
    )(rank, in_hbm(x), *([in_hbm(key_weight), in_hbm(value_weight)] * split))


def finish_kernel(keep_ref, *refs):
    cos_ref, sin_ref, o_ref = refs[-3:]
    summed = keep_ref[0]
    for ref in refs[:-3]:
        summed = summed + (ref[0] if len(ref.shape) == 3 else ref[...]).astype(jnp.float32)
    keys = summed[:, :HD]
    turned = keys * cos_ref[...] + pltpu.roll(keys, HD // 2, 1) * sin_ref[...]
    o_ref[:, :HD] = turned.astype(jnp.bfloat16)
    o_ref[:, HD:] = summed[:, HD:].astype(jnp.bfloat16)


def finish(keep, others, tables):
    n = keep.shape[1]
    first = pl.BlockSpec((1, n, 2 * HD), lambda i: (0, 0, 0))
    flat = lambda w: pl.BlockSpec((n, w), lambda i: (0, 0))
    return pl.pallas_call(
        finish_kernel,
        grid=(1,),
        in_specs=[first]
        + [first if x.ndim == 3 else flat(2 * HD) for x in others]
        + [flat(HD), flat(HD)],
        out_specs=flat(2 * HD),
        out_shape=jax.ShapeDtypeStruct((n, 2 * HD), jnp.bfloat16),
        compiler_params=SMALL,
        name="finish",
    )(keep, *others, *tables)


def turn_tables(places):
    half = HD // 2
    freq = rope_base ** (-(2.0 / HD) * jnp.arange(half, dtype=jnp.float32))
    angle = places.astype(jnp.float32)[:, None] * freq
    cosine = jnp.cos(angle)
    sine = jnp.sin(angle)
    return lax.optimization_barrier(
        (jnp.concatenate([cosine, cosine], 1), jnp.concatenate([-sine, sine], 1))
    )


def swap(x, axis, bit):
    return lax.ppermute(x, axis, [(i, i ^ bit) for i in range(lax.axis_size(axis))])


def swap_sum(keep, send, tables):
    got = swap(send, "tensor", 1)
    half = (keep[1] + got[1].astype(jnp.float32)).astype(jnp.bfloat16)
    last = swap(half, "tensor", 2)
    return finish(keep, (got, last), tables)


def chain_sum(keep, send, tables):
    one = lax.ppermute(send, "tensor", [(0, 1), (3, 2)])
    inward = jnp.stack([keep[3] + one[1].astype(jnp.float32), keep[2] + one[2].astype(jnp.float32)])
    two = lax.ppermute(inward.astype(jnp.bfloat16), "tensor", [(1, 2), (2, 1)])
    outward = (keep[1] + two[1].astype(jnp.float32)).astype(jnp.bfloat16)
    three = lax.ppermute(outward, "tensor", [(1, 0), (2, 3)])
    return finish(keep, (one, two, three), tables)


def out_kernel(rels, pick, cuts, add, final, rank_ref, *refs):
    refs = list(refs)
    pieces = [refs.pop(0) for _ in rels]
    other = refs.pop(0) if pick else None
    partial = refs.pop(0) if add else None
    w_ref, o_ref, buf, sem = refs[0], refs[-3], refs[-2], refs[-1]
    width = pieces[0].shape[1]
    depth = width // cuts
    rank = rank_ref[0]
    copies = []
    for p, rel in enumerate(rels):
        for c in range(cuts):
            row = pl.multiple_of((rank ^ rel) * width + c * depth, depth)
            slot = p * cuts + c
            copies.append(
                pltpu.make_async_copy(w_ref.at[pl.ds(row, depth), :], buf.at[slot], sem.at[slot])
            )
            copies[-1].start()
    total = partial[...] if add else None
    for p in range(len(rels)):
        a = pieces[p][...]
        if pick and p == len(rels) - 1:
            inner = (rank == 1) | (rank == 2)
            a = jnp.where(inner, a, other[...])
        for c in range(cuts):
            slot = p * cuts + c
            copies[slot].wait()
            one = jnp.dot(
                a[:, c * depth : (c + 1) * depth], buf[slot], preferred_element_type=jnp.float32
            )
            total = one if total is None else total + one
    o_ref[...] = total.reshape(o_ref.shape).astype(o_ref.dtype)


def out_project(rank, pieces, rels, weight, shape, start, pick=None, partial=None, into=None, final=True):
    m, width = pieces[0].shape
    columns = weight.shape[1]
    steps = shape[1]
    cuts = 4
    flat = lambda w: pl.BlockSpec((m, w), lambda i, r: (0, 0))
    args = list(pieces)
    in_specs = [flat(width) for _ in pieces]
    if pick is not None:
        args.append(pick)
        in_specs.append(flat(width))
    if partial is not None:
        args.append(partial)
        in_specs.append(flat(columns))
    args.append(in_hbm(weight))
    in_specs.append(pl.BlockSpec(memory_space=pl.ANY))
    aliases = {}
    if into is not None:
        args.append(into)
        in_specs.append(pl.BlockSpec(memory_space=pl.ANY))
        aliases = {len(args): 0}
    if final:
        out_spec = pl.BlockSpec(
            (pl.Element(m // steps), pl.Element(steps), pl.Element(columns)),
            lambda i, r: (start, 0, 0),
        )
        out_shape = jax.ShapeDtypeStruct(shape, jnp.bfloat16)
    else:
        out_spec = flat(columns)
        out_shape = jax.ShapeDtypeStruct((m, columns), jnp.float32)
    slots = len(rels) * cuts
    return pl.pallas_call(
        functools.partial(out_kernel, rels, pick is not None, cuts, partial is not None, final),
        grid_spec=pltpu.PrefetchScalarGridSpec(
            num_scalar_prefetch=1,
            grid=(1,),
            in_specs=in_specs,
            out_specs=out_spec,
            scratch_shapes=[
                pltpu.VMEM((slots, width // cuts, columns), jnp.bfloat16),
                pltpu.SemaphoreType.DMA((slots,)),
            ],
        ),
        out_shape=out_shape,
        input_output_aliases=aliases,
        cost_estimate=pl.CostEstimate(
            flops=2 * m * width * columns * len(rels),
            transcendentals=0,
            bytes_accessed=2 * width * columns * len(rels),
        ),
        compiler_params=LARGE,
        name="out_project",
    )(rank, *args)


def mask_tables(prompt_owner, page_table, prompt_length, page_size, span, order):
    n_replica = order.shape[0]
    prompts = jnp.arange(n_replica, dtype=jnp.int32)
    pool_pages = page_table.shape[0]
    cpages = pool_pages // n_replica
    entries = jnp.arange(pool_pages, dtype=jnp.int32)
    page_hits = page_table[None, :] == entries[:, None]
    page_prompt = jnp.sum(jnp.where(page_hits, entries[None, :] // cpages, 0), 1)
    page_slot = jnp.sum(jnp.where(page_hits, entries[None, :] % cpages, 0), 1)
    page_length = jnp.sum(
        jnp.where(page_prompt[:, None] == prompts[None, :], prompt_length[None, :], 0), 1
    )
    visible = (
        page_slot[:, None] * page_size + jnp.arange(page_size, dtype=jnp.int32)[None, :]
        < page_length[:, None]
    )
    pool_prompt = jnp.where(visible, page_prompt[:, None], -1).reshape(-1)
    owners = jnp.sum(jnp.where(order[:, None] == prompts[None, :], prompt_owner[None, :], 0), 1)
    return jnp.concatenate([pool_prompt, jnp.repeat(owners, span)])[None, :]


def gather_heads(own):
    far = swap(own, "tensor", 2)
    near = swap(own, "tensor", 1)
    across = lax.ppermute(own, "tensor", [(1, 2), (2, 1)])
    passed = lax.ppermute(far, "tensor", [(1, 0), (2, 3)])
    return far, near, across, passed


def on_device(
    prompt_owner,
    fork_map,
    page_table,
    prompt_length,
    span_states,
    decode_states,
    decode_queries,
    key_weight,
    value_weight,
    out_weight,
    page_pool,
):
    replica = lax.axis_index("replica")
    device_rank = lax.axis_index("tensor")
    n_replica = lax.axis_size("replica")
    n_tensor = lax.axis_size("tensor")
    span = span_states.shape[0]
    rows, steps, width = decode_states.shape
    kv_heads = key_weight.shape[1] // HD
    sharing = n_tensor // kv_heads
    prompts = jnp.arange(n_replica, dtype=jnp.int32)
    own_prompt = jnp.sum(jnp.where(prompts == replica, prompt_owner, 0))
    own_length = jnp.sum(jnp.where(prompts == own_prompt, prompt_length, 0))
    row_hits = fork_map[:, None] == prompts[None, :]
    row_length = jnp.sum(jnp.where(row_hits, prompt_length[None, :], 0), 1)
    span_places = own_length + jnp.arange(span, dtype=jnp.int32)
    tail_places = (
        row_length[:, None] + span + jnp.arange(steps, dtype=jnp.int32)[None, :]
    ).reshape(-1)
    row_prompt = jnp.repeat(fork_map, steps)[:, None]
    pool = page_pool.reshape(-1, 2 * HD)
    cached = pool.shape[0]
    short_line = n_tensor == kv_heads == 4 and n_replica == 4
    first = min(SET_ROWS, rows)
    blocks = rows // first

    if not short_line:
        positions = jnp.concatenate([span_places, tail_places])
        tokens = jnp.concatenate([span_states, decode_states.reshape(rows * steps, width)], 0)
        projected = jnp.dot(
            tokens,
            jnp.concatenate([key_weight, value_weight], 1),
            preferred_element_type=jnp.float32,
        )
        share = lax.psum_scatter(projected, "tensor", scatter_dimension=0, tiled=True)
        number = share.shape[0]
        places = lax.dynamic_slice_in_dim(positions, device_rank * number, number)
        turned = rotate_round(share, places, kv_heads)
        groups = jnp.stack([own_pair(turned, g, kv_heads) for g in range(kv_heads)], 0)
        outgoing = jnp.repeat(groups, sharing, axis=0)
        paired = lax.all_to_all(
            outgoing, "tensor", split_axis=0, concat_axis=1, tiled=True
        ).reshape(-1, 2 * HD)
        arrived = lax.all_gather(paired[:span], "replica", axis=0, tiled=True)
        key_prompt = mask_tables(
            prompt_owner, page_table, prompt_length, page_pool.shape[2], span, prompts
        )
        mixed, stat = attend_cached(
            decode_queries, row_prompt, key_prompt[:, :cached], pool, 0, blocks
        )
        own = attend_new(
            decode_queries, row_prompt, key_prompt[:, cached:], arrived, paired[span:], mixed, stat, 0, blocks
        )
        decoded = jnp.dot(
            lax.all_gather(own, "tensor", axis=1, tiled=True),
            out_weight,
            preferred_element_type=jnp.float32,
        )
        return decoded.astype(jnp.bfloat16).reshape(rows, steps, out_weight.shape[1])

    rank = device_rank.reshape(1).astype(jnp.int32)
    order = replica ^ prompts
    key_prompt = mask_tables(
        prompt_owner, page_table, prompt_length, page_pool.shape[2], span, order
    )
    pool_prompt, span_prompt = key_prompt[:, :cached], key_prompt[:, cached:]
    return line_of_four(
        rank, span_states, decode_states, decode_queries, key_weight, value_weight,
        out_weight, pool, row_prompt, pool_prompt, span_prompt, span_places, tail_places,
    )


def line_of_four(
    rank, span_states, decode_states, decode_queries, key_weight, value_weight,
    out_weight, pool, row_prompt, pool_prompt, span_prompt, span_places, tail_places,
):
    n_replica = lax.axis_size("replica")
    span = span_states.shape[0]
    rows, steps, _ = decode_states.shape
    first = min(SET_ROWS, rows)
    blocks = rows // first
    cut = first * steps

    def units(x, start, count, kept, sent):
        return project(rank, x, start, count, key_weight, value_weight, kept, sent)

    span_units = units(span_states, 0, span, (0, 2), (1, 3))
    first_units = units(decode_states, 0, first, (0, 2), (1, 3))
    rest_units = units(decode_states, first, rows - first, (0, 1, 2, 3), (1, 2, 3))
    span_tables = turn_tables(span_places)
    cos, sin = turn_tables(tail_places)
    own_span = swap_sum(*span_units, span_tables)
    arrived = [own_span]
    for j in range(1, n_replica):
        arrived.append(swap(own_span, "replica", j))
    arrived = jnp.concatenate(arrived, 0)
    first_tail = swap_sum(*first_units, (cos[:cut], sin[:cut]))
    rest_tail = chain_sum(*rest_units, (cos[cut:], sin[cut:]))

    def cached_part(start, count):
        return attend_cached(decode_queries, row_prompt, pool_prompt, pool, start, count)

    def new_part(tail, parts, start, count):
        return attend_new(
            decode_queries, row_prompt, span_prompt, arrived, tail, *parts, start, count
        )

    middle = blocks - 2
    shape = (rows, steps, out_weight.shape[1])
    first_own = new_part(first_tail, cached_part(0, 1), 0, 1)
    middle_own = new_part(rest_tail[: middle * cut], cached_part(1, middle), 1, middle)
    last_own = new_part(rest_tail[middle * cut :], cached_part(blocks - 1, 1), blocks - 1, 1)
    every = (0, 2, 1, 3)
    far, near, across, passed = gather_heads(first_own)
    decoded = out_project(
        rank, [first_own, far, near, across], every, out_weight, shape, 0, pick=passed
    )
    far, near, across, passed = gather_heads(middle_own)
    decoded = out_project(
        rank, [middle_own, far, near, across], every, out_weight, shape, first,
        pick=passed, into=decoded,
    )
    far, near, across, passed = gather_heads(last_own)
    partial = out_project(rank, [last_own, far], (0, 2), out_weight, shape, 0, final=False)
    return out_project(
        rank, [near, across], (1, 3), out_weight, shape, first * (blocks - 1),
        pick=passed, partial=partial, into=decoded,
    )


def solution(mesh):
    in_specs = (
        P("parts"),
        P(("parts", "replica")),
        P("parts"),
        P("parts"),
        P(("parts", "replica"), "tensor"),
        P(("parts", "replica"), None, "tensor"),
        P(("parts", "replica"), None, "tensor"),
        P("tensor", None),
        P("tensor", None),
        P(None, "tensor"),
        P("tensor", "parts", None, None),
    )
    out_specs = P(("parts", "replica"), None, "tensor")
    return jax.shard_map(
        on_device, mesh=mesh, in_specs=in_specs, out_specs=out_specs, check_vma=False
    )
```

```python
import functools
import math

import jax
import jax.numpy as jnp
from jax import lax
from jax.experimental import pallas as pl
from jax.experimental.pallas import tpu as pltpu
from jax.sharding import PartitionSpec as P


HD = 128
rope_base = 1000000.0
LOG2E = math.log2(math.e)
HIDDEN = -1e30


def rotary(vectors, places):
    half = vectors.shape[-1] // 2
    freq = rope_base ** (-(2.0 / vectors.shape[-1]) * jnp.arange(half, dtype=jnp.float32))
    angle = places.astype(jnp.float32)[..., None, None] * freq
    cosine = jnp.cos(angle)
    sine = jnp.sin(angle)
    first = vectors[..., :half]
    second = vectors[..., half:]
    return jnp.concatenate([first * cosine - second * sine, second * cosine + first * sine], -1)


def rotate_round(summed, places, kv_heads):
    number = summed.shape[0]
    turned = rotary(summed[:, : kv_heads * HD].reshape(number, kv_heads, HD), places)
    turned = turned.astype(jnp.bfloat16).reshape(number, kv_heads * HD)
    return jnp.concatenate([turned, summed[:, kv_heads * HD :].astype(jnp.bfloat16)], 1)


def own_pair(packed, head_group, kv_heads):
    key_part = lax.dynamic_slice_in_dim(packed, head_group * HD, HD, 1)
    value_part = lax.dynamic_slice_in_dim(packed, (kv_heads + head_group) * HD, HD, 1)
    return jnp.concatenate([key_part, value_part], 1)


NT = (((1,), (1,)), ((), ()))
SMALL = pltpu.CompilerParams(vmem_limit_bytes=24 << 20)
LARGE = pltpu.CompilerParams(vmem_limit_bytes=36 << 20)
SET_ROWS = 32


def in_hbm(x):
    return pltpu.with_memory_space_constraint(x, pltpu.HBM)


def lane_tiles(combine, x):
    out = x[..., :HD]
    for i in range(1, x.shape[-1] // HD):
        out = combine(out, x[..., i * HD : (i + 1) * HD])
    return out


def stacked_heads(q_ref, heads):
    m = q_ref.shape[0] * q_ref.shape[1]
    q = q_ref[...].reshape(m, heads * HD)
    return jnp.concatenate([q[:, h * HD : (h + 1) * HD] for h in range(heads)], 0)


def softmax_parts(qs, heads, parts, scale2, s_ref):
    m = qs.shape[0] // heads
    top = None
    at = 0
    for n, load, bias in parts:
        s = lax.dot_general(qs, load()[:, :HD], NT, preferred_element_type=jnp.float32)
        s = s.reshape(heads, m, n) * scale2 + bias()[None]
        s_ref[:, :, at : at + n] = s
        most = lane_tiles(jnp.maximum, s)
        top = most if top is None else jnp.maximum(top, most)
        at += n
    top = jnp.max(top, -1, keepdims=True)
    total = mixed = None
    at = 0
    for n, load, _ in parts:
        w = jnp.exp2(s_ref[:, :, at : at + n] - top)
        summed = lane_tiles(jnp.add, w)
        one = jnp.dot(
            w.astype(jnp.bfloat16).reshape(heads * m, n),
            load()[:, HD:],
            preferred_element_type=jnp.float32,
        ).reshape(heads, m, HD)
        total = summed if total is None else total + summed
        mixed = one if mixed is None else mixed + one
        at += n
    return top, jnp.sum(total, -1, keepdims=True), mixed


def shown(allowed):
    return jnp.where(allowed, 0.0, HIDDEN)


def cached_kernel(
    heads, cpages, scale2, table_ref, length_ref, q_ref, prompt_ref, pool_ref, mixed_ref, stat_ref, s_ref
):
    qs = stacked_heads(q_ref, heads)
    m = qs.shape[0] // heads
    pages, size = pool_ref.shape[:2]
    group = 2 * cpages

    def part(at):
        mine = range(at, min(at + group, pages))

        def load():
            return jnp.concatenate([pool_ref[table_ref[i]] for i in mine], 0)

        def bias():
            lane = lax.broadcasted_iota(jnp.int32, (m, size), 1)
            prompt = prompt_ref[...]
            return jnp.concatenate(
                [
                    shown(
                        (prompt == i // cpages)
                        & (lane < length_ref[i // cpages] - (i % cpages) * size)
                    )
                    for i in mine
                ],
                1,
            )

        return len(mine) * size, load, bias

    parts = [part(at) for at in range(0, pages, group)]
    top, total, mixed = softmax_parts(qs, heads, parts, scale2, s_ref)
    mixed_ref[...] = mixed
    lane = lax.broadcasted_iota(jnp.int32, mixed.shape, 2)
    stat_ref[...] = jnp.where(lane < HD // 2, top, total)


def new_kernel(heads, steps, scale2, owner_ref, base_ref, q_ref, prompt_ref, tail_ref, mixed_ref, stat_ref, *refs):
    span_refs, o_ref, s_ref = refs[:-2], refs[-2], refs[-1]
    qs = stacked_heads(q_ref, heads)
    m = qs.shape[0] // heads
    span = span_refs[0].shape[0]

    def loaded():
        return jnp.concatenate([ref[...] for ref in span_refs], 0)

    def owned():
        prompt = prompt_ref[...]
        return jnp.concatenate(
            [
                jnp.broadcast_to(shown(prompt == owner_ref[base_ref[0] ^ j]), (m, span))
                for j in range(len(span_refs))
            ],
            1,
        )

    def causal():
        row = lax.broadcasted_iota(jnp.int32, (m, m), 0)
        col = lax.broadcasted_iota(jnp.int32, (m, m), 1)
        return shown((row // steps == col // steps) & (col <= row))

    parts = (
        (span * len(span_refs), loaded, owned),
        (m, lambda: tail_ref[...], causal),
    )
    top, total, mixed = softmax_parts(qs, heads, parts, scale2, s_ref)
    old_top = stat_ref[:, :, :1]
    old_total = stat_ref[:, :, HD // 2 : HD // 2 + 1]
    both = jnp.maximum(top, old_top)
    new_share = jnp.exp2(top - both)
    old_share = jnp.exp2(old_top - both)
    total = total * new_share + old_total * old_share
    mixed = mixed * new_share + mixed_ref[...] * old_share
    out = (mixed / total).astype(jnp.bfloat16)
    for h in range(heads):
        o_ref[:, h * HD : (h + 1) * HD] = out[h]


def attend_cached(q, row_prompt, page_table, prompt_length, pool, start, count):
    steps, width = q.shape[1:]
    heads = width // HD
    block = min(SET_ROWS, q.shape[0])
    m = block * steps
    cached = pool.shape[0] * pool.shape[1]
    cpages = pool.shape[0] // prompt_length.shape[0]
    return pl.pallas_call(
        functools.partial(cached_kernel, heads, cpages, LOG2E / math.sqrt(HD)),
        grid_spec=pltpu.PrefetchScalarGridSpec(
            num_scalar_prefetch=2,
            grid=(count,),
            in_specs=[
                pl.BlockSpec((block, steps, width), lambda i, *_: (i + start, 0, 0)),
                pl.BlockSpec((m, 1), lambda i, *_: (i + start, 0)),
                pl.BlockSpec(pool.shape, lambda i, *_: (0, 0, 0)),
            ],
            out_specs=[pl.BlockSpec((heads, m, HD), lambda i, *_: (0, i, 0))] * 2,
            scratch_shapes=[pltpu.VMEM((heads, m, cached), jnp.float32)],
        ),
        out_shape=[jax.ShapeDtypeStruct((heads, m * count, HD), jnp.float32)] * 2,
        cost_estimate=pl.CostEstimate(
            flops=4 * count * heads * m * cached * HD,
            transcendentals=count * heads * m * cached,
            bytes_accessed=8 * count * heads * m * HD,
        ),
        compiler_params=SMALL,
        name="attend_cached",
    )(page_table, prompt_length, q, row_prompt, pool)


def attend_new(q, row_prompt, owner, base, span_pairs, tail_pairs, mixed, stat, start, count):
    steps, width = q.shape[1:]
    heads = width // HD
    block = min(SET_ROWS, q.shape[0])
    m = block * steps
    span = span_pairs[0].shape[0]
    keys = span * len(span_pairs)
    part = pl.BlockSpec((heads, m, HD), lambda i, *_: (0, i, 0))
    return pl.pallas_call(
        functools.partial(new_kernel, heads, steps, LOG2E / math.sqrt(HD)),
        grid_spec=pltpu.PrefetchScalarGridSpec(
            num_scalar_prefetch=2,
            grid=(count,),
            in_specs=[
                pl.BlockSpec((block, steps, width), lambda i, *_: (i + start, 0, 0)),
                pl.BlockSpec((m, 1), lambda i, *_: (i + start, 0)),
                pl.BlockSpec((m, 2 * HD), lambda i, *_: (i, 0)),
                part,
                part,
            ]
            + [pl.BlockSpec((span, 2 * HD), lambda i, *_: (0, 0))] * len(span_pairs),
            out_specs=pl.BlockSpec((m, width), lambda i, *_: (i, 0)),
            scratch_shapes=[pltpu.VMEM((heads, m, keys + m), jnp.float32)],
        ),
        out_shape=jax.ShapeDtypeStruct((m * count, width), jnp.bfloat16),
        cost_estimate=pl.CostEstimate(
            flops=4 * count * heads * m * (keys + m) * HD,
            transcendentals=count * heads * m * (keys + m),
            bytes_accessed=10 * count * heads * m * HD,
        ),
        compiler_params=SMALL,
        name="attend_new",
    )(owner, base, q, row_prompt, tail_pairs, mixed, stat, *span_pairs)


def project_kernel(groups, split, kept, sent, rank_ref, *refs):
    keep_ref, send_ref, acc = refs[-3:]
    s = pl.program_id(0)
    rows = [ref[...].reshape(-1, ref.shape[-1]) for ref in refs[:groups]]
    x = rows[0] if groups == 1 else jnp.concatenate(rows, 0)
    refs = refs[groups:]
    w = jnp.concatenate(
        [jnp.concatenate([refs[2 * i][...], refs[2 * i + 1][...]], 1) for i in range(split)], 0
    )
    one = jnp.dot(x, w, preferred_element_type=jnp.float32)

    @pl.when(s == 0)
    def _():
        acc[...] = one

    @pl.when(s > 0)
    def _():
        acc[...] += one

    @pl.when(s == pl.num_programs(0) - 1)
    def _():
        keys = acc.shape[1] // 2
        for ref, rels in ((send_ref, sent), (keep_ref, kept)):
            for i, rel in enumerate(rels):
                at = pl.multiple_of((rank_ref[0] ^ rel) * HD, HD)
                ref[i, :, :HD] = acc[:, pl.ds(at, HD)].astype(ref.dtype)
                ref[i, :, HD:] = acc[:, pl.ds(pl.multiple_of(at + keys, HD), HD)].astype(ref.dtype)


def project(rank, groups, key_weight, value_weight, kept, sent):
    width, columns = key_weight.shape
    depth, split = width // 2, 2
    in_specs = []
    n = 0
    for x, start, rows in groups:
        lead = (rows,) + x.shape[1:-1]
        n += math.prod(lead)
        in_specs.append(
            pl.BlockSpec(
                tuple(pl.Element(d) for d in lead + (depth,)),
                lambda s, r, start=start, lead=lead: (start,) + (0,) * (len(lead) - 1) + (s * depth,),
            )
        )
    for i in range(split):
        piece = pl.BlockSpec((depth // split, columns), lambda s, r, i=i: (s * split + i, 0))
        in_specs += [piece, piece]
    return pl.pallas_call(
        functools.partial(project_kernel, len(groups), split, kept, sent),
        grid_spec=pltpu.PrefetchScalarGridSpec(
            num_scalar_prefetch=1,
            grid=(width // depth,),
            in_specs=in_specs,
            out_specs=[
                pl.BlockSpec((len(rels), n, 2 * HD), lambda s, r: (0, 0, 0)) for rels in (kept, sent)
            ],
            scratch_shapes=[pltpu.VMEM((n, 2 * columns), jnp.float32)],
        ),
        out_shape=[
            jax.ShapeDtypeStruct((len(kept), n, 2 * HD), jnp.float32),
            jax.ShapeDtypeStruct((len(sent), n, 2 * HD), jnp.bfloat16),
        ],
        cost_estimate=pl.CostEstimate(
            flops=4 * n * width * columns, transcendentals=0, bytes_accessed=4 * width * columns
        ),
        compiler_params=SMALL,
        name="project",
    )(
        rank,
        *[in_hbm(x) for x, _, _ in groups],
        *([in_hbm(key_weight), in_hbm(value_weight)] * split),
    )


def finish_kernel(sizes, keep_ref, *refs):
    outs = refs[-len(sizes) :]
    refs = refs[: -len(sizes)]
    cos_ref, sin_ref = refs[-2:]
    summed = keep_ref[0]
    for ref in refs[:-2]:
        summed = summed + (ref[0] if len(ref.shape) == 3 else ref[...]).astype(jnp.float32)
    keys = summed[:, :HD]
    turned = keys * cos_ref[...] + pltpu.roll(keys, HD // 2, 1) * sin_ref[...]
    at = 0
    for size, o_ref in zip(sizes, outs):
        o_ref[:, :HD] = turned[at : at + size].astype(jnp.bfloat16)
        o_ref[:, HD:] = summed[at : at + size, HD:].astype(jnp.bfloat16)
        at += size


def finish(keep, others, tables, start, sizes):
    n = keep.shape[1]
    first = pl.BlockSpec((1, n, 2 * HD), lambda i: (0, 0, 0))
    flat = lambda rows: pl.BlockSpec((rows, 2 * HD), lambda i: (0, 0))
    table = pl.BlockSpec((pl.Element(n), pl.Element(HD)), lambda i: (start, 0))
    return pl.pallas_call(
        functools.partial(finish_kernel, sizes),
        grid=(1,),
        in_specs=[first] + [first if x.ndim == 3 else flat(n) for x in others] + [table, table],
        out_specs=[flat(size) for size in sizes],
        out_shape=[jax.ShapeDtypeStruct((size, 2 * HD), jnp.bfloat16) for size in sizes],
        compiler_params=SMALL,
        name="finish",
    )(keep, *others, *tables)


def turn_tables(places):
    half = HD // 2
    freq = rope_base ** (-(2.0 / HD) * jnp.arange(half, dtype=jnp.float32))
    angle = places.astype(jnp.float32)[:, None] * freq
    cosine = jnp.cos(angle)
    sine = jnp.sin(angle)
    return lax.optimization_barrier(
        (jnp.concatenate([cosine, cosine], 1), jnp.concatenate([-sine, sine], 1))
    )


def swap(x, axis, bit):
    return lax.ppermute(x, axis, [(i, i ^ bit) for i in range(lax.axis_size(axis))])


def swap_sum(keep, send, tables, start, sizes):
    got = swap(send, "tensor", 1)
    half = (keep[1] + got[1].astype(jnp.float32)).astype(jnp.bfloat16)
    last = swap(half, "tensor", 2)
    return finish(keep, (got, last), tables, start, sizes)


def chain_sum(keep, send, tables, start, sizes):
    one = lax.ppermute(send, "tensor", [(0, 1), (3, 2)])
    inward = jnp.stack([keep[3] + one[1].astype(jnp.float32), keep[2] + one[2].astype(jnp.float32)])
    two = lax.ppermute(inward.astype(jnp.bfloat16), "tensor", [(1, 2), (2, 1)])
    outward = (keep[1] + two[1].astype(jnp.float32)).astype(jnp.bfloat16)
    three = lax.ppermute(outward, "tensor", [(1, 0), (2, 3)])
    return finish(keep, (one, two, three), tables, start, sizes)


def out_kernel(rels, pick, cuts, add, final, rank_ref, *refs):
    refs = list(refs)
    pieces = [refs.pop(0) for _ in rels]
    other = refs.pop(0) if pick else None
    partial = refs.pop(0) if add else None
    w_ref, o_ref, buf, sem = refs[0], refs[-3], refs[-2], refs[-1]
    width = pieces[0].shape[1]
    depth = width // cuts
    rank = rank_ref[0]
    copies = []
    for p, rel in enumerate(rels):
        for c in range(cuts):
            row = pl.multiple_of((rank ^ rel) * width + c * depth, depth)
            slot = p * cuts + c
            copies.append(
                pltpu.make_async_copy(w_ref.at[pl.ds(row, depth), :], buf.at[slot], sem.at[slot])
            )
            copies[-1].start()
    total = partial[...] if add else None
    for p in range(len(rels)):
        a = pieces[p][...]
        if pick and p == len(rels) - 1:
            inner = (rank == 1) | (rank == 2)
            a = jnp.where(inner, a, other[...])
        for c in range(cuts):
            slot = p * cuts + c
            copies[slot].wait()
            one = jnp.dot(
                a[:, c * depth : (c + 1) * depth], buf[slot], preferred_element_type=jnp.float32
            )
            total = one if total is None else total + one
    o_ref[...] = total.reshape(o_ref.shape).astype(o_ref.dtype)


def out_project(rank, pieces, rels, weight, shape, start, pick=None, partial=None, into=None, final=True):
    m, width = pieces[0].shape
    columns = weight.shape[1]
    steps = shape[1]
    cuts = 4
    flat = lambda w: pl.BlockSpec((m, w), lambda i, r: (0, 0))
    args = list(pieces)
    in_specs = [flat(width) for _ in pieces]
    if pick is not None:
        args.append(pick)
        in_specs.append(flat(width))
    if partial is not None:
        args.append(partial)
        in_specs.append(flat(columns))
    args.append(in_hbm(weight))
    in_specs.append(pl.BlockSpec(memory_space=pl.ANY))
    aliases = {}
    if into is not None:
        args.append(into)
        in_specs.append(pl.BlockSpec(memory_space=pl.ANY))
        aliases = {len(args): 0}
    if final:
        out_spec = pl.BlockSpec(
            (pl.Element(m // steps), pl.Element(steps), pl.Element(columns)),
            lambda i, r: (start, 0, 0),
        )
        out_shape = jax.ShapeDtypeStruct(shape, jnp.bfloat16)
    else:
        out_spec = flat(columns)
        out_shape = jax.ShapeDtypeStruct((m, columns), jnp.float32)
    slots = len(rels) * cuts
    return pl.pallas_call(
        functools.partial(out_kernel, rels, pick is not None, cuts, partial is not None, final),
        grid_spec=pltpu.PrefetchScalarGridSpec(
            num_scalar_prefetch=1,
            grid=(1,),
            in_specs=in_specs,
            out_specs=out_spec,
            scratch_shapes=[
                pltpu.VMEM((slots, width // cuts, columns), jnp.bfloat16),
                pltpu.SemaphoreType.DMA((slots,)),
            ],
        ),
        out_shape=out_shape,
        input_output_aliases=aliases,
        cost_estimate=pl.CostEstimate(
            flops=2 * m * width * columns * len(rels),
            transcendentals=0,
            bytes_accessed=2 * width * columns * len(rels),
        ),
        compiler_params=LARGE,
        name="out_project",
    )(rank, *args)


def gather_heads(own):
    far = swap(own, "tensor", 2)
    near = swap(own, "tensor", 1)
    across = lax.ppermute(own, "tensor", [(1, 2), (2, 1)])
    passed = lax.ppermute(far, "tensor", [(1, 0), (2, 3)])
    return far, near, across, passed


def on_device(
    prompt_owner,
    fork_map,
    page_table,
    prompt_length,
    span_states,
    decode_states,
    decode_queries,
    key_weight,
    value_weight,
    out_weight,
    page_pool,
):
    replica = lax.axis_index("replica")
    device_rank = lax.axis_index("tensor")
    n_replica = lax.axis_size("replica")
    n_tensor = lax.axis_size("tensor")
    span = span_states.shape[0]
    rows, steps, width = decode_states.shape
    kv_heads = key_weight.shape[1] // HD
    sharing = n_tensor // kv_heads
    prompts = jnp.arange(n_replica, dtype=jnp.int32)
    own_prompt = jnp.sum(jnp.where(prompts == replica, prompt_owner, 0))
    own_length = jnp.sum(jnp.where(prompts == own_prompt, prompt_length, 0))
    row_hits = fork_map[:, None] == prompts[None, :]
    row_length = jnp.sum(jnp.where(row_hits, prompt_length[None, :], 0), 1)
    span_places = own_length + jnp.arange(span, dtype=jnp.int32)
    tail_places = (
        row_length[:, None] + span + jnp.arange(steps, dtype=jnp.int32)[None, :]
    ).reshape(-1)
    row_prompt = jnp.repeat(fork_map, steps)[:, None]
    pool = page_pool.reshape(page_pool.shape[1:])
    short_line = n_tensor == kv_heads == 4 and n_replica == 4
    first = min(SET_ROWS, rows)
    blocks = rows // first

    if not short_line:
        positions = jnp.concatenate([span_places, tail_places])
        tokens = jnp.concatenate([span_states, decode_states.reshape(rows * steps, width)], 0)
        projected = jnp.dot(
            tokens,
            jnp.concatenate([key_weight, value_weight], 1),
            preferred_element_type=jnp.float32,
        )
        share = lax.psum_scatter(projected, "tensor", scatter_dimension=0, tiled=True)
        number = share.shape[0]
        places = lax.dynamic_slice_in_dim(positions, device_rank * number, number)
        turned = rotate_round(share, places, kv_heads)
        groups = jnp.stack([own_pair(turned, g, kv_heads) for g in range(kv_heads)], 0)
        outgoing = jnp.repeat(groups, sharing, axis=0)
        paired = lax.all_to_all(
            outgoing, "tensor", split_axis=0, concat_axis=1, tiled=True
        ).reshape(-1, 2 * HD)
        arrived = lax.all_gather(paired[:span], "replica", axis=0, tiled=True)
        mixed, stat = attend_cached(
            decode_queries, row_prompt, page_table, prompt_length, pool, 0, blocks
        )
        own = attend_new(
            decode_queries,
            row_prompt,
            prompt_owner,
            jnp.zeros((1,), jnp.int32),
            jnp.split(arrived, n_replica),
            paired[span:],
            mixed,
            stat,
            0,
            blocks,
        )
        decoded = jnp.dot(
            lax.all_gather(own, "tensor", axis=1, tiled=True),
            out_weight,
            preferred_element_type=jnp.float32,
        )
        return decoded.astype(jnp.bfloat16).reshape(rows, steps, out_weight.shape[1])

    rank = device_rank.reshape(1).astype(jnp.int32)
    return line_of_four(
        rank, replica.reshape(1).astype(jnp.int32), prompt_owner, fork_map, page_table,
        prompt_length, span_states, decode_states, decode_queries, key_weight, value_weight,
        out_weight, pool,
    )


def line_of_four(
    rank, replica, prompt_owner, fork_map, page_table, prompt_length, span_states, decode_states,
    decode_queries, key_weight, value_weight, out_weight, pool,
):
    n_replica = lax.axis_size("replica")
    span = span_states.shape[0]
    rows, steps, _ = decode_states.shape
    first = min(SET_ROWS, rows)
    blocks = rows // first
    middle = blocks - 2
    cut = first * steps

    first_units = project(
        rank, ((span_states, 0, span), (decode_states, 0, first)), key_weight, value_weight,
        (0, 2), (1, 3),
    )
    rest_units = project(
        rank, ((decode_states, first, rows - first),), key_weight, value_weight,
        (0, 1, 2, 3), (1, 2, 3),
    )
    late_owner, late_fork, late_length, rest_send = lax.optimization_barrier(
        (prompt_owner, fork_map, prompt_length, rest_units[1])
    )
    prompts = jnp.arange(n_replica, dtype=jnp.int32)
    own_prompt = jnp.sum(jnp.where(prompts == replica, late_owner, 0))
    own_length = jnp.sum(jnp.where(prompts == own_prompt, late_length, 0))
    row_hits = late_fork[:, None] == prompts[None, :]
    row_length = jnp.sum(jnp.where(row_hits, late_length[None, :], 0), 1)
    places = jnp.concatenate(
        [
            own_length + jnp.arange(span, dtype=jnp.int32),
            (row_length[:, None] + span + jnp.arange(steps, dtype=jnp.int32)[None, :]).reshape(-1),
        ]
    )
    tables = turn_tables(places)
    row_prompt = jnp.repeat(late_fork, steps)[:, None]

    own_span, first_tail = swap_sum(*first_units, tables, 0, (span, cut))
    arrived = [own_span]
    for j in range(1, n_replica):
        arrived.append(swap(own_span, "replica", j))
    middle_tail, last_tail = chain_sum(
        rest_units[0], rest_send, tables, span + cut, (middle * cut, cut)
    )

    def attended(tail, start, count):
        old = attend_cached(
            decode_queries, row_prompt, page_table, prompt_length, pool, start, count
        )
        return attend_new(
            decode_queries, row_prompt, prompt_owner, replica, arrived, tail, *old, start, count
        )

    shape = (rows, steps, out_weight.shape[1])
    first_own = attended(first_tail, 0, 1)
    middle_own = attended(middle_tail, 1, middle)
    last_own = attended(last_tail, blocks - 1, 1)
    far, near, across, passed = gather_heads(first_own)
    decoded = out_project(
        rank, [first_own, far, near, across], (0, 2, 1, 3), out_weight, shape, 0, pick=passed
    )
    far, near, across, passed = gather_heads(middle_own)
    partial = out_project(
        rank, [middle_own, far, near], (0, 2, 1), out_weight, shape, 0, final=False
    )
    decoded = out_project(
        rank, [across], (3,), out_weight, shape, first, pick=passed, partial=partial, into=decoded
    )
    far, near, across, passed = gather_heads(last_own)
    partial = out_project(rank, [last_own, far], (0, 2), out_weight, shape, 0, final=False)
    return out_project(
        rank, [near, across], (1, 3), out_weight, shape, first * (blocks - 1),
        pick=passed, partial=partial, into=decoded,
    )


def solution(mesh):
    in_specs = (
        P("parts"),
        P(("parts", "replica")),
        P("parts"),
        P("parts"),
        P(("parts", "replica"), "tensor"),
        P(("parts", "replica"), None, "tensor"),
        P(("parts", "replica"), None, "tensor"),
        P("tensor", None),
        P("tensor", None),
        P(None, "tensor"),
        P("tensor", "parts", None, None),
    )
    out_specs = P(("parts", "replica"), None, "tensor")
    return jax.shard_map(
        on_device, mesh=mesh, in_specs=in_specs, out_specs=out_specs, check_vma=False
    )
```

```python
import functools
import math

import jax
import jax.numpy as jnp
from jax import lax
from jax.experimental import pallas as pl
from jax.experimental.pallas import tpu as pltpu
from jax.sharding import PartitionSpec as P


HD = 128
rope_base = 1000000.0
LOG2E = math.log2(math.e)
HIDDEN = -1e30


def rotary(vectors, places):
    half = vectors.shape[-1] // 2
    freq = rope_base ** (-(2.0 / vectors.shape[-1]) * jnp.arange(half, dtype=jnp.float32))
    angle = places.astype(jnp.float32)[..., None, None] * freq
    cosine = jnp.cos(angle)
    sine = jnp.sin(angle)
    first = vectors[..., :half]
    second = vectors[..., half:]
    return jnp.concatenate([first * cosine - second * sine, second * cosine + first * sine], -1)


def rotate_round(summed, places, kv_heads):
    number = summed.shape[0]
    turned = rotary(summed[:, : kv_heads * HD].reshape(number, kv_heads, HD), places)
    turned = turned.astype(jnp.bfloat16).reshape(number, kv_heads * HD)
    return jnp.concatenate([turned, summed[:, kv_heads * HD :].astype(jnp.bfloat16)], 1)


def own_pair(packed, head_group, kv_heads):
    key_part = lax.dynamic_slice_in_dim(packed, head_group * HD, HD, 1)
    value_part = lax.dynamic_slice_in_dim(packed, (kv_heads + head_group) * HD, HD, 1)
    return jnp.concatenate([key_part, value_part], 1)


NT = (((1,), (1,)), ((), ()))
SMALL = pltpu.CompilerParams(vmem_limit_bytes=24 << 20)
LARGE = pltpu.CompilerParams(vmem_limit_bytes=36 << 20)
SET_ROWS = 32


def in_hbm(x):
    return pltpu.with_memory_space_constraint(x, pltpu.HBM)


def lane_tiles(combine, x):
    out = x[..., :HD]
    for i in range(1, x.shape[-1] // HD):
        out = combine(out, x[..., i * HD : (i + 1) * HD])
    return out


def stacked_heads(q_ref, heads):
    m = q_ref.shape[0] * q_ref.shape[1]
    q = q_ref[...].reshape(m, heads * HD)
    return jnp.concatenate([q[:, h * HD : (h + 1) * HD] for h in range(heads)], 0)


def softmax_parts(qs, heads, parts, scale2, s_ref):
    m = qs.shape[0] // heads
    top = None
    at = 0
    for n, load, bias in parts:
        s = lax.dot_general(qs, load()[:, :HD], NT, preferred_element_type=jnp.float32)
        s = s.reshape(heads, m, n) * scale2 + bias()[None]
        s_ref[:, :, at : at + n] = s
        most = lane_tiles(jnp.maximum, s)
        top = most if top is None else jnp.maximum(top, most)
        at += n
    top = jnp.max(top, -1, keepdims=True)
    total = mixed = None
    at = 0
    for n, load, _ in parts:
        w = jnp.exp2(s_ref[:, :, at : at + n] - top)
        summed = lane_tiles(jnp.add, w)
        one = jnp.dot(
            w.astype(jnp.bfloat16).reshape(heads * m, n),
            load()[:, HD:],
            preferred_element_type=jnp.float32,
        ).reshape(heads, m, HD)
        total = summed if total is None else total + summed
        mixed = one if mixed is None else mixed + one
        at += n
    return top, jnp.sum(total, -1, keepdims=True), mixed


def by_row(values, first, rows, steps):
    lane = lax.broadcasted_iota(jnp.int32, (rows, values.shape[1]), 1)
    row = lax.broadcasted_iota(jnp.int32, (rows, values.shape[1]), 0)
    mine = jnp.where(lane == first + row // steps, values.astype(jnp.float32), 0.0)
    return jnp.sum(mine, 1, keepdims=True)


def shown(allowed):
    return jnp.where(allowed, 0.0, HIDDEN)


def cached_kernel(
    heads, cpages, scale2, start, table_ref, length_ref, q_ref, fork_ref, pool_ref, mixed_ref, stat_ref, s_ref
):
    qs = stacked_heads(q_ref, heads)
    m = qs.shape[0] // heads
    block, steps = q_ref.shape[:2]
    prompt = by_row(fork_ref[...], (pl.program_id(0) + start) * block, m, steps)
    pages, size = pool_ref.shape[:2]
    group = 2 * cpages

    def part(at):
        mine = range(at, min(at + group, pages))

        def load():
            return jnp.concatenate([pool_ref[table_ref[i]] for i in mine], 0)

        def bias():
            lane = lax.broadcasted_iota(jnp.int32, (m, size), 1)
            return jnp.concatenate(
                [
                    shown(
                        (prompt == float(i // cpages))
                        & (lane < length_ref[i // cpages] - (i % cpages) * size)
                    )
                    for i in mine
                ],
                1,
            )

        return len(mine) * size, load, bias

    parts = [part(at) for at in range(0, pages, group)]
    top, total, mixed = softmax_parts(qs, heads, parts, scale2, s_ref)
    mixed_ref[...] = mixed
    lane = lax.broadcasted_iota(jnp.int32, mixed.shape, 2)
    stat_ref[...] = jnp.where(lane < HD // 2, top, total)


def new_kernel(
    heads, steps, scale2, start, owner_ref, base_ref, q_ref, fork_ref, tail_ref, mixed_ref, stat_ref, *refs
):
    span_refs, o_ref, s_ref = refs[:-2], refs[-2], refs[-1]
    qs = stacked_heads(q_ref, heads)
    m = qs.shape[0] // heads
    span = span_refs[0].shape[0]
    prompt = by_row(fork_ref[...], (pl.program_id(0) + start) * q_ref.shape[0], m, steps)

    def loaded():
        return jnp.concatenate([ref[...] for ref in span_refs], 0)

    def owned():
        return jnp.concatenate(
            [
                jnp.broadcast_to(
                    shown(prompt == owner_ref[base_ref[0] ^ j].astype(jnp.float32)), (m, span)
                )
                for j in range(len(span_refs))
            ],
            1,
        )

    def causal():
        row = lax.broadcasted_iota(jnp.int32, (m, m), 0)
        col = lax.broadcasted_iota(jnp.int32, (m, m), 1)
        return shown((row // steps == col // steps) & (col <= row))

    parts = (
        (span * len(span_refs), loaded, owned),
        (m, lambda: tail_ref[...], causal),
    )
    top, total, mixed = softmax_parts(qs, heads, parts, scale2, s_ref)
    old_top = stat_ref[:, :, :1]
    old_total = stat_ref[:, :, HD // 2 : HD // 2 + 1]
    both = jnp.maximum(top, old_top)
    new_share = jnp.exp2(top - both)
    old_share = jnp.exp2(old_top - both)
    total = total * new_share + old_total * old_share
    mixed = mixed * new_share + mixed_ref[...] * old_share
    out = (mixed / total).astype(jnp.bfloat16)
    for h in range(heads):
        o_ref[:, h * HD : (h + 1) * HD] = out[h]


def attend_cached(q, fork_row, page_table, prompt_length, pool, start, count):
    steps, width = q.shape[1:]
    heads = width // HD
    block = min(SET_ROWS, q.shape[0])
    m = block * steps
    cached = pool.shape[0] * pool.shape[1]
    cpages = pool.shape[0] // prompt_length.shape[0]
    return pl.pallas_call(
        functools.partial(cached_kernel, heads, cpages, LOG2E / math.sqrt(HD), start),
        grid_spec=pltpu.PrefetchScalarGridSpec(
            num_scalar_prefetch=2,
            grid=(count,),
            in_specs=[
                pl.BlockSpec((block, steps, width), lambda i, *_: (i + start, 0, 0)),
                pl.BlockSpec(fork_row.shape, lambda i, *_: (0, 0)),
                pl.BlockSpec(pool.shape, lambda i, *_: (0, 0, 0)),
            ],
            out_specs=[pl.BlockSpec((heads, m, HD), lambda i, *_: (0, i, 0))] * 2,
            scratch_shapes=[pltpu.VMEM((heads, m, cached), jnp.float32)],
        ),
        out_shape=[jax.ShapeDtypeStruct((heads, m * count, HD), jnp.float32)] * 2,
        cost_estimate=pl.CostEstimate(
            flops=4 * count * heads * m * cached * HD,
            transcendentals=count * heads * m * cached,
            bytes_accessed=8 * count * heads * m * HD,
        ),
        compiler_params=SMALL,
        name="attend_cached",
    )(page_table, prompt_length, in_hbm(q), fork_row, in_hbm(pool))


def attend_new(q, fork_row, owner, base, span_pairs, tail_pairs, mixed, stat, start, count):
    steps, width = q.shape[1:]
    heads = width // HD
    block = min(SET_ROWS, q.shape[0])
    m = block * steps
    span = span_pairs[0].shape[0]
    keys = span * len(span_pairs)
    part = pl.BlockSpec((heads, m, HD), lambda i, *_: (0, i, 0))
    return pl.pallas_call(
        functools.partial(new_kernel, heads, steps, LOG2E / math.sqrt(HD), start),
        grid_spec=pltpu.PrefetchScalarGridSpec(
            num_scalar_prefetch=2,
            grid=(count,),
            in_specs=[
                pl.BlockSpec((block, steps, width), lambda i, *_: (i + start, 0, 0)),
                pl.BlockSpec(fork_row.shape, lambda i, *_: (0, 0)),
                pl.BlockSpec((m, 2 * HD), lambda i, *_: (i, 0)),
                part,
                part,
            ]
            + [pl.BlockSpec((span, 2 * HD), lambda i, *_: (0, 0))] * len(span_pairs),
            out_specs=pl.BlockSpec((m, width), lambda i, *_: (i, 0)),
            scratch_shapes=[pltpu.VMEM((heads, m, keys + m), jnp.float32)],
        ),
        out_shape=jax.ShapeDtypeStruct((m * count, width), jnp.bfloat16),
        cost_estimate=pl.CostEstimate(
            flops=4 * count * heads * m * (keys + m) * HD,
            transcendentals=count * heads * m * (keys + m),
            bytes_accessed=10 * count * heads * m * HD,
        ),
        compiler_params=SMALL,
        name="attend_new",
    )(owner, base, in_hbm(q), fork_row, tail_pairs, mixed, stat, *span_pairs)


def project_kernel(groups, split, kept, sent, rank_ref, *refs):
    keep_ref, send_ref, acc = refs[-3:]
    s = pl.program_id(0)
    rows = [ref[...].reshape(-1, ref.shape[-1]) for ref in refs[:groups]]
    x = rows[0] if groups == 1 else jnp.concatenate(rows, 0)
    refs = refs[groups:]
    w = jnp.concatenate(
        [jnp.concatenate([refs[2 * i][...], refs[2 * i + 1][...]], 1) for i in range(split)], 0
    )
    one = jnp.dot(x, w, preferred_element_type=jnp.float32)

    @pl.when(s == 0)
    def _():
        acc[...] = one

    @pl.when(s > 0)
    def _():
        acc[...] += one

    @pl.when(s == pl.num_programs(0) - 1)
    def _():
        keys = acc.shape[1] // 2
        for ref, rels in ((send_ref, sent), (keep_ref, kept)):
            for i, rel in enumerate(rels):
                at = pl.multiple_of((rank_ref[0] ^ rel) * HD, HD)
                ref[i, :, :HD] = acc[:, pl.ds(at, HD)].astype(ref.dtype)
                ref[i, :, HD:] = acc[:, pl.ds(pl.multiple_of(at + keys, HD), HD)].astype(ref.dtype)


def project(rank, groups, key_weight, value_weight, kept, sent):
    width, columns = key_weight.shape
    depth, split = width // 2, 2
    in_specs = []
    n = 0
    for x, start, rows in groups:
        lead = (rows,) + x.shape[1:-1]
        n += math.prod(lead)
        in_specs.append(
            pl.BlockSpec(
                tuple(pl.Element(d) for d in lead + (depth,)),
                lambda s, r, start=start, lead=lead: (start,) + (0,) * (len(lead) - 1) + (s * depth,),
            )
        )
    for i in range(split):
        piece = pl.BlockSpec((depth // split, columns), lambda s, r, i=i: (s * split + i, 0))
        in_specs += [piece, piece]
    return pl.pallas_call(
        functools.partial(project_kernel, len(groups), split, kept, sent),
        grid_spec=pltpu.PrefetchScalarGridSpec(
            num_scalar_prefetch=1,
            grid=(width // depth,),
            in_specs=in_specs,
            out_specs=[
                pl.BlockSpec((len(rels), n, 2 * HD), lambda s, r: (0, 0, 0)) for rels in (kept, sent)
            ],
            scratch_shapes=[pltpu.VMEM((n, 2 * columns), jnp.float32)],
        ),
        out_shape=[
            jax.ShapeDtypeStruct((len(kept), n, 2 * HD), jnp.float32),
            jax.ShapeDtypeStruct((len(sent), n, 2 * HD), jnp.bfloat16),
        ],
        cost_estimate=pl.CostEstimate(
            flops=4 * n * width * columns, transcendentals=0, bytes_accessed=4 * width * columns
        ),
        compiler_params=SMALL,
        name="project",
    )(
        rank,
        *[in_hbm(x) for x, _, _ in groups],
        *([in_hbm(key_weight), in_hbm(value_weight)] * split),
    )


def finish_kernel(
    span, steps, start, sizes, owner_ref, length_ref, replica_ref, fork_ref, freq_ref, keep_ref, *refs
):
    outs = refs[-len(sizes) :]
    summed = keep_ref[0]
    for ref in refs[: -len(sizes)]:
        summed = summed + (ref[0] if len(ref.shape) == 3 else ref[...]).astype(jnp.float32)
    n = summed.shape[0]
    fork = fork_ref[...]
    lengths = jnp.zeros_like(fork)
    for p in range(length_ref.shape[0]):
        lengths = jnp.where(fork == p, length_ref[p], lengths)
    lead = max(0, span - start)
    places = []
    if lead:
        own = length_ref[owner_ref[replica_ref[0]]]
        places.append(own + start + lax.broadcasted_iota(jnp.int32, (lead, 1), 0).astype(jnp.int32))
        places[0] = places[0].astype(jnp.float32)
    tail = n - lead
    first = start + lead - span
    step = lax.broadcasted_iota(jnp.int32, (tail, 1), 0) % steps
    places.append(
        by_row(lengths, first // steps, tail, steps) + (span + step).astype(jnp.float32)
    )
    places = places[0] if len(places) == 1 else jnp.concatenate(places, 0)
    angle = places * freq_ref[...]
    lane = lax.broadcasted_iota(jnp.int32, (n, HD), 1)
    sine = jnp.where(lane < HD // 2, -jnp.sin(angle), jnp.sin(angle))
    keys = summed[:, :HD]
    turned = keys * jnp.cos(angle) + pltpu.roll(keys, HD // 2, 1) * sine
    at = 0
    for size, o_ref in zip(sizes, outs):
        o_ref[:, :HD] = turned[at : at + size].astype(jnp.bfloat16)
        o_ref[:, HD:] = summed[at : at + size, HD:].astype(jnp.bfloat16)
        at += size


def finish(keep, others, places, start, sizes):
    span, steps, owner, length, replica, fork_row, freq = places
    n = keep.shape[1]
    unit = pl.BlockSpec((1, n, 2 * HD), lambda i, *_: (0, 0, 0))
    flat = lambda rows, width: pl.BlockSpec((rows, width), lambda i, *_: (0, 0))
    return pl.pallas_call(
        functools.partial(finish_kernel, span, steps, start, sizes),
        grid_spec=pltpu.PrefetchScalarGridSpec(
            num_scalar_prefetch=3,
            grid=(1,),
            in_specs=[flat(*fork_row.shape), flat(*freq.shape), unit]
            + [unit if x.ndim == 3 else flat(n, 2 * HD) for x in others],
            out_specs=[flat(size, 2 * HD) for size in sizes],
        ),
        out_shape=[jax.ShapeDtypeStruct((size, 2 * HD), jnp.bfloat16) for size in sizes],
        compiler_params=SMALL,
        name="finish",
    )(owner, length, replica, fork_row, freq, keep, *others)


def swap(x, axis, bit):
    return lax.ppermute(x, axis, [(i, i ^ bit) for i in range(lax.axis_size(axis))])


def swap_sum(keep, send, places, start, sizes):
    got = swap(send, "tensor", 1)
    half = (keep[1] + got[1].astype(jnp.float32)).astype(jnp.bfloat16)
    last = swap(half, "tensor", 2)
    return finish(keep, (got, last), places, start, sizes)


def out_kernel(rels, pick, cuts, add, final, rank_ref, *refs):
    refs = list(refs)
    pieces = [refs.pop(0) for _ in rels]
    other = refs.pop(0) if pick else None
    partial = refs.pop(0) if add else None
    w_ref, o_ref, buf, sem = refs[0], refs[-3], refs[-2], refs[-1]
    width = pieces[0].shape[1]
    depth = width // cuts
    rank = rank_ref[0]
    copies = []
    for p, rel in enumerate(rels):
        for c in range(cuts):
            row = pl.multiple_of((rank ^ rel) * width + c * depth, depth)
            slot = p * cuts + c
            copies.append(
                pltpu.make_async_copy(w_ref.at[pl.ds(row, depth), :], buf.at[slot], sem.at[slot])
            )
            copies[-1].start()
    total = partial[...] if add else None
    for p in range(len(rels)):
        a = pieces[p][...]
        if pick and p == len(rels) - 1:
            inner = (rank == 1) | (rank == 2)
            a = jnp.where(inner, a, other[...])
        for c in range(cuts):
            slot = p * cuts + c
            copies[slot].wait()
            one = jnp.dot(
                a[:, c * depth : (c + 1) * depth], buf[slot], preferred_element_type=jnp.float32
            )
            total = one if total is None else total + one
    o_ref[...] = total.reshape(o_ref.shape).astype(o_ref.dtype)


def out_project(rank, pieces, rels, weight, shape, start, pick=None, partial=None, into=None, final=True):
    m, width = pieces[0].shape
    columns = weight.shape[1]
    steps = shape[1]
    cuts = 4
    flat = lambda w: pl.BlockSpec((m, w), lambda i, r: (0, 0))
    args = list(pieces)
    in_specs = [flat(width) for _ in pieces]
    if pick is not None:
        args.append(pick)
        in_specs.append(flat(width))
    if partial is not None:
        args.append(partial)
        in_specs.append(flat(columns))
    args.append(in_hbm(weight))
    in_specs.append(pl.BlockSpec(memory_space=pl.ANY))
    aliases = {}
    if into is not None:
        args.append(into)
        in_specs.append(pl.BlockSpec(memory_space=pl.ANY))
        aliases = {len(args): 0}
    if final:
        out_spec = pl.BlockSpec(
            (pl.Element(m // steps), pl.Element(steps), pl.Element(columns)),
            lambda i, r: (start, 0, 0),
        )
        out_shape = jax.ShapeDtypeStruct(shape, jnp.bfloat16)
    else:
        out_spec = flat(columns)
        out_shape = jax.ShapeDtypeStruct((m, columns), jnp.float32)
    slots = len(rels) * cuts
    return pl.pallas_call(
        functools.partial(out_kernel, rels, pick is not None, cuts, partial is not None, final),
        grid_spec=pltpu.PrefetchScalarGridSpec(
            num_scalar_prefetch=1,
            grid=(1,),
            in_specs=in_specs,
            out_specs=out_spec,
            scratch_shapes=[
                pltpu.VMEM((slots, width // cuts, columns), jnp.bfloat16),
                pltpu.SemaphoreType.DMA((slots,)),
            ],
        ),
        out_shape=out_shape,
        input_output_aliases=aliases,
        cost_estimate=pl.CostEstimate(
            flops=2 * m * width * columns * len(rels),
            transcendentals=0,
            bytes_accessed=2 * width * columns * len(rels),
        ),
        compiler_params=LARGE,
        name="out_project",
    )(rank, *args)


def gather_heads(own):
    far = swap(own, "tensor", 2)
    near = swap(own, "tensor", 1)
    across = lax.ppermute(own, "tensor", [(1, 2), (2, 1)])
    passed = lax.ppermute(far, "tensor", [(1, 0), (2, 3)])
    return far, near, across, passed


def on_device(
    prompt_owner,
    fork_map,
    page_table,
    prompt_length,
    span_states,
    decode_states,
    decode_queries,
    key_weight,
    value_weight,
    out_weight,
    page_pool,
):
    replica = lax.axis_index("replica")
    device_rank = lax.axis_index("tensor")
    n_replica = lax.axis_size("replica")
    n_tensor = lax.axis_size("tensor")
    span = span_states.shape[0]
    rows, steps, width = decode_states.shape
    kv_heads = key_weight.shape[1] // HD
    sharing = n_tensor // kv_heads
    prompts = jnp.arange(n_replica, dtype=jnp.int32)
    own_prompt = jnp.sum(jnp.where(prompts == replica, prompt_owner, 0))
    own_length = jnp.sum(jnp.where(prompts == own_prompt, prompt_length, 0))
    row_hits = fork_map[:, None] == prompts[None, :]
    row_length = jnp.sum(jnp.where(row_hits, prompt_length[None, :], 0), 1)
    span_places = own_length + jnp.arange(span, dtype=jnp.int32)
    tail_places = (
        row_length[:, None] + span + jnp.arange(steps, dtype=jnp.int32)[None, :]
    ).reshape(-1)
    pool = page_pool.reshape(page_pool.shape[1:])
    short_line = n_tensor == kv_heads == 4 and n_replica == 4
    first = min(SET_ROWS, rows)
    blocks = rows // first

    if not short_line:
        positions = jnp.concatenate([span_places, tail_places])
        tokens = jnp.concatenate([span_states, decode_states.reshape(rows * steps, width)], 0)
        projected = jnp.dot(
            tokens,
            jnp.concatenate([key_weight, value_weight], 1),
            preferred_element_type=jnp.float32,
        )
        share = lax.psum_scatter(projected, "tensor", scatter_dimension=0, tiled=True)
        number = share.shape[0]
        places = lax.dynamic_slice_in_dim(positions, device_rank * number, number)
        turned = rotate_round(share, places, kv_heads)
        groups = jnp.stack([own_pair(turned, g, kv_heads) for g in range(kv_heads)], 0)
        outgoing = jnp.repeat(groups, sharing, axis=0)
        paired = lax.all_to_all(
            outgoing, "tensor", split_axis=0, concat_axis=1, tiled=True
        ).reshape(-1, 2 * HD)
        arrived = lax.all_gather(paired[:span], "replica", axis=0, tiled=True)
        mixed, stat = attend_cached(
            decode_queries, fork_map[None, :], page_table, prompt_length, pool, 0, blocks
        )
        own = attend_new(
            decode_queries,
            fork_map[None, :],
            prompt_owner,
            jnp.zeros((1,), jnp.int32),
            jnp.split(arrived, n_replica),
            paired[span:],
            mixed,
            stat,
            0,
            blocks,
        )
        decoded = jnp.dot(
            lax.all_gather(own, "tensor", axis=1, tiled=True),
            out_weight,
            preferred_element_type=jnp.float32,
        )
        return decoded.astype(jnp.bfloat16).reshape(rows, steps, out_weight.shape[1])

    rank = device_rank.reshape(1).astype(jnp.int32)
    return line_of_four(
        rank, replica.reshape(1).astype(jnp.int32), prompt_owner, fork_map, page_table,
        prompt_length, span_states, decode_states, decode_queries, key_weight, value_weight,
        out_weight, pool,
    )


def line_of_four(
    rank, replica, prompt_owner, fork_map, page_table, prompt_length, span_states, decode_states,
    decode_queries, key_weight, value_weight, out_weight, pool,
):
    n_replica = lax.axis_size("replica")
    span = span_states.shape[0]
    rows, steps, _ = decode_states.shape
    first = min(SET_ROWS, rows)
    blocks = rows // first
    middle = blocks - 2
    cut = first * steps

    first_units = project(
        rank, ((span_states, 0, span), (decode_states, 0, first)), key_weight, value_weight,
        (0, 2), (1, 3),
    )
    rest_units = project(
        rank, ((decode_states, first, rows - first),), key_weight, value_weight, (0, 2), (1, 3)
    )
    fork_row = fork_map[None, :]
    half = rope_base ** (-(2.0 / HD) * jnp.arange(HD // 2, dtype=jnp.float32))
    freq = jnp.concatenate([half, half])[None, :]
    places = (span, steps, prompt_owner, prompt_length, replica, fork_row, freq)
    own_span, first_tail = swap_sum(*first_units, places, 0, (span, cut))
    arrived = [own_span]
    for j in range(1, n_replica):
        arrived.append(swap(own_span, "replica", j))
    middle_tail, last_tail = swap_sum(*rest_units, places, span + cut, (middle * cut, cut))

    def attended(tail, start, count):
        old = attend_cached(decode_queries, fork_row, page_table, prompt_length, pool, start, count)
        return attend_new(
            decode_queries, fork_row, prompt_owner, replica, arrived, tail, *old, start, count
        )

    shape = (rows, steps, out_weight.shape[1])
    first_own = attended(first_tail, 0, 1)
    middle_own = attended(middle_tail, 1, middle)
    last_own = attended(last_tail, blocks - 1, 1)
    far, near, across, passed = gather_heads(first_own)
    decoded = out_project(
        rank, [first_own, far, near, across], (0, 2, 1, 3), out_weight, shape, 0, pick=passed
    )
    far, near, across, passed = gather_heads(middle_own)
    partial = out_project(
        rank, [middle_own, far, near], (0, 2, 1), out_weight, shape, 0, final=False
    )
    decoded = out_project(
        rank, [across], (3,), out_weight, shape, first, pick=passed, partial=partial, into=decoded
    )
    far, near, across, passed = gather_heads(last_own)
    partial = out_project(rank, [last_own, far, near], (0, 2, 1), out_weight, shape, 0, final=False)
    return out_project(
        rank, [across], (3,), out_weight, shape, first * (blocks - 1),
        pick=passed, partial=partial, into=decoded,
    )


def solution(mesh):
    in_specs = (
        P("parts"),
        P(("parts", "replica")),
        P("parts"),
        P("parts"),
        P(("parts", "replica"), "tensor"),
        P(("parts", "replica"), None, "tensor"),
        P(("parts", "replica"), None, "tensor"),
        P("tensor", None),
        P("tensor", None),
        P(None, "tensor"),
        P("tensor", "parts", None, None),
    )
    out_specs = P(("parts", "replica"), None, "tensor")
    return jax.shard_map(
        on_device, mesh=mesh, in_specs=in_specs, out_specs=out_specs, check_vma=False
    )
```

```python
import functools
import math

import jax
import jax.numpy as jnp
from jax import lax
from jax.experimental import pallas as pl
from jax.experimental.pallas import tpu as pltpu
from jax.sharding import PartitionSpec as P


HD = 128
rope_base = 1000000.0
LOG2E = math.log2(math.e)
HIDDEN = -1e30


def rotary(vectors, places):
    half = vectors.shape[-1] // 2
    freq = rope_base ** (-(2.0 / vectors.shape[-1]) * jnp.arange(half, dtype=jnp.float32))
    angle = places.astype(jnp.float32)[..., None, None] * freq
    cosine = jnp.cos(angle)
    sine = jnp.sin(angle)
    first = vectors[..., :half]
    second = vectors[..., half:]
    return jnp.concatenate([first * cosine - second * sine, second * cosine + first * sine], -1)


def rotate_round(summed, places, kv_heads):
    number = summed.shape[0]
    turned = rotary(summed[:, : kv_heads * HD].reshape(number, kv_heads, HD), places)
    turned = turned.astype(jnp.bfloat16).reshape(number, kv_heads * HD)
    return jnp.concatenate([turned, summed[:, kv_heads * HD :].astype(jnp.bfloat16)], 1)


def own_pair(packed, head_group, kv_heads):
    key_part = lax.dynamic_slice_in_dim(packed, head_group * HD, HD, 1)
    value_part = lax.dynamic_slice_in_dim(packed, (kv_heads + head_group) * HD, HD, 1)
    return jnp.concatenate([key_part, value_part], 1)


NT = (((1,), (1,)), ((), ()))
SMALL = pltpu.CompilerParams(vmem_limit_bytes=24 << 20)
LARGE = pltpu.CompilerParams(vmem_limit_bytes=36 << 20)
SET_ROWS = 32


def in_hbm(x):
    return pltpu.with_memory_space_constraint(x, pltpu.HBM)


def lane_tiles(combine, x):
    out = x[..., :HD]
    for i in range(1, x.shape[-1] // HD):
        out = combine(out, x[..., i * HD : (i + 1) * HD])
    return out


def stacked_heads(q_ref, heads):
    m = q_ref.shape[0] * q_ref.shape[1]
    q = q_ref[...].reshape(m, heads * HD)
    return jnp.concatenate([q[:, h * HD : (h + 1) * HD] for h in range(heads)], 0)


def softmax_parts(qs, heads, parts, scale2, s_ref):
    m = qs.shape[0] // heads
    top = None
    at = 0
    for n, load, bias in parts:
        s = lax.dot_general(qs, load()[:, :HD], NT, preferred_element_type=jnp.float32)
        s = s.reshape(heads, m, n) * scale2 + bias()[None]
        s_ref[:, :, at : at + n] = s
        most = lane_tiles(jnp.maximum, s)
        top = most if top is None else jnp.maximum(top, most)
        at += n
    top = jnp.max(top, -1, keepdims=True)
    total = mixed = None
    at = 0
    for n, load, _ in parts:
        w = jnp.exp2(s_ref[:, :, at : at + n] - top)
        summed = lane_tiles(jnp.add, w)
        one = jnp.dot(
            w.astype(jnp.bfloat16).reshape(heads * m, n),
            load()[:, HD:],
            preferred_element_type=jnp.float32,
        ).reshape(heads, m, HD)
        total = summed if total is None else total + summed
        mixed = one if mixed is None else mixed + one
        at += n
    return top, jnp.sum(total, -1, keepdims=True), mixed


def by_row(values, first, rows, steps):
    lane = lax.broadcasted_iota(jnp.int32, (rows, values.shape[1]), 1)
    row = lax.broadcasted_iota(jnp.int32, (rows, values.shape[1]), 0)
    mine = jnp.where(lane == first + row // steps, values.astype(jnp.float32), 0.0)
    return jnp.sum(mine, 1, keepdims=True)


def shown(allowed):
    return jnp.where(allowed, 0.0, HIDDEN)


def cached_kernel(
    heads, cpages, scale2, start, table_ref, length_ref, q_ref, fork_ref, pool_ref, mixed_ref, stat_ref, s_ref
):
    qs = stacked_heads(q_ref, heads)
    m = qs.shape[0] // heads
    block, steps = q_ref.shape[:2]
    prompt = by_row(fork_ref[...], (pl.program_id(0) + start) * block, m, steps)
    pages, size = pool_ref.shape[:2]
    group = 2 * cpages

    def part(at):
        mine = range(at, min(at + group, pages))

        def load():
            return jnp.concatenate([pool_ref[table_ref[i]] for i in mine], 0)

        def bias():
            lane = lax.broadcasted_iota(jnp.int32, (m, size), 1)
            return jnp.concatenate(
                [
                    shown(
                        (prompt == float(i // cpages))
                        & (lane < length_ref[i // cpages] - (i % cpages) * size)
                    )
                    for i in mine
                ],
                1,
            )

        return len(mine) * size, load, bias

    parts = [part(at) for at in range(0, pages, group)]
    top, total, mixed = softmax_parts(qs, heads, parts, scale2, s_ref)
    mixed_ref[...] = mixed
    lane = lax.broadcasted_iota(jnp.int32, mixed.shape, 2)
    stat_ref[...] = jnp.where(lane < HD // 2, top, total)


def new_kernel(
    heads, steps, scale2, start, owner_ref, base_ref, q_ref, fork_ref, tail_ref, mixed_ref, stat_ref, *refs
):
    span_refs, o_ref, s_ref = refs[:-2], refs[-2], refs[-1]
    qs = stacked_heads(q_ref, heads)
    m = qs.shape[0] // heads
    span = span_refs[0].shape[0]
    prompt = by_row(fork_ref[...], (pl.program_id(0) + start) * q_ref.shape[0], m, steps)

    def loaded():
        return jnp.concatenate([ref[...] for ref in span_refs], 0)

    def owned():
        return jnp.concatenate(
            [
                jnp.broadcast_to(
                    shown(prompt == owner_ref[base_ref[0] ^ j].astype(jnp.float32)), (m, span)
                )
                for j in range(len(span_refs))
            ],
            1,
        )

    def causal():
        row = lax.broadcasted_iota(jnp.int32, (m, m), 0)
        col = lax.broadcasted_iota(jnp.int32, (m, m), 1)
        return shown((row // steps == col // steps) & (col <= row))

    parts = (
        (span * len(span_refs), loaded, owned),
        (m, lambda: tail_ref[...], causal),
    )
    top, total, mixed = softmax_parts(qs, heads, parts, scale2, s_ref)
    old_top = stat_ref[:, :, :1]
    old_total = stat_ref[:, :, HD // 2 : HD // 2 + 1]
    both = jnp.maximum(top, old_top)
    new_share = jnp.exp2(top - both)
    old_share = jnp.exp2(old_top - both)
    total = total * new_share + old_total * old_share
    mixed = mixed * new_share + mixed_ref[...] * old_share
    out = (mixed / total).astype(jnp.bfloat16)
    for h in range(heads):
        o_ref[:, h * HD : (h + 1) * HD] = out[h]


def attend_cached(q, fork_row, page_table, prompt_length, pool, start, count):
    steps, width = q.shape[1:]
    heads = width // HD
    block = min(SET_ROWS, q.shape[0])
    m = block * steps
    cached = pool.shape[0] * pool.shape[1]
    cpages = pool.shape[0] // prompt_length.shape[0]
    return pl.pallas_call(
        functools.partial(cached_kernel, heads, cpages, LOG2E / math.sqrt(HD), start),
        grid_spec=pltpu.PrefetchScalarGridSpec(
            num_scalar_prefetch=2,
            grid=(count,),
            in_specs=[
                pl.BlockSpec((block, steps, width), lambda i, *_: (i + start, 0, 0)),
                pl.BlockSpec(fork_row.shape, lambda i, *_: (0, 0)),
                pl.BlockSpec(pool.shape, lambda i, *_: (0, 0, 0)),
            ],
            out_specs=[pl.BlockSpec((heads, m, HD), lambda i, *_: (0, i, 0))] * 2,
            scratch_shapes=[pltpu.VMEM((heads, m, cached), jnp.float32)],
        ),
        out_shape=[jax.ShapeDtypeStruct((heads, m * count, HD), jnp.float32)] * 2,
        cost_estimate=pl.CostEstimate(
            flops=4 * count * heads * m * cached * HD,
            transcendentals=count * heads * m * cached,
            bytes_accessed=8 * count * heads * m * HD,
        ),
        compiler_params=SMALL,
        name="attend_cached",
    )(page_table, prompt_length, q, fork_row, pool)


def attend_new(q, fork_row, owner, base, span_pairs, tail_pairs, mixed, stat, start, count):
    steps, width = q.shape[1:]
    heads = width // HD
    block = min(SET_ROWS, q.shape[0])
    m = block * steps
    span = span_pairs[0].shape[0]
    keys = span * len(span_pairs)
    part = pl.BlockSpec((heads, m, HD), lambda i, *_: (0, i, 0))
    return pl.pallas_call(
        functools.partial(new_kernel, heads, steps, LOG2E / math.sqrt(HD), start),
        grid_spec=pltpu.PrefetchScalarGridSpec(
            num_scalar_prefetch=2,
            grid=(count,),
            in_specs=[
                pl.BlockSpec((block, steps, width), lambda i, *_: (i + start, 0, 0)),
                pl.BlockSpec(fork_row.shape, lambda i, *_: (0, 0)),
                pl.BlockSpec((m, 2 * HD), lambda i, *_: (i, 0)),
                part,
                part,
            ]
            + [pl.BlockSpec((span, 2 * HD), lambda i, *_: (0, 0))] * len(span_pairs),
            out_specs=pl.BlockSpec((m, width), lambda i, *_: (i, 0)),
            scratch_shapes=[pltpu.VMEM((heads, m, keys + m), jnp.float32)],
        ),
        out_shape=jax.ShapeDtypeStruct((m * count, width), jnp.bfloat16),
        cost_estimate=pl.CostEstimate(
            flops=4 * count * heads * m * (keys + m) * HD,
            transcendentals=count * heads * m * (keys + m),
            bytes_accessed=10 * count * heads * m * HD,
        ),
        compiler_params=SMALL,
        name="attend_new",
    )(owner, base, q, fork_row, tail_pairs, mixed, stat, *span_pairs)


def project_kernel(groups, split, kept, sent, rank_ref, *refs):
    keep_ref, send_ref, acc = refs[-3:]
    s = pl.program_id(0)
    rows = [ref[...].reshape(-1, ref.shape[-1]) for ref in refs[:groups]]
    x = rows[0] if groups == 1 else jnp.concatenate(rows, 0)
    refs = refs[groups:]
    w = jnp.concatenate(
        [jnp.concatenate([refs[2 * i][...], refs[2 * i + 1][...]], 1) for i in range(split)], 0
    )
    one = jnp.dot(x, w, preferred_element_type=jnp.float32)

    @pl.when(s == 0)
    def _():
        acc[...] = one

    @pl.when(s > 0)
    def _():
        acc[...] += one

    @pl.when(s == pl.num_programs(0) - 1)
    def _():
        keys = acc.shape[1] // 2
        for ref, rels in ((send_ref, sent), (keep_ref, kept)):
            for i, rel in enumerate(rels):
                at = pl.multiple_of((rank_ref[0] ^ rel) * HD, HD)
                ref[i, :, :HD] = acc[:, pl.ds(at, HD)].astype(ref.dtype)
                ref[i, :, HD:] = acc[:, pl.ds(pl.multiple_of(at + keys, HD), HD)].astype(ref.dtype)


def project(rank, groups, key_weight, value_weight, kept, sent):
    width, columns = key_weight.shape
    depth, split = width // 2, 2
    in_specs = []
    n = 0
    for x, start, rows in groups:
        lead = (rows,) + x.shape[1:-1]
        n += math.prod(lead)
        in_specs.append(
            pl.BlockSpec(
                tuple(pl.Element(d) for d in lead + (depth,)),
                lambda s, r, start=start, lead=lead: (start,) + (0,) * (len(lead) - 1) + (s * depth,),
            )
        )
    for i in range(split):
        piece = pl.BlockSpec((depth // split, columns), lambda s, r, i=i: (s * split + i, 0))
        in_specs += [piece, piece]
    return pl.pallas_call(
        functools.partial(project_kernel, len(groups), split, kept, sent),
        grid_spec=pltpu.PrefetchScalarGridSpec(
            num_scalar_prefetch=1,
            grid=(width // depth,),
            in_specs=in_specs,
            out_specs=[
                pl.BlockSpec((len(rels), n, 2 * HD), lambda s, r: (0, 0, 0)) for rels in (kept, sent)
            ],
            scratch_shapes=[pltpu.VMEM((n, 2 * columns), jnp.float32)],
        ),
        out_shape=[
            jax.ShapeDtypeStruct((len(kept), n, 2 * HD), jnp.float32),
            jax.ShapeDtypeStruct((len(sent), n, 2 * HD), jnp.bfloat16),
        ],
        cost_estimate=pl.CostEstimate(
            flops=4 * n * width * columns, transcendentals=0, bytes_accessed=4 * width * columns
        ),
        compiler_params=SMALL,
        name="project",
    )(
        rank,
        *[in_hbm(x) for x, _, _ in groups],
        *([in_hbm(key_weight), in_hbm(value_weight)] * split),
    )


def finish_kernel(
    span, steps, start, sizes, owner_ref, length_ref, replica_ref, fork_ref, freq_ref, keep_ref, *refs
):
    outs = refs[-len(sizes) :]
    summed = keep_ref[0]
    for ref in refs[: -len(sizes)]:
        summed = summed + (ref[0] if len(ref.shape) == 3 else ref[...]).astype(jnp.float32)
    n = summed.shape[0]
    fork = fork_ref[...]
    lengths = jnp.zeros_like(fork)
    for p in range(length_ref.shape[0]):
        lengths = jnp.where(fork == p, length_ref[p], lengths)
    lead = max(0, span - start)
    places = []
    if lead:
        own = length_ref[owner_ref[replica_ref[0]]]
        places.append(own + start + lax.broadcasted_iota(jnp.int32, (lead, 1), 0).astype(jnp.int32))
        places[0] = places[0].astype(jnp.float32)
    tail = n - lead
    first = start + lead - span
    step = lax.broadcasted_iota(jnp.int32, (tail, 1), 0) % steps
    places.append(
        by_row(lengths, first // steps, tail, steps) + (span + step).astype(jnp.float32)
    )
    places = places[0] if len(places) == 1 else jnp.concatenate(places, 0)
    angle = places * freq_ref[...]
    lane = lax.broadcasted_iota(jnp.int32, (n, HD), 1)
    sine = jnp.where(lane < HD // 2, -jnp.sin(angle), jnp.sin(angle))
    keys = summed[:, :HD]
    turned = keys * jnp.cos(angle) + pltpu.roll(keys, HD // 2, 1) * sine
    at = 0
    for size, o_ref in zip(sizes, outs):
        o_ref[:, :HD] = turned[at : at + size].astype(jnp.bfloat16)
        o_ref[:, HD:] = summed[at : at + size, HD:].astype(jnp.bfloat16)
        at += size


def finish(keep, others, places, start, sizes):
    span, steps, owner, length, replica, fork_row, freq = places
    n = keep.shape[1]
    unit = pl.BlockSpec((1, n, 2 * HD), lambda i, *_: (0, 0, 0))
    flat = lambda rows, width: pl.BlockSpec((rows, width), lambda i, *_: (0, 0))
    return pl.pallas_call(
        functools.partial(finish_kernel, span, steps, start, sizes),
        grid_spec=pltpu.PrefetchScalarGridSpec(
            num_scalar_prefetch=3,
            grid=(1,),
            in_specs=[flat(*fork_row.shape), flat(*freq.shape), unit]
            + [unit if x.ndim == 3 else flat(n, 2 * HD) for x in others],
            out_specs=[flat(size, 2 * HD) for size in sizes],
        ),
        out_shape=[jax.ShapeDtypeStruct((size, 2 * HD), jnp.bfloat16) for size in sizes],
        compiler_params=SMALL,
        name="finish",
    )(owner, length, replica, fork_row, freq, keep, *others)


def swap(x, axis, bit):
    return lax.ppermute(x, axis, [(i, i ^ bit) for i in range(lax.axis_size(axis))])


def swap_sum(keep, send, places, start, sizes):
    got = swap(send, "tensor", 1)
    half = (keep[1] + got[1].astype(jnp.float32)).astype(jnp.bfloat16)
    last = swap(half, "tensor", 2)
    return finish(keep, (got, last), places, start, sizes)


def out_kernel(rels, pick, cuts, add, held, rank_ref, *refs):
    refs = list(refs)
    pieces = [refs.pop(0) for _ in rels]
    other = refs.pop(0) if pick else None
    partial = refs.pop(0) if add else None
    w_ref = refs[0]
    o_ref, buf, sem = (refs[-1], None, None) if held else refs[-3:]
    width = pieces[0].shape[1]
    depth = width // cuts
    rank = rank_ref[0]
    copies = []
    for p, rel in enumerate(rels if buf is not None else ()):
        for c in range(cuts):
            row = pl.multiple_of((rank ^ rel) * width + c * depth, depth)
            slot = p * cuts + c
            copies.append(
                pltpu.make_async_copy(w_ref.at[pl.ds(row, depth), :], buf.at[slot], sem.at[slot])
            )
            copies[-1].start()
    total = partial[...] if add else None
    for p in range(len(rels)):
        a = pieces[p][...]
        if pick and p == len(rels) - 1:
            inner = (rank == 1) | (rank == 2)
            a = jnp.where(inner, a, other[...])
        for c in range(cuts):
            slot = p * cuts + c
            if held:
                w = w_ref[c * depth : (c + 1) * depth, :]
            else:
                copies[slot].wait()
                w = buf[slot]
            one = jnp.dot(
                a[:, c * depth : (c + 1) * depth], w, preferred_element_type=jnp.float32
            )
            total = one if total is None else total + one
    o_ref[...] = total.reshape(o_ref.shape).astype(o_ref.dtype)


def out_project(rank, pieces, rels, weight, shape, start, pick=None, partial=None, into=None, final=True, held=False):
    m, width = pieces[0].shape
    columns = weight.shape[1]
    steps = shape[1]
    cuts = 4
    flat = lambda w: pl.BlockSpec((m, w), lambda i, r: (0, 0))
    args = list(pieces)
    in_specs = [flat(width) for _ in pieces]
    if pick is not None:
        args.append(pick)
        in_specs.append(flat(width))
    if partial is not None:
        args.append(partial)
        in_specs.append(flat(columns))
    args.append(weight if held else in_hbm(weight))
    in_specs.append(pl.BlockSpec(memory_space=pltpu.VMEM if held else pl.ANY))
    aliases = {}
    if into is not None:
        args.append(into)
        in_specs.append(pl.BlockSpec(memory_space=pl.ANY))
        aliases = {len(args): 0}
    if final:
        out_spec = pl.BlockSpec(
            (pl.Element(m // steps), pl.Element(steps), pl.Element(columns)),
            lambda i, r: (start, 0, 0),
        )
        out_shape = jax.ShapeDtypeStruct(shape, jnp.bfloat16)
    else:
        out_spec = flat(columns)
        out_shape = jax.ShapeDtypeStruct((m, columns), jnp.float32)
    slots = len(rels) * cuts
    return pl.pallas_call(
        functools.partial(out_kernel, rels, pick is not None, cuts, partial is not None, held),
        grid_spec=pltpu.PrefetchScalarGridSpec(
            num_scalar_prefetch=1,
            grid=(1,),
            in_specs=in_specs,
            out_specs=out_spec,
            scratch_shapes=[]
            if held
            else [
                pltpu.VMEM((slots, width // cuts, columns), jnp.bfloat16),
                pltpu.SemaphoreType.DMA((slots,)),
            ],
        ),
        out_shape=out_shape,
        input_output_aliases=aliases,
        cost_estimate=pl.CostEstimate(
            flops=2 * m * width * columns * len(rels),
            transcendentals=0,
            bytes_accessed=2 * width * columns * len(rels),
        ),
        compiler_params=LARGE,
        name="out_project",
    )(rank, *args)


def hold_kernel(rel, rank_ref, w_ref, o_ref, sem):
    rows = o_ref.shape[0]
    at = pl.multiple_of((rank_ref[0] ^ rel) * rows, rows)
    copy = pltpu.make_async_copy(w_ref.at[pl.ds(at, rows), :], o_ref, sem)
    copy.start()
    copy.wait()


def hold(rank, rel, weight, rows):
    shape = (rows, weight.shape[1])
    held = pl.pallas_call(
        functools.partial(hold_kernel, rel),
        grid_spec=pltpu.PrefetchScalarGridSpec(
            num_scalar_prefetch=1,
            grid=(1,),
            in_specs=[pl.BlockSpec(memory_space=pl.ANY)],
            out_specs=pl.BlockSpec(memory_space=pltpu.VMEM),
            scratch_shapes=[pltpu.SemaphoreType.DMA],
        ),
        out_shape=jax.ShapeDtypeStruct(shape, weight.dtype),
        compiler_params=SMALL,
        name="hold",
    )(rank, in_hbm(weight))
    return pltpu.with_memory_space_constraint(held, pltpu.VMEM)


def gather_heads(own):
    far = swap(own, "tensor", 2)
    near = swap(own, "tensor", 1)
    across = lax.ppermute(own, "tensor", [(1, 2), (2, 1)])
    passed = lax.ppermute(far, "tensor", [(1, 0), (2, 3)])
    return far, near, across, passed


def on_device(
    prompt_owner,
    fork_map,
    page_table,
    prompt_length,
    span_states,
    decode_states,
    decode_queries,
    key_weight,
    value_weight,
    out_weight,
    page_pool,
):
    replica = lax.axis_index("replica")
    device_rank = lax.axis_index("tensor")
    n_replica = lax.axis_size("replica")
    n_tensor = lax.axis_size("tensor")
    span = span_states.shape[0]
    rows, steps, width = decode_states.shape
    kv_heads = key_weight.shape[1] // HD
    sharing = n_tensor // kv_heads
    prompts = jnp.arange(n_replica, dtype=jnp.int32)
    own_prompt = jnp.sum(jnp.where(prompts == replica, prompt_owner, 0))
    own_length = jnp.sum(jnp.where(prompts == own_prompt, prompt_length, 0))
    row_hits = fork_map[:, None] == prompts[None, :]
    row_length = jnp.sum(jnp.where(row_hits, prompt_length[None, :], 0), 1)
    span_places = own_length + jnp.arange(span, dtype=jnp.int32)
    tail_places = (
        row_length[:, None] + span + jnp.arange(steps, dtype=jnp.int32)[None, :]
    ).reshape(-1)
    pool = page_pool.reshape(page_pool.shape[1:])
    short_line = n_tensor == kv_heads == 4 and n_replica == 4
    first = min(SET_ROWS, rows)
    blocks = rows // first

    if not short_line:
        positions = jnp.concatenate([span_places, tail_places])
        tokens = jnp.concatenate([span_states, decode_states.reshape(rows * steps, width)], 0)
        projected = jnp.dot(
            tokens,
            jnp.concatenate([key_weight, value_weight], 1),
            preferred_element_type=jnp.float32,
        )
        share = lax.psum_scatter(projected, "tensor", scatter_dimension=0, tiled=True)
        number = share.shape[0]
        places = lax.dynamic_slice_in_dim(positions, device_rank * number, number)
        turned = rotate_round(share, places, kv_heads)
        groups = jnp.stack([own_pair(turned, g, kv_heads) for g in range(kv_heads)], 0)
        outgoing = jnp.repeat(groups, sharing, axis=0)
        paired = lax.all_to_all(
            outgoing, "tensor", split_axis=0, concat_axis=1, tiled=True
        ).reshape(-1, 2 * HD)
        arrived = lax.all_gather(paired[:span], "replica", axis=0, tiled=True)
        mixed, stat = attend_cached(
            decode_queries, fork_map[None, :], page_table, prompt_length, pool, 0, blocks
        )
        own = attend_new(
            decode_queries,
            fork_map[None, :],
            prompt_owner,
            jnp.zeros((1,), jnp.int32),
            jnp.split(arrived, n_replica),
            paired[span:],
            mixed,
            stat,
            0,
            blocks,
        )
        decoded = jnp.dot(
            lax.all_gather(own, "tensor", axis=1, tiled=True),
            out_weight,
            preferred_element_type=jnp.float32,
        )
        return decoded.astype(jnp.bfloat16).reshape(rows, steps, out_weight.shape[1])

    rank = device_rank.reshape(1).astype(jnp.int32)
    return line_of_four(
        rank, replica.reshape(1).astype(jnp.int32), prompt_owner, fork_map, page_table,
        prompt_length, span_states, decode_states, decode_queries, key_weight, value_weight,
        out_weight, pool,
    )


def line_of_four(
    rank, replica, prompt_owner, fork_map, page_table, prompt_length, span_states, decode_states,
    decode_queries, key_weight, value_weight, out_weight, pool,
):
    n_replica = lax.axis_size("replica")
    span = span_states.shape[0]
    rows, steps, _ = decode_states.shape
    first = min(SET_ROWS, rows)
    blocks = rows // first
    middle = blocks - 2
    cut = first * steps

    first_units = project(
        rank, ((span_states, 0, span), (decode_states, 0, first)), key_weight, value_weight,
        (0, 2), (1, 3),
    )
    rest_units = project(
        rank, ((decode_states, first, rows - first),), key_weight, value_weight, (0, 2), (1, 3)
    )
    fork_row = fork_map[None, :]
    half = rope_base ** (-(2.0 / HD) * jnp.arange(HD // 2, dtype=jnp.float32))
    freq = jnp.concatenate([half, half])[None, :]
    places = (span, steps, prompt_owner, prompt_length, replica, fork_row, freq)
    own_span, first_tail = swap_sum(*first_units, places, 0, (span, cut))
    arrived = [own_span]
    for j in range(1, n_replica):
        arrived.append(swap(own_span, "replica", j))
    middle_tail, last_tail = swap_sum(*rest_units, places, span + cut, (middle * cut, cut))

    def attended(tail, start, count):
        old = attend_cached(decode_queries, fork_row, page_table, prompt_length, pool, start, count)
        return attend_new(
            decode_queries, fork_row, prompt_owner, replica, arrived, tail, *old, start, count
        )

    shape = (rows, steps, out_weight.shape[1])
    first_own = attended(first_tail, 0, 1)
    middle_own = attended(middle_tail, 1, middle)
    last_own = attended(last_tail, blocks - 1, 1)
    far, near, across, passed = gather_heads(first_own)
    decoded = out_project(
        rank, [first_own, far, near, across], (0, 2, 1, 3), out_weight, shape, 0, pick=passed
    )
    far, near, across, passed = gather_heads(middle_own)
    partial = out_project(
        rank, [middle_own, far, near], (0, 2, 1), out_weight, shape, 0, final=False
    )
    last_rows = hold(rank, 3, out_weight, middle_own.shape[1])
    decoded = out_project(
        rank, [across], (3,), last_rows, shape, first,
        pick=passed, partial=partial, into=decoded, held=True,
    )
    far, near, across, passed = gather_heads(last_own)
    partial = out_project(rank, [last_own, far], (0, 2), out_weight, shape, 0, final=False)
    partial = out_project(rank, [near], (1,), out_weight, shape, 0, partial=partial, final=False)
    return out_project(
        rank, [across], (3,), last_rows, shape, first * (blocks - 1),
        pick=passed, partial=partial, into=decoded, held=True,
    )


def solution(mesh):
    in_specs = (
        P("parts"),
        P(("parts", "replica")),
        P("parts"),
        P("parts"),
        P(("parts", "replica"), "tensor"),
        P(("parts", "replica"), None, "tensor"),
        P(("parts", "replica"), None, "tensor"),
        P("tensor", None),
        P("tensor", None),
        P(None, "tensor"),
        P("tensor", "parts", None, None),
    )
    out_specs = P(("parts", "replica"), None, "tensor")
    return jax.shard_map(
        on_device, mesh=mesh, in_specs=in_specs, out_specs=out_specs, check_vma=False
    )
```

```python
import functools
import math

import jax
import jax.numpy as jnp
from jax import lax
from jax.experimental import pallas as pl
from jax.experimental.pallas import tpu as pltpu
from jax.sharding import PartitionSpec as P


HD = 128
rope_base = 1000000.0
LOG2E = math.log2(math.e)
HIDDEN = -1e30


def rotary(vectors, places):
    half = vectors.shape[-1] // 2
    freq = rope_base ** (-(2.0 / vectors.shape[-1]) * jnp.arange(half, dtype=jnp.float32))
    angle = places.astype(jnp.float32)[..., None, None] * freq
    cosine = jnp.cos(angle)
    sine = jnp.sin(angle)
    first = vectors[..., :half]
    second = vectors[..., half:]
    return jnp.concatenate([first * cosine - second * sine, second * cosine + first * sine], -1)


def rotate_round(summed, places, kv_heads):
    number = summed.shape[0]
    turned = rotary(summed[:, : kv_heads * HD].reshape(number, kv_heads, HD), places)
    turned = turned.astype(jnp.bfloat16).reshape(number, kv_heads * HD)
    return jnp.concatenate([turned, summed[:, kv_heads * HD :].astype(jnp.bfloat16)], 1)


def own_pair(packed, head_group, kv_heads):
    key_part = lax.dynamic_slice_in_dim(packed, head_group * HD, HD, 1)
    value_part = lax.dynamic_slice_in_dim(packed, (kv_heads + head_group) * HD, HD, 1)
    return jnp.concatenate([key_part, value_part], 1)


NT = (((1,), (1,)), ((), ()))
SMALL = pltpu.CompilerParams(vmem_limit_bytes=24 << 20)
LARGE = pltpu.CompilerParams(vmem_limit_bytes=36 << 20)
SET_ROWS = 32


def in_hbm(x):
    return pltpu.with_memory_space_constraint(x, pltpu.HBM)


def lane_tiles(combine, x):
    out = x[..., :HD]
    for i in range(1, x.shape[-1] // HD):
        out = combine(out, x[..., i * HD : (i + 1) * HD])
    return out


def stacked_heads(q_ref, heads):
    m = q_ref.shape[0] * q_ref.shape[1]
    q = q_ref[...].reshape(m, heads * HD)
    return jnp.concatenate([q[:, h * HD : (h + 1) * HD] for h in range(heads)], 0)


def softmax_parts(qs, heads, parts, scale2, s_ref):
    m = qs.shape[0] // heads
    top = None
    at = 0
    for n, load, bias in parts:
        s = lax.dot_general(qs, load()[:, :HD], NT, preferred_element_type=jnp.float32)
        s = s.reshape(heads, m, n) * scale2 + bias()[None]
        s_ref[:, :, at : at + n] = s
        most = lane_tiles(jnp.maximum, s)
        top = most if top is None else jnp.maximum(top, most)
        at += n
    top = jnp.max(top, -1, keepdims=True)
    total = mixed = None
    at = 0
    for n, load, _ in parts:
        w = jnp.exp2(s_ref[:, :, at : at + n] - top)
        summed = lane_tiles(jnp.add, w)
        one = jnp.dot(
            w.astype(jnp.bfloat16).reshape(heads * m, n),
            load()[:, HD:],
            preferred_element_type=jnp.float32,
        ).reshape(heads, m, HD)
        total = summed if total is None else total + summed
        mixed = one if mixed is None else mixed + one
        at += n
    return top, jnp.sum(total, -1, keepdims=True), mixed


def by_row(values, first, rows, steps):
    lane = lax.broadcasted_iota(jnp.int32, (rows, values.shape[1]), 1)
    row = lax.broadcasted_iota(jnp.int32, (rows, values.shape[1]), 0)
    mine = jnp.where(lane == first + row // steps, values.astype(jnp.float32), 0.0)
    return jnp.sum(mine, 1, keepdims=True)


def shown(allowed):
    return jnp.where(allowed, 0.0, HIDDEN)


def cached_kernel(
    heads, cpages, scale2, start, table_ref, length_ref, q_ref, fork_ref, pool_ref, mixed_ref, stat_ref, s_ref
):
    qs = stacked_heads(q_ref, heads)
    m = qs.shape[0] // heads
    block, steps = q_ref.shape[:2]
    prompt = by_row(fork_ref[...], (pl.program_id(0) + start) * block, m, steps)
    pages, size = pool_ref.shape[:2]
    group = cpages

    def part(at):
        mine = range(at, min(at + group, pages))

        def load():
            return jnp.concatenate([pool_ref[table_ref[i]] for i in mine], 0)

        def bias():
            lane = lax.broadcasted_iota(jnp.int32, (m, size), 1)
            return jnp.concatenate(
                [
                    shown(
                        (prompt == float(i // cpages))
                        & (lane < length_ref[i // cpages] - (i % cpages) * size)
                    )
                    for i in mine
                ],
                1,
            )

        return len(mine) * size, load, bias

    parts = [part(at) for at in range(0, pages, group)]
    top, total, mixed = softmax_parts(qs, heads, parts, scale2, s_ref)
    mixed_ref[...] = mixed
    lane = lax.broadcasted_iota(jnp.int32, mixed.shape, 2)
    stat_ref[...] = jnp.where(lane < HD // 2, top, total)


def new_kernel(
    heads, steps, scale2, start, owner_ref, base_ref, q_ref, fork_ref, tail_ref, mixed_ref, stat_ref, *refs
):
    span_refs, o_ref, s_ref = refs[:-2], refs[-2], refs[-1]
    qs = stacked_heads(q_ref, heads)
    m = qs.shape[0] // heads
    span = span_refs[0].shape[0]
    prompt = by_row(fork_ref[...], (pl.program_id(0) + start) * q_ref.shape[0], m, steps)

    def loaded():
        return jnp.concatenate([ref[...] for ref in span_refs], 0)

    def owned():
        return jnp.concatenate(
            [
                jnp.broadcast_to(
                    shown(prompt == owner_ref[base_ref[0] ^ j].astype(jnp.float32)), (m, span)
                )
                for j in range(len(span_refs))
            ],
            1,
        )

    def causal():
        row = lax.broadcasted_iota(jnp.int32, (m, m), 0)
        col = lax.broadcasted_iota(jnp.int32, (m, m), 1)
        return shown((row // steps == col // steps) & (col <= row))

    parts = (
        (span * len(span_refs), loaded, owned),
        (m, lambda: tail_ref[...], causal),
    )
    top, total, mixed = softmax_parts(qs, heads, parts, scale2, s_ref)
    old_top = stat_ref[:, :, :1]
    old_total = stat_ref[:, :, HD // 2 : HD // 2 + 1]
    both = jnp.maximum(top, old_top)
    new_share = jnp.exp2(top - both)
    old_share = jnp.exp2(old_top - both)
    total = total * new_share + old_total * old_share
    mixed = mixed * new_share + mixed_ref[...] * old_share
    out = (mixed / total).astype(jnp.bfloat16)
    for h in range(heads):
        o_ref[:, h * HD : (h + 1) * HD] = out[h]


def attend_cached(q, fork_row, page_table, prompt_length, pool, start, count):
    steps, width = q.shape[1:]
    heads = width // HD
    block = min(SET_ROWS, q.shape[0])
    m = block * steps
    cached = pool.shape[0] * pool.shape[1]
    cpages = pool.shape[0] // prompt_length.shape[0]
    return pl.pallas_call(
        functools.partial(cached_kernel, heads, cpages, LOG2E / math.sqrt(HD), start),
        grid_spec=pltpu.PrefetchScalarGridSpec(
            num_scalar_prefetch=2,
            grid=(count,),
            in_specs=[
                pl.BlockSpec((block, steps, width), lambda i, *_: (i + start, 0, 0)),
                pl.BlockSpec(fork_row.shape, lambda i, *_: (0, 0)),
                pl.BlockSpec(pool.shape, lambda i, *_: (0, 0, 0)),
            ],
            out_specs=[pl.BlockSpec((heads, m, HD), lambda i, *_: (0, i, 0))] * 2,
            scratch_shapes=[pltpu.VMEM((heads, m, cached), jnp.float32)],
        ),
        out_shape=[jax.ShapeDtypeStruct((heads, m * count, HD), jnp.float32)] * 2,
        cost_estimate=pl.CostEstimate(
            flops=4 * count * heads * m * cached * HD,
            transcendentals=count * heads * m * cached,
            bytes_accessed=8 * count * heads * m * HD,
        ),
        compiler_params=SMALL,
        name="attend_cached",
    )(page_table, prompt_length, q, fork_row, pool)


def attend_new(q, fork_row, owner, base, span_pairs, tail_pairs, mixed, stat, start, count, skip=0):
    steps, width = q.shape[1:]
    heads = width // HD
    block = min(SET_ROWS, q.shape[0])
    m = block * steps
    span = span_pairs[0].shape[0]
    keys = span * len(span_pairs)
    part = pl.BlockSpec((heads, m, HD), lambda i, *_: (0, i + skip, 0))
    return pl.pallas_call(
        functools.partial(new_kernel, heads, steps, LOG2E / math.sqrt(HD), start),
        grid_spec=pltpu.PrefetchScalarGridSpec(
            num_scalar_prefetch=2,
            grid=(count,),
            in_specs=[
                pl.BlockSpec((block, steps, width), lambda i, *_: (i + start, 0, 0)),
                pl.BlockSpec(fork_row.shape, lambda i, *_: (0, 0)),
                pl.BlockSpec((m, 2 * HD), lambda i, *_: (i, 0)),
                part,
                part,
            ]
            + [pl.BlockSpec((span, 2 * HD), lambda i, *_: (0, 0))] * len(span_pairs),
            out_specs=pl.BlockSpec((m, width), lambda i, *_: (i, 0)),
            scratch_shapes=[pltpu.VMEM((heads, m, keys + m), jnp.float32)],
        ),
        out_shape=jax.ShapeDtypeStruct((m * count, width), jnp.bfloat16),
        cost_estimate=pl.CostEstimate(
            flops=4 * count * heads * m * (keys + m) * HD,
            transcendentals=count * heads * m * (keys + m),
            bytes_accessed=10 * count * heads * m * HD,
        ),
        compiler_params=SMALL,
        name="attend_new",
    )(owner, base, q, fork_row, tail_pairs, mixed, stat, *span_pairs)


def project_kernel(groups, split, kept, sent, rank_ref, *refs):
    keep_ref, send_ref, acc = refs[-3:]
    s = pl.program_id(0)
    rows = [ref[...].reshape(-1, ref.shape[-1]) for ref in refs[:groups]]
    x = rows[0] if groups == 1 else jnp.concatenate(rows, 0)
    refs = refs[groups:]
    w = jnp.concatenate(
        [jnp.concatenate([refs[2 * i][...], refs[2 * i + 1][...]], 1) for i in range(split)], 0
    )
    one = jnp.dot(x, w, preferred_element_type=jnp.float32)

    @pl.when(s == 0)
    def _():
        acc[...] = one

    @pl.when(s > 0)
    def _():
        acc[...] += one

    @pl.when(s == pl.num_programs(0) - 1)
    def _():
        keys = acc.shape[1] // 2
        for ref, rels in ((send_ref, sent), (keep_ref, kept)):
            for i, rel in enumerate(rels):
                at = pl.multiple_of((rank_ref[0] ^ rel) * HD, HD)
                ref[i, :, :HD] = acc[:, pl.ds(at, HD)].astype(ref.dtype)
                ref[i, :, HD:] = acc[:, pl.ds(pl.multiple_of(at + keys, HD), HD)].astype(ref.dtype)


def project(rank, groups, key_weight, value_weight, kept, sent):
    width, columns = key_weight.shape
    depth, split = width // 2, 2
    in_specs = []
    n = 0
    for x, start, rows in groups:
        lead = (rows,) + x.shape[1:-1]
        n += math.prod(lead)
        in_specs.append(
            pl.BlockSpec(
                tuple(pl.Element(d) for d in lead + (depth,)),
                lambda s, r, start=start, lead=lead: (start,) + (0,) * (len(lead) - 1) + (s * depth,),
            )
        )
    for i in range(split):
        piece = pl.BlockSpec((depth // split, columns), lambda s, r, i=i: (s * split + i, 0))
        in_specs += [piece, piece]
    return pl.pallas_call(
        functools.partial(project_kernel, len(groups), split, kept, sent),
        grid_spec=pltpu.PrefetchScalarGridSpec(
            num_scalar_prefetch=1,
            grid=(width // depth,),
            in_specs=in_specs,
            out_specs=[
                pl.BlockSpec((len(rels), n, 2 * HD), lambda s, r: (0, 0, 0)) for rels in (kept, sent)
            ],
            scratch_shapes=[pltpu.VMEM((n, 2 * columns), jnp.float32)],
        ),
        out_shape=[
            jax.ShapeDtypeStruct((len(kept), n, 2 * HD), jnp.float32),
            jax.ShapeDtypeStruct((len(sent), n, 2 * HD), jnp.bfloat16),
        ],
        cost_estimate=pl.CostEstimate(
            flops=4 * n * width * columns, transcendentals=0, bytes_accessed=4 * width * columns
        ),
        compiler_params=SMALL,
        name="project",
    )(
        rank,
        *[in_hbm(x) for x, _, _ in groups],
        *([in_hbm(key_weight), in_hbm(value_weight)] * split),
    )


def finish_kernel(
    span, steps, start, sizes, owner_ref, length_ref, replica_ref, fork_ref, freq_ref, keep_ref, *refs
):
    outs = refs[-len(sizes) :]
    summed = keep_ref[0]
    for ref in refs[: -len(sizes)]:
        summed = summed + (ref[0] if len(ref.shape) == 3 else ref[...]).astype(jnp.float32)
    n = summed.shape[0]
    fork = fork_ref[...]
    lengths = jnp.zeros_like(fork)
    for p in range(length_ref.shape[0]):
        lengths = jnp.where(fork == p, length_ref[p], lengths)
    lead = max(0, span - start)
    places = []
    if lead:
        own = length_ref[owner_ref[replica_ref[0]]]
        places.append(own + start + lax.broadcasted_iota(jnp.int32, (lead, 1), 0).astype(jnp.int32))
        places[0] = places[0].astype(jnp.float32)
    tail = n - lead
    first = start + lead - span
    step = lax.broadcasted_iota(jnp.int32, (tail, 1), 0) % steps
    places.append(
        by_row(lengths, first // steps, tail, steps) + (span + step).astype(jnp.float32)
    )
    places = places[0] if len(places) == 1 else jnp.concatenate(places, 0)
    angle = places * freq_ref[...]
    lane = lax.broadcasted_iota(jnp.int32, (n, HD), 1)
    sine = jnp.where(lane < HD // 2, -jnp.sin(angle), jnp.sin(angle))
    keys = summed[:, :HD]
    turned = keys * jnp.cos(angle) + pltpu.roll(keys, HD // 2, 1) * sine
    at = 0
    for size, o_ref in zip(sizes, outs):
        o_ref[:, :HD] = turned[at : at + size].astype(jnp.bfloat16)
        o_ref[:, HD:] = summed[at : at + size, HD:].astype(jnp.bfloat16)
        at += size


def finish(keep, others, places, start, sizes):
    span, steps, owner, length, replica, fork_row, freq = places
    n = keep.shape[1]
    unit = pl.BlockSpec((1, n, 2 * HD), lambda i, *_: (0, 0, 0))
    flat = lambda rows, width: pl.BlockSpec((rows, width), lambda i, *_: (0, 0))
    return pl.pallas_call(
        functools.partial(finish_kernel, span, steps, start, sizes),
        grid_spec=pltpu.PrefetchScalarGridSpec(
            num_scalar_prefetch=3,
            grid=(1,),
            in_specs=[flat(*fork_row.shape), flat(*freq.shape), unit]
            + [unit if x.ndim == 3 else flat(n, 2 * HD) for x in others],
            out_specs=[flat(size, 2 * HD) for size in sizes],
        ),
        out_shape=[jax.ShapeDtypeStruct((size, 2 * HD), jnp.bfloat16) for size in sizes],
        compiler_params=SMALL,
        name="finish",
    )(owner, length, replica, fork_row, freq, keep, *others)


def swap(x, axis, bit):
    return lax.ppermute(x, axis, [(i, i ^ bit) for i in range(lax.axis_size(axis))])


def swap_sum(keep, send, places, start, sizes):
    got = swap(send, "tensor", 1)
    half = (keep[1] + got[1].astype(jnp.float32)).astype(jnp.bfloat16)
    last = swap(half, "tensor", 2)
    return finish(keep, (got, last), places, start, sizes)


def out_kernel(rels, shapes, cuts, add, held, rank_ref, *refs):
    refs = list(refs)
    pieces = [([refs.pop(0) for _ in range(n)], refs.pop(0) if outer else None) for n, outer in shapes]
    partial = refs.pop(0) if add else None
    w_ref = refs[0]
    o_ref, buf, sem = (refs[-1], None, None) if held else refs[-3:]
    width = pieces[0][0][0].shape[1]
    depth = width // cuts
    rank = rank_ref[0]
    inner = (rank == 1) | (rank == 2)
    copies = []
    for p, rel in enumerate(() if held else rels):
        for c in range(cuts):
            row = pl.multiple_of((rank ^ rel) * width + c * depth, depth)
            slot = p * cuts + c
            copies.append(
                pltpu.make_async_copy(w_ref.at[pl.ds(row, depth), :], buf.at[slot], sem.at[slot])
            )
            copies[-1].start()
    total = partial[...] if add else None
    for p, (groups, outer) in enumerate(pieces):
        a = [ref[...] for ref in groups]
        a = a[0] if len(a) == 1 else jnp.concatenate(a, 0)
        if outer is not None:
            a = jnp.where(inner, a, outer[...])
        for c in range(cuts):
            if held:
                at = held.index(rels[p]) * width + c * depth
                w = w_ref[at : at + depth, :]
            else:
                copies[p * cuts + c].wait()
                w = buf[p * cuts + c]
            one = jnp.dot(
                a[:, c * depth : (c + 1) * depth], w, preferred_element_type=jnp.float32
            )
            total = one if total is None else total + one
    o_ref[...] = total.reshape(o_ref.shape).astype(o_ref.dtype)


def out_project(rank, pieces, weight, shape, start, partial=None, into=None, final=True, held=()):
    width = pieces[0][1][0].shape[1]
    m = sum(x.shape[0] for x in pieces[0][1])
    columns = weight.shape[1]
    steps = shape[1]
    cuts = 1 if held else 4
    flat = lambda x: pl.BlockSpec(x.shape, lambda i, r: (0, 0))
    args = []
    for _, groups, outer in pieces:
        args += list(groups) + ([] if outer is None else [outer])
    if partial is not None:
        args.append(partial)
    in_specs = [flat(x) for x in args]
    args.append(weight if held else in_hbm(weight))
    in_specs.append(pl.BlockSpec(memory_space=pltpu.VMEM if held else pl.ANY))
    aliases = {}
    if into is not None:
        args.append(into)
        in_specs.append(pl.BlockSpec(memory_space=pl.ANY))
        aliases = {len(args): 0}
    if final:
        out_spec = pl.BlockSpec(
            (pl.Element(m // steps), pl.Element(steps), pl.Element(columns)),
            lambda i, r: (start, 0, 0),
        )
        out_shape = jax.ShapeDtypeStruct(shape, jnp.bfloat16)
    else:
        out_spec = pl.BlockSpec((m, columns), lambda i, r: (0, 0))
        out_shape = jax.ShapeDtypeStruct((m, columns), jnp.float32)
    rels = tuple(rel for rel, _, _ in pieces)
    shapes = tuple((len(groups), outer is not None) for _, groups, outer in pieces)
    slots = len(rels) * cuts
    return pl.pallas_call(
        functools.partial(out_kernel, rels, shapes, cuts, partial is not None, held),
        grid_spec=pltpu.PrefetchScalarGridSpec(
            num_scalar_prefetch=1,
            grid=(1,),
            in_specs=in_specs,
            out_specs=out_spec,
            scratch_shapes=[]
            if held
            else [
                pltpu.VMEM((slots, width // cuts, columns), jnp.bfloat16),
                pltpu.SemaphoreType.DMA((slots,)),
            ],
        ),
        out_shape=out_shape,
        input_output_aliases=aliases,
        cost_estimate=pl.CostEstimate(
            flops=2 * m * width * columns * len(rels),
            transcendentals=0,
            bytes_accessed=2 * width * columns * len(rels),
        ),
        compiler_params=LARGE,
        name="out_project",
    )(rank, *args)


def hold_kernel(rels, rank_ref, w_ref, o_ref, sem):
    rows = o_ref.shape[0] // len(rels)
    copies = []
    for i, rel in enumerate(rels):
        at = pl.multiple_of((rank_ref[0] ^ rel) * rows, rows)
        copies.append(
            pltpu.make_async_copy(
                w_ref.at[pl.ds(at, rows), :], o_ref.at[i * rows : (i + 1) * rows, :], sem.at[i]
            )
        )
        copies[-1].start()
    for copy in copies:
        copy.wait()


def hold(rank, rels, weight, rows):
    held = pl.pallas_call(
        functools.partial(hold_kernel, rels),
        grid_spec=pltpu.PrefetchScalarGridSpec(
            num_scalar_prefetch=1,
            grid=(1,),
            in_specs=[pl.BlockSpec(memory_space=pl.ANY)],
            out_specs=pl.BlockSpec(memory_space=pltpu.VMEM),
            scratch_shapes=[pltpu.SemaphoreType.DMA((len(rels),))],
        ),
        out_shape=jax.ShapeDtypeStruct((len(rels) * rows, weight.shape[1]), weight.dtype),
        compiler_params=SMALL,
        name="hold",
    )(rank, in_hbm(weight))
    return pltpu.with_memory_space_constraint(held, pltpu.VMEM)


def gather_heads(own):
    far = swap(own, "tensor", 2)
    near = swap(own, "tensor", 1)
    across = lax.ppermute(own, "tensor", [(1, 2), (2, 1)])
    passed = lax.ppermute(far, "tensor", [(1, 0), (2, 3)])
    return far, near, across, passed


def relay_heads(groups):
    near = []
    for group in groups:
        near.append(swap(group, "tensor", 1))
    own = jnp.concatenate(groups, 0)
    across = lax.ppermute(own, "tensor", [(1, 2), (2, 1)])
    far = lax.ppermute(own, "tensor", [(0, 2), (3, 1)])
    outward = [(1, 0), (2, 3)]
    forward = lax.ppermute(across, "tensor", outward)
    passed = lax.ppermute(far, "tensor", outward)
    return near, far, across, forward, passed


def on_device(
    prompt_owner,
    fork_map,
    page_table,
    prompt_length,
    span_states,
    decode_states,
    decode_queries,
    key_weight,
    value_weight,
    out_weight,
    page_pool,
):
    replica = lax.axis_index("replica")
    device_rank = lax.axis_index("tensor")
    n_replica = lax.axis_size("replica")
    n_tensor = lax.axis_size("tensor")
    span = span_states.shape[0]
    rows, steps, width = decode_states.shape
    kv_heads = key_weight.shape[1] // HD
    sharing = n_tensor // kv_heads
    prompts = jnp.arange(n_replica, dtype=jnp.int32)
    own_prompt = jnp.sum(jnp.where(prompts == replica, prompt_owner, 0))
    own_length = jnp.sum(jnp.where(prompts == own_prompt, prompt_length, 0))
    row_hits = fork_map[:, None] == prompts[None, :]
    row_length = jnp.sum(jnp.where(row_hits, prompt_length[None, :], 0), 1)
    span_places = own_length + jnp.arange(span, dtype=jnp.int32)
    tail_places = (
        row_length[:, None] + span + jnp.arange(steps, dtype=jnp.int32)[None, :]
    ).reshape(-1)
    pool = page_pool.reshape(page_pool.shape[1:])
    short_line = n_tensor == kv_heads == 4 and n_replica == 4
    first = min(SET_ROWS, rows)
    blocks = rows // first

    if not short_line:
        positions = jnp.concatenate([span_places, tail_places])
        tokens = jnp.concatenate([span_states, decode_states.reshape(rows * steps, width)], 0)
        projected = jnp.dot(
            tokens,
            jnp.concatenate([key_weight, value_weight], 1),
            preferred_element_type=jnp.float32,
        )
        share = lax.psum_scatter(projected, "tensor", scatter_dimension=0, tiled=True)
        number = share.shape[0]
        places = lax.dynamic_slice_in_dim(positions, device_rank * number, number)
        turned = rotate_round(share, places, kv_heads)
        groups = jnp.stack([own_pair(turned, g, kv_heads) for g in range(kv_heads)], 0)
        outgoing = jnp.repeat(groups, sharing, axis=0)
        paired = lax.all_to_all(
            outgoing, "tensor", split_axis=0, concat_axis=1, tiled=True
        ).reshape(-1, 2 * HD)
        arrived = lax.all_gather(paired[:span], "replica", axis=0, tiled=True)
        mixed, stat = attend_cached(
            decode_queries, fork_map[None, :], page_table, prompt_length, pool, 0, blocks
        )
        own = attend_new(
            decode_queries,
            fork_map[None, :],
            prompt_owner,
            jnp.zeros((1,), jnp.int32),
            jnp.split(arrived, n_replica),
            paired[span:],
            mixed,
            stat,
            0,
            blocks,
        )
        decoded = jnp.dot(
            lax.all_gather(own, "tensor", axis=1, tiled=True),
            out_weight,
            preferred_element_type=jnp.float32,
        )
        return decoded.astype(jnp.bfloat16).reshape(rows, steps, out_weight.shape[1])

    rank = device_rank.reshape(1).astype(jnp.int32)
    return line_of_four(
        rank, replica.reshape(1).astype(jnp.int32), prompt_owner, fork_map, page_table,
        prompt_length, span_states, decode_states, decode_queries, key_weight, value_weight,
        out_weight, pool,
    )


def line_of_four(
    rank, replica, prompt_owner, fork_map, page_table, prompt_length, span_states, decode_states,
    decode_queries, key_weight, value_weight, out_weight, pool,
):
    n_replica = lax.axis_size("replica")
    span = span_states.shape[0]
    rows, steps, _ = decode_states.shape
    first = min(SET_ROWS, rows)
    blocks = rows // first
    middle = blocks - 2
    cut = first * steps

    first_units = project(
        rank, ((span_states, 0, span), (decode_states, 0, first)), key_weight, value_weight,
        (0, 2), (1, 3),
    )
    rest_units = project(
        rank, ((decode_states, first, rows - first),), key_weight, value_weight, (0, 2), (1, 3)
    )
    fork_row = fork_map[None, :]
    half = rope_base ** (-(2.0 / HD) * jnp.arange(HD // 2, dtype=jnp.float32))
    freq = jnp.concatenate([half, half])[None, :]
    places = (span, steps, prompt_owner, prompt_length, replica, fork_row, freq)
    own_span, first_tail = swap_sum(*first_units, places, 0, (span, cut))
    arrived = [own_span]
    for j in range(1, n_replica):
        arrived.append(swap(own_span, "replica", j))
    rest_tails = swap_sum(*rest_units, places, span + cut, (cut,) * (blocks - 1))

    def old_part(start, count):
        return attend_cached(
            decode_queries, fork_row, page_table, prompt_length, pool, start, count
        )

    def new_part(tail, old, start, skip=0):
        return attend_new(
            decode_queries, fork_row, prompt_owner, replica, arrived, tail, *old, start, 1, skip
        )

    shape = (rows, steps, out_weight.shape[1])
    first_own = new_part(first_tail, old_part(0, 1), 0)
    middle_old = old_part(1, middle)
    middle_own = [new_part(rest_tails[i], middle_old, 1 + i, i) for i in range(middle)]
    last_own = new_part(rest_tails[-1], old_part(blocks - 1, 1), blocks - 1)
    far, near, across, passed = gather_heads(first_own)
    pieces = ((0, [first_own], None), (2, [far], None), (1, [near], None), (3, [across], passed))
    decoded = out_project(rank, pieces, out_weight, shape, 0)
    near, far, across, forward, passed = relay_heads(middle_own)
    held = (2, 3)
    held_rows = hold(rank, held, out_weight, first_own.shape[1])
    pieces = ((0, middle_own, None), (1, near, None))
    partial = out_project(rank, pieces, out_weight, shape, 0, final=False)
    pieces = ((2, [far], forward), (3, [across], passed))
    decoded = out_project(
        rank, pieces, held_rows, shape, first, partial=partial, into=decoded, held=held
    )
    far, near, across, passed = gather_heads(last_own)
    pieces = ((0, [last_own], None), (2, [far], None))
    partial = out_project(rank, pieces, out_weight, shape, 0, final=False)
    partial = out_project(
        rank, ((1, [near], None),), out_weight, shape, 0, partial=partial, final=False
    )
    return out_project(
        rank, ((3, [across], passed),), held_rows, shape, first * (blocks - 1),
        partial=partial, into=decoded, held=held,
    )


def solution(mesh):
    in_specs = (
        P("parts"),
        P(("parts", "replica")),
        P("parts"),
        P("parts"),
        P(("parts", "replica"), "tensor"),
        P(("parts", "replica"), None, "tensor"),
        P(("parts", "replica"), None, "tensor"),
        P("tensor", None),
        P("tensor", None),
        P(None, "tensor"),
        P("tensor", "parts", None, None),
    )
    out_specs = P(("parts", "replica"), None, "tensor")
    return jax.shard_map(
        on_device, mesh=mesh, in_specs=in_specs, out_specs=out_specs, check_vma=False
    )
```

```python
import functools
import math

import jax
import jax.numpy as jnp
from jax import lax
from jax.experimental import pallas as pl
from jax.experimental.pallas import tpu as pltpu
from jax.sharding import PartitionSpec as P


HD = 128
rope_base = 1000000.0
LOG2E = math.log2(math.e)
HIDDEN = -1e30


def rotary(vectors, places):
    half = vectors.shape[-1] // 2
    freq = rope_base ** (-(2.0 / vectors.shape[-1]) * jnp.arange(half, dtype=jnp.float32))
    angle = places.astype(jnp.float32)[..., None, None] * freq
    cosine = jnp.cos(angle)
    sine = jnp.sin(angle)
    first = vectors[..., :half]
    second = vectors[..., half:]
    return jnp.concatenate([first * cosine - second * sine, second * cosine + first * sine], -1)


def rotate_round(summed, places, kv_heads):
    number = summed.shape[0]
    turned = rotary(summed[:, : kv_heads * HD].reshape(number, kv_heads, HD), places)
    turned = turned.astype(jnp.bfloat16).reshape(number, kv_heads * HD)
    return jnp.concatenate([turned, summed[:, kv_heads * HD :].astype(jnp.bfloat16)], 1)


def own_pair(packed, head_group, kv_heads):
    key_part = lax.dynamic_slice_in_dim(packed, head_group * HD, HD, 1)
    value_part = lax.dynamic_slice_in_dim(packed, (kv_heads + head_group) * HD, HD, 1)
    return jnp.concatenate([key_part, value_part], 1)


NT = (((1,), (1,)), ((), ()))
SMALL = pltpu.CompilerParams(vmem_limit_bytes=24 << 20)
LARGE = pltpu.CompilerParams(vmem_limit_bytes=36 << 20)
SET_ROWS = 32


def in_hbm(x):
    return pltpu.with_memory_space_constraint(x, pltpu.HBM)


def lane_tiles(combine, x):
    out = x[..., :HD]
    for i in range(1, x.shape[-1] // HD):
        out = combine(out, x[..., i * HD : (i + 1) * HD])
    return out


def stacked_heads(q_ref, heads):
    m = q_ref.shape[0] * q_ref.shape[1]
    q = q_ref[...].reshape(m, heads * HD)
    return jnp.concatenate([q[:, h * HD : (h + 1) * HD] for h in range(heads)], 0)


def softmax_parts(qs, heads, parts, scale2, s_ref):
    m = qs.shape[0] // heads
    top = None
    at = 0
    for n, load, bias in parts:
        s = lax.dot_general(qs, load()[:, :HD], NT, preferred_element_type=jnp.float32)
        s = s.reshape(heads, m, n) * scale2 + bias()[None]
        s_ref[:, :, at : at + n] = s
        most = lane_tiles(jnp.maximum, s)
        top = most if top is None else jnp.maximum(top, most)
        at += n
    top = jnp.max(top, -1, keepdims=True)
    total = mixed = None
    at = 0
    for n, load, _ in parts:
        w = jnp.exp2(s_ref[:, :, at : at + n] - top)
        summed = lane_tiles(jnp.add, w)
        one = jnp.dot(
            w.astype(jnp.bfloat16).reshape(heads * m, n),
            load()[:, HD:],
            preferred_element_type=jnp.float32,
        ).reshape(heads, m, HD)
        total = summed if total is None else total + summed
        mixed = one if mixed is None else mixed + one
        at += n
    return top, jnp.sum(total, -1, keepdims=True), mixed


def by_row(values, first, rows, steps):
    lane = lax.broadcasted_iota(jnp.int32, (rows, values.shape[1]), 1)
    row = lax.broadcasted_iota(jnp.int32, (rows, values.shape[1]), 0)
    mine = jnp.where(lane == first + row // steps, values.astype(jnp.float32), 0.0)
    return jnp.sum(mine, 1, keepdims=True)


def shown(allowed):
    return jnp.where(allowed, 0.0, HIDDEN)


def cached_kernel(
    heads, cpages, scale2, start, table_ref, length_ref, q_ref, fork_ref, pool_ref, mixed_ref, stat_ref, s_ref
):
    qs = stacked_heads(q_ref, heads)
    m = qs.shape[0] // heads
    block, steps = q_ref.shape[:2]
    prompt = by_row(fork_ref[...], (pl.program_id(0) + start) * block, m, steps)
    pages, size = pool_ref.shape[:2]
    group = cpages

    def part(at):
        mine = range(at, min(at + group, pages))

        def load():
            return jnp.concatenate([pool_ref[table_ref[i]] for i in mine], 0)

        def bias():
            lane = lax.broadcasted_iota(jnp.int32, (m, size), 1)
            return jnp.concatenate(
                [
                    shown(
                        (prompt == float(i // cpages))
                        & (lane < length_ref[i // cpages] - (i % cpages) * size)
                    )
                    for i in mine
                ],
                1,
            )

        return len(mine) * size, load, bias

    parts = [part(at) for at in range(0, pages, group)]
    top, total, mixed = softmax_parts(qs, heads, parts, scale2, s_ref)
    mixed_ref[...] = mixed
    lane = lax.broadcasted_iota(jnp.int32, mixed.shape, 2)
    stat_ref[...] = jnp.where(lane < HD // 2, top, total)


def new_kernel(
    heads, steps, scale2, start, owner_ref, base_ref, q_ref, fork_ref, tail_ref, mixed_ref, stat_ref, *refs
):
    span_refs, o_ref, s_ref = refs[:-2], refs[-2], refs[-1]
    qs = stacked_heads(q_ref, heads)
    m = qs.shape[0] // heads
    span = span_refs[0].shape[0]
    prompt = by_row(fork_ref[...], (pl.program_id(0) + start) * q_ref.shape[0], m, steps)

    def loaded():
        return jnp.concatenate([ref[...] for ref in span_refs], 0)

    def owned():
        return jnp.concatenate(
            [
                jnp.broadcast_to(
                    shown(prompt == owner_ref[base_ref[0] ^ j].astype(jnp.float32)), (m, span)
                )
                for j in range(len(span_refs))
            ],
            1,
        )

    def causal():
        row = lax.broadcasted_iota(jnp.int32, (m, m), 0)
        col = lax.broadcasted_iota(jnp.int32, (m, m), 1)
        return shown((row // steps == col // steps) & (col <= row))

    parts = (
        (span * len(span_refs), loaded, owned),
        (m, lambda: tail_ref[...], causal),
    )
    top, total, mixed = softmax_parts(qs, heads, parts, scale2, s_ref)
    old_top = stat_ref[:, :, :1]
    old_total = stat_ref[:, :, HD // 2 : HD // 2 + 1]
    both = jnp.maximum(top, old_top)
    new_share = jnp.exp2(top - both)
    old_share = jnp.exp2(old_top - both)
    total = total * new_share + old_total * old_share
    mixed = mixed * new_share + mixed_ref[...] * old_share
    out = (mixed / total).astype(jnp.bfloat16)
    for h in range(heads):
        o_ref[:, h * HD : (h + 1) * HD] = out[h]


def attend_cached(q, fork_row, page_table, prompt_length, pool, start, count):
    steps, width = q.shape[1:]
    heads = width // HD
    block = min(SET_ROWS, q.shape[0])
    m = block * steps
    cached = pool.shape[0] * pool.shape[1]
    cpages = pool.shape[0] // prompt_length.shape[0]
    return pl.pallas_call(
        functools.partial(cached_kernel, heads, cpages, LOG2E / math.sqrt(HD), start),
        grid_spec=pltpu.PrefetchScalarGridSpec(
            num_scalar_prefetch=2,
            grid=(count,),
            in_specs=[
                pl.BlockSpec((block, steps, width), lambda i, *_: (i + start, 0, 0)),
                pl.BlockSpec(fork_row.shape, lambda i, *_: (0, 0)),
                pl.BlockSpec(pool.shape, lambda i, *_: (0, 0, 0)),
            ],
            out_specs=[pl.BlockSpec((heads, m, HD), lambda i, *_: (0, i, 0))] * 2,
            scratch_shapes=[pltpu.VMEM((heads, m, cached), jnp.float32)],
        ),
        out_shape=[jax.ShapeDtypeStruct((heads, m * count, HD), jnp.float32)] * 2,
        cost_estimate=pl.CostEstimate(
            flops=4 * count * heads * m * cached * HD,
            transcendentals=count * heads * m * cached,
            bytes_accessed=8 * count * heads * m * HD,
        ),
        compiler_params=SMALL,
        name="attend_cached",
    )(page_table, prompt_length, q, fork_row, pool)


def attend_new(q, fork_row, owner, base, span_pairs, tail_pairs, mixed, stat, start, count, skip=0):
    steps, width = q.shape[1:]
    heads = width // HD
    block = min(SET_ROWS, q.shape[0])
    m = block * steps
    span = span_pairs[0].shape[0]
    keys = span * len(span_pairs)
    part = pl.BlockSpec((heads, m, HD), lambda i, *_: (0, i + skip, 0))
    return pl.pallas_call(
        functools.partial(new_kernel, heads, steps, LOG2E / math.sqrt(HD), start),
        grid_spec=pltpu.PrefetchScalarGridSpec(
            num_scalar_prefetch=2,
            grid=(count,),
            in_specs=[
                pl.BlockSpec((block, steps, width), lambda i, *_: (i + start, 0, 0)),
                pl.BlockSpec(fork_row.shape, lambda i, *_: (0, 0)),
                pl.BlockSpec((m, 2 * HD), lambda i, *_: (i, 0)),
                part,
                part,
            ]
            + [pl.BlockSpec((span, 2 * HD), lambda i, *_: (0, 0))] * len(span_pairs),
            out_specs=pl.BlockSpec((m, width), lambda i, *_: (i, 0)),
            scratch_shapes=[pltpu.VMEM((heads, m, keys + m), jnp.float32)],
        ),
        out_shape=jax.ShapeDtypeStruct((m * count, width), jnp.bfloat16),
        cost_estimate=pl.CostEstimate(
            flops=4 * count * heads * m * (keys + m) * HD,
            transcendentals=count * heads * m * (keys + m),
            bytes_accessed=10 * count * heads * m * HD,
        ),
        compiler_params=SMALL,
        name="attend_new",
    )(owner, base, q, fork_row, tail_pairs, mixed, stat, *span_pairs)


def project_kernel(groups, split, kept, sent, rank_ref, *refs):
    keep_ref, send_ref, acc = refs[-3:]
    s = pl.program_id(0)
    rows = [ref[...].reshape(-1, ref.shape[-1]) for ref in refs[:groups]]
    x = rows[0] if groups == 1 else jnp.concatenate(rows, 0)
    refs = refs[groups:]
    w = jnp.concatenate(
        [jnp.concatenate([refs[2 * i][...], refs[2 * i + 1][...]], 1) for i in range(split)], 0
    )
    one = jnp.dot(x, w, preferred_element_type=jnp.float32)

    @pl.when(s == 0)
    def _():
        acc[...] = one

    @pl.when(s > 0)
    def _():
        acc[...] += one

    @pl.when(s == pl.num_programs(0) - 1)
    def _():
        keys = acc.shape[1] // 2
        for ref, rels in ((send_ref, sent), (keep_ref, kept)):
            for i, rel in enumerate(rels):
                at = pl.multiple_of((rank_ref[0] ^ rel) * HD, HD)
                ref[i, :, :HD] = acc[:, pl.ds(at, HD)].astype(ref.dtype)
                ref[i, :, HD:] = acc[:, pl.ds(pl.multiple_of(at + keys, HD), HD)].astype(ref.dtype)


def project(rank, groups, key_weight, value_weight, kept, sent):
    width, columns = key_weight.shape
    depth, split = width // 2, 2
    in_specs = []
    n = 0
    for x, start, rows in groups:
        lead = (rows,) + x.shape[1:-1]
        n += math.prod(lead)
        in_specs.append(
            pl.BlockSpec(
                tuple(pl.Element(d) for d in lead + (depth,)),
                lambda s, r, start=start, lead=lead: (start,) + (0,) * (len(lead) - 1) + (s * depth,),
            )
        )
    for i in range(split):
        piece = pl.BlockSpec((depth // split, columns), lambda s, r, i=i: (s * split + i, 0))
        in_specs += [piece, piece]
    return pl.pallas_call(
        functools.partial(project_kernel, len(groups), split, kept, sent),
        grid_spec=pltpu.PrefetchScalarGridSpec(
            num_scalar_prefetch=1,
            grid=(width // depth,),
            in_specs=in_specs,
            out_specs=[
                pl.BlockSpec((len(rels), n, 2 * HD), lambda s, r: (0, 0, 0)) for rels in (kept, sent)
            ],
            scratch_shapes=[pltpu.VMEM((n, 2 * columns), jnp.float32)],
        ),
        out_shape=[
            jax.ShapeDtypeStruct((len(kept), n, 2 * HD), jnp.float32),
            jax.ShapeDtypeStruct((len(sent), n, 2 * HD), jnp.bfloat16),
        ],
        cost_estimate=pl.CostEstimate(
            flops=4 * n * width * columns, transcendentals=0, bytes_accessed=4 * width * columns
        ),
        compiler_params=SMALL,
        name="project",
    )(
        rank,
        *[in_hbm(x) for x, _, _ in groups],
        *([in_hbm(key_weight), in_hbm(value_weight)] * split),
    )


def finish_kernel(
    span, steps, start, sizes, owner_ref, length_ref, replica_ref, fork_ref, freq_ref, keep_ref, *refs
):
    outs = refs[-len(sizes) :]
    summed = keep_ref[0]
    for ref in refs[: -len(sizes)]:
        summed = summed + (ref[0] if len(ref.shape) == 3 else ref[...]).astype(jnp.float32)
    n = summed.shape[0]
    fork = fork_ref[...]
    lengths = jnp.zeros_like(fork)
    for p in range(length_ref.shape[0]):
        lengths = jnp.where(fork == p, length_ref[p], lengths)
    lead = max(0, span - start)
    places = []
    if lead:
        own = length_ref[owner_ref[replica_ref[0]]]
        places.append(own + start + lax.broadcasted_iota(jnp.int32, (lead, 1), 0).astype(jnp.int32))
        places[0] = places[0].astype(jnp.float32)
    tail = n - lead
    first = start + lead - span
    step = lax.broadcasted_iota(jnp.int32, (tail, 1), 0) % steps
    places.append(
        by_row(lengths, first // steps, tail, steps) + (span + step).astype(jnp.float32)
    )
    places = places[0] if len(places) == 1 else jnp.concatenate(places, 0)
    angle = places * freq_ref[...]
    lane = lax.broadcasted_iota(jnp.int32, (n, HD), 1)
    sine = jnp.where(lane < HD // 2, -jnp.sin(angle), jnp.sin(angle))
    keys = summed[:, :HD]
    turned = keys * jnp.cos(angle) + pltpu.roll(keys, HD // 2, 1) * sine
    at = 0
    for size, o_ref in zip(sizes, outs):
        o_ref[:, :HD] = turned[at : at + size].astype(jnp.bfloat16)
        o_ref[:, HD:] = summed[at : at + size, HD:].astype(jnp.bfloat16)
        at += size


def finish(keep, others, places, start, sizes):
    span, steps, owner, length, replica, fork_row, freq = places
    n = keep.shape[1]
    unit = pl.BlockSpec((1, n, 2 * HD), lambda i, *_: (0, 0, 0))
    flat = lambda rows, width: pl.BlockSpec((rows, width), lambda i, *_: (0, 0))
    return pl.pallas_call(
        functools.partial(finish_kernel, span, steps, start, sizes),
        grid_spec=pltpu.PrefetchScalarGridSpec(
            num_scalar_prefetch=3,
            grid=(1,),
            in_specs=[flat(*fork_row.shape), flat(*freq.shape), unit]
            + [unit if x.ndim == 3 else flat(n, 2 * HD) for x in others],
            out_specs=[flat(size, 2 * HD) for size in sizes],
        ),
        out_shape=[jax.ShapeDtypeStruct((size, 2 * HD), jnp.bfloat16) for size in sizes],
        compiler_params=SMALL,
        name="finish",
    )(owner, length, replica, fork_row, freq, keep, *others)


def swap(x, axis, bit):
    return lax.ppermute(x, axis, [(i, i ^ bit) for i in range(lax.axis_size(axis))])


def swap_sum(keep, send, places, start, sizes):
    got = swap(send, "tensor", 1)
    half = (keep[1] + got[1].astype(jnp.float32)).astype(jnp.bfloat16)
    last = swap(half, "tensor", 2)
    return finish(keep, (got, last), places, start, sizes)


def out_kernel(rels, shapes, cuts, add, held, rank_ref, *refs):
    refs = list(refs)
    pieces = [([refs.pop(0) for _ in range(n)], refs.pop(0) if outer else None) for n, outer in shapes]
    partial = refs.pop(0) if add else None
    w_ref = refs[0]
    o_ref, buf, sem = (refs[-1], None, None) if held else refs[-3:]
    width = pieces[0][0][0].shape[1]
    depth = width // cuts
    rank = rank_ref[0]
    inner = (rank == 1) | (rank == 2)
    copies = []
    for p, rel in enumerate(() if held else rels):
        for c in range(cuts):
            row = pl.multiple_of((rank ^ rel) * width + c * depth, depth)
            slot = p * cuts + c
            copies.append(
                pltpu.make_async_copy(w_ref.at[pl.ds(row, depth), :], buf.at[slot], sem.at[slot])
            )
            copies[-1].start()
    total = partial[...] if add else None
    for p, (groups, outer) in enumerate(pieces):
        a = [ref[...] for ref in groups]
        a = a[0] if len(a) == 1 else jnp.concatenate(a, 0)
        if outer is not None:
            a = jnp.where(inner, a, outer[...])
        for c in range(cuts):
            if held:
                at = held.index(rels[p]) * width + c * depth
                w = w_ref[at : at + depth, :]
            else:
                copies[p * cuts + c].wait()
                w = buf[p * cuts + c]
            one = jnp.dot(
                a[:, c * depth : (c + 1) * depth], w, preferred_element_type=jnp.float32
            )
            total = one if total is None else total + one
    o_ref[...] = total.reshape(o_ref.shape).astype(o_ref.dtype)


def out_project(rank, pieces, weight, shape, start, partial=None, into=None, final=True, held=()):
    width = pieces[0][1][0].shape[1]
    m = sum(x.shape[0] for x in pieces[0][1])
    columns = weight.shape[1]
    steps = shape[1]
    cuts = 1 if held else 4
    flat = lambda x: pl.BlockSpec(x.shape, lambda i, r: (0, 0))
    args = []
    for _, groups, outer in pieces:
        args += list(groups) + ([] if outer is None else [outer])
    if partial is not None:
        args.append(partial)
    in_specs = [flat(x) for x in args]
    args.append(weight if held else in_hbm(weight))
    in_specs.append(pl.BlockSpec(memory_space=pltpu.VMEM if held else pl.ANY))
    aliases = {}
    if into is not None:
        args.append(into)
        in_specs.append(pl.BlockSpec(memory_space=pl.ANY))
        aliases = {len(args): 0}
    if final:
        out_spec = pl.BlockSpec(
            (pl.Element(m // steps), pl.Element(steps), pl.Element(columns)),
            lambda i, r: (start, 0, 0),
        )
        out_shape = jax.ShapeDtypeStruct(shape, jnp.bfloat16)
    else:
        out_spec = pl.BlockSpec((m, columns), lambda i, r: (0, 0))
        out_shape = jax.ShapeDtypeStruct((m, columns), jnp.float32)
    rels = tuple(rel for rel, _, _ in pieces)
    shapes = tuple((len(groups), outer is not None) for _, groups, outer in pieces)
    slots = len(rels) * cuts
    return pl.pallas_call(
        functools.partial(out_kernel, rels, shapes, cuts, partial is not None, held),
        grid_spec=pltpu.PrefetchScalarGridSpec(
            num_scalar_prefetch=1,
            grid=(1,),
            in_specs=in_specs,
            out_specs=out_spec,
            scratch_shapes=[]
            if held
            else [
                pltpu.VMEM((slots, width // cuts, columns), jnp.bfloat16),
                pltpu.SemaphoreType.DMA((slots,)),
            ],
        ),
        out_shape=out_shape,
        input_output_aliases=aliases,
        cost_estimate=pl.CostEstimate(
            flops=2 * m * width * columns * len(rels),
            transcendentals=0,
            bytes_accessed=2 * width * columns * len(rels),
        ),
        compiler_params=LARGE,
        name="out_project",
    )(rank, *args)


def hold_kernel(rels, rank_ref, w_ref, o_ref, sem):
    rows = o_ref.shape[0] // len(rels)
    copies = []
    for i, rel in enumerate(rels):
        at = pl.multiple_of((rank_ref[0] ^ rel) * rows, rows)
        copies.append(
            pltpu.make_async_copy(
                w_ref.at[pl.ds(at, rows), :], o_ref.at[i * rows : (i + 1) * rows, :], sem.at[i]
            )
        )
        copies[-1].start()
    for copy in copies:
        copy.wait()


def hold(rank, rels, weight, rows):
    held = pl.pallas_call(
        functools.partial(hold_kernel, rels),
        grid_spec=pltpu.PrefetchScalarGridSpec(
            num_scalar_prefetch=1,
            grid=(1,),
            in_specs=[pl.BlockSpec(memory_space=pl.ANY)],
            out_specs=pl.BlockSpec(memory_space=pltpu.VMEM),
            scratch_shapes=[pltpu.SemaphoreType.DMA((len(rels),))],
        ),
        out_shape=jax.ShapeDtypeStruct((len(rels) * rows, weight.shape[1]), weight.dtype),
        compiler_params=SMALL,
        name="hold",
    )(rank, in_hbm(weight))
    return pltpu.with_memory_space_constraint(held, pltpu.VMEM)


def near_heads(groups):
    near = []
    for group in groups:
        near.append(swap(group, "tensor", 1))
    return near


def far_heads(own, relay):
    outward = [(1, 0), (2, 3)]
    far = lax.ppermute(own, "tensor", [(0, 2), (3, 1)]) if relay else swap(own, "tensor", 2)
    across = lax.ppermute(own, "tensor", [(1, 2), (2, 1)])
    forward = None
    if relay:
        forward = lax.ppermute(across, "tensor", outward)
    passed = lax.ppermute(far, "tensor", outward)
    return (2, [far], forward), (3, [across], passed)


def on_device(
    prompt_owner,
    fork_map,
    page_table,
    prompt_length,
    span_states,
    decode_states,
    decode_queries,
    key_weight,
    value_weight,
    out_weight,
    page_pool,
):
    replica = lax.axis_index("replica")
    device_rank = lax.axis_index("tensor")
    n_replica = lax.axis_size("replica")
    n_tensor = lax.axis_size("tensor")
    span = span_states.shape[0]
    rows, steps, width = decode_states.shape
    kv_heads = key_weight.shape[1] // HD
    sharing = n_tensor // kv_heads
    prompts = jnp.arange(n_replica, dtype=jnp.int32)
    own_prompt = jnp.sum(jnp.where(prompts == replica, prompt_owner, 0))
    own_length = jnp.sum(jnp.where(prompts == own_prompt, prompt_length, 0))
    row_hits = fork_map[:, None] == prompts[None, :]
    row_length = jnp.sum(jnp.where(row_hits, prompt_length[None, :], 0), 1)
    span_places = own_length + jnp.arange(span, dtype=jnp.int32)
    tail_places = (
        row_length[:, None] + span + jnp.arange(steps, dtype=jnp.int32)[None, :]
    ).reshape(-1)
    pool = page_pool.reshape(page_pool.shape[1:])
    short_line = n_tensor == kv_heads == 4 and n_replica == 4
    first = min(SET_ROWS, rows)
    blocks = rows // first

    if not short_line:
        positions = jnp.concatenate([span_places, tail_places])
        tokens = jnp.concatenate([span_states, decode_states.reshape(rows * steps, width)], 0)
        projected = jnp.dot(
            tokens,
            jnp.concatenate([key_weight, value_weight], 1),
            preferred_element_type=jnp.float32,
        )
        share = lax.psum_scatter(projected, "tensor", scatter_dimension=0, tiled=True)
        number = share.shape[0]
        places = lax.dynamic_slice_in_dim(positions, device_rank * number, number)
        turned = rotate_round(share, places, kv_heads)
        groups = jnp.stack([own_pair(turned, g, kv_heads) for g in range(kv_heads)], 0)
        outgoing = jnp.repeat(groups, sharing, axis=0)
        paired = lax.all_to_all(
            outgoing, "tensor", split_axis=0, concat_axis=1, tiled=True
        ).reshape(-1, 2 * HD)
        arrived = lax.all_gather(paired[:span], "replica", axis=0, tiled=True)
        mixed, stat = attend_cached(
            decode_queries, fork_map[None, :], page_table, prompt_length, pool, 0, blocks
        )
        own = attend_new(
            decode_queries,
            fork_map[None, :],
            prompt_owner,
            jnp.zeros((1,), jnp.int32),
            jnp.split(arrived, n_replica),
            paired[span:],
            mixed,
            stat,
            0,
            blocks,
        )
        decoded = jnp.dot(
            lax.all_gather(own, "tensor", axis=1, tiled=True),
            out_weight,
            preferred_element_type=jnp.float32,
        )
        return decoded.astype(jnp.bfloat16).reshape(rows, steps, out_weight.shape[1])

    rank = device_rank.reshape(1).astype(jnp.int32)
    return line_of_four(
        rank, replica.reshape(1).astype(jnp.int32), prompt_owner, fork_map, page_table,
        prompt_length, span_states, decode_states, decode_queries, key_weight, value_weight,
        out_weight, pool,
    )


def line_of_four(
    rank, replica, prompt_owner, fork_map, page_table, prompt_length, span_states, decode_states,
    decode_queries, key_weight, value_weight, out_weight, pool,
):
    n_replica = lax.axis_size("replica")
    span = span_states.shape[0]
    rows, steps, _ = decode_states.shape
    first = min(SET_ROWS, rows)
    blocks = rows // first
    middle = blocks - 2
    cut = first * steps

    first_units = project(
        rank, ((span_states, 0, span), (decode_states, 0, first)), key_weight, value_weight,
        (0, 2), (1, 3),
    )
    rest_units = project(
        rank, ((decode_states, first, rows - first),), key_weight, value_weight, (0, 2), (1, 3)
    )
    fork_row = fork_map[None, :]
    half = rope_base ** (-(2.0 / HD) * jnp.arange(HD // 2, dtype=jnp.float32))
    freq = jnp.concatenate([half, half])[None, :]
    places = (span, steps, prompt_owner, prompt_length, replica, fork_row, freq)
    own_span, first_tail = swap_sum(*first_units, places, 0, (span, cut))
    arrived = [own_span]
    for j in range(1, n_replica):
        arrived.append(swap(own_span, "replica", j))
    rest_tails = swap_sum(*rest_units, places, span + cut, (cut,) * (blocks - 1))

    def old_part(start, count):
        return attend_cached(
            decode_queries, fork_row, page_table, prompt_length, pool, start, count
        )

    def new_part(tail, old, start, skip=0):
        return attend_new(
            decode_queries, fork_row, prompt_owner, replica, arrived, tail, *old, start, 1, skip
        )

    shape = (rows, steps, out_weight.shape[1])
    first_own = new_part(first_tail, old_part(0, 1), 0)
    middle_old = old_part(1, middle)
    middle_own = [new_part(rest_tails[i], middle_old, 1 + i, i) for i in range(middle)]
    last_own = new_part(rest_tails[-1], old_part(blocks - 1, 1), blocks - 1)
    near = near_heads([first_own])
    two, three = far_heads(first_own, False)
    decoded = out_project(
        rank, ((0, [first_own], None), two, (1, near, None), three), out_weight, shape, 0
    )
    held = (2, 3)
    held_rows = hold(rank, held, out_weight, first_own.shape[1])
    near = near_heads(middle_own)
    two, three = far_heads(jnp.concatenate(middle_own, 0), False)
    pieces = ((0, middle_own, None), (1, near, None), two)
    partial = out_project(rank, pieces, out_weight, shape, 0, final=False)
    decoded = out_project(
        rank, (three,), held_rows, shape, first, partial=partial, into=decoded, held=held
    )
    near = near_heads([last_own])
    two, three = far_heads(last_own, True)
    pieces = ((0, [last_own], None), (1, near, None))
    partial = out_project(rank, pieces, out_weight, shape, 0, final=False)
    return out_project(
        rank, (two, three), held_rows, shape, first * (blocks - 1),
        partial=partial, into=decoded, held=held,
    )


def solution(mesh):
    in_specs = (
        P("parts"),
        P(("parts", "replica")),
        P("parts"),
        P("parts"),
        P(("parts", "replica"), "tensor"),
        P(("parts", "replica"), None, "tensor"),
        P(("parts", "replica"), None, "tensor"),
        P("tensor", None),
        P("tensor", None),
        P(None, "tensor"),
        P("tensor", "parts", None, None),
    )
    out_specs = P(("parts", "replica"), None, "tensor")
    return jax.shard_map(
        on_device, mesh=mesh, in_specs=in_specs, out_specs=out_specs, check_vma=False
    )
```

```python
import functools
import math

import jax
import jax.numpy as jnp
from jax import lax
from jax.experimental import pallas as pl
from jax.experimental.pallas import tpu as pltpu
from jax.sharding import PartitionSpec as P


HD = 128
rope_base = 1000000.0
LOG2E = math.log2(math.e)
HIDDEN = -1e30


def rotary(vectors, places):
    half = vectors.shape[-1] // 2
    freq = rope_base ** (-(2.0 / vectors.shape[-1]) * jnp.arange(half, dtype=jnp.float32))
    angle = places.astype(jnp.float32)[..., None, None] * freq
    cosine = jnp.cos(angle)
    sine = jnp.sin(angle)
    first = vectors[..., :half]
    second = vectors[..., half:]
    return jnp.concatenate([first * cosine - second * sine, second * cosine + first * sine], -1)


def rotate_round(summed, places, kv_heads):
    number = summed.shape[0]
    turned = rotary(summed[:, : kv_heads * HD].reshape(number, kv_heads, HD), places)
    turned = turned.astype(jnp.bfloat16).reshape(number, kv_heads * HD)
    return jnp.concatenate([turned, summed[:, kv_heads * HD :].astype(jnp.bfloat16)], 1)


def own_pair(packed, head_group, kv_heads):
    key_part = lax.dynamic_slice_in_dim(packed, head_group * HD, HD, 1)
    value_part = lax.dynamic_slice_in_dim(packed, (kv_heads + head_group) * HD, HD, 1)
    return jnp.concatenate([key_part, value_part], 1)


NT = (((1,), (1,)), ((), ()))
SMALL = pltpu.CompilerParams(vmem_limit_bytes=24 << 20)
LARGE = pltpu.CompilerParams(vmem_limit_bytes=36 << 20)
SET_ROWS = 32


def in_hbm(x):
    return pltpu.with_memory_space_constraint(x, pltpu.HBM)


def lane_tiles(combine, x):
    out = x[..., :HD]
    for i in range(1, x.shape[-1] // HD):
        out = combine(out, x[..., i * HD : (i + 1) * HD])
    return out


ON_CHIP = pl.BlockSpec(memory_space=pltpu.VMEM)


def stacked_heads(q_ref, heads, block, direct, start):
    at = start * block if direct else 0
    m = block * q_ref.shape[1]
    q = q_ref[at : at + block].reshape(m, heads * HD)
    return jnp.concatenate([q[:, h * HD : (h + 1) * HD] for h in range(heads)], 0)


def softmax_parts(qs, heads, parts, scale2, s_ref):
    m = qs.shape[0] // heads
    top = None
    at = 0
    for n, load, bias in parts:
        s = lax.dot_general(qs, load()[:, :HD], NT, preferred_element_type=jnp.float32)
        s = s.reshape(heads, m, n) * scale2 + bias()[None]
        s_ref[:, :, at : at + n] = s
        most = lane_tiles(jnp.maximum, s)
        top = most if top is None else jnp.maximum(top, most)
        at += n
    top = jnp.max(top, -1, keepdims=True)
    total = mixed = None
    at = 0
    for n, load, _ in parts:
        w = jnp.exp2(s_ref[:, :, at : at + n] - top)
        summed = lane_tiles(jnp.add, w)
        one = jnp.dot(
            w.astype(jnp.bfloat16).reshape(heads * m, n),
            load()[:, HD:],
            preferred_element_type=jnp.float32,
        ).reshape(heads, m, HD)
        total = summed if total is None else total + summed
        mixed = one if mixed is None else mixed + one
        at += n
    return top, jnp.sum(total, -1, keepdims=True), mixed


def by_row(values, first, rows, steps):
    lane = lax.broadcasted_iota(jnp.int32, (rows, values.shape[1]), 1)
    row = lax.broadcasted_iota(jnp.int32, (rows, values.shape[1]), 0)
    mine = jnp.where(lane == first + row // steps, values.astype(jnp.float32), 0.0)
    return jnp.sum(mine, 1, keepdims=True)


def shown(allowed):
    return jnp.where(allowed, 0.0, HIDDEN)


def cached_kernel(
    heads, block, direct, cpages, scale2, start, table_ref, length_ref, q_ref, fork_ref, pool_ref, mixed_ref, stat_ref, s_ref
):
    qs = stacked_heads(q_ref, heads, block, direct, start)
    m = qs.shape[0] // heads
    steps = q_ref.shape[1]
    prompt = by_row(fork_ref[...], (pl.program_id(0) + start) * block, m, steps)
    pages, size = pool_ref.shape[:2]
    group = cpages

    def part(at):
        mine = range(at, min(at + group, pages))

        def load():
            return jnp.concatenate([pool_ref[table_ref[i]] for i in mine], 0)

        def bias():
            lane = lax.broadcasted_iota(jnp.int32, (m, size), 1)
            return jnp.concatenate(
                [
                    shown(
                        (prompt == float(i // cpages))
                        & (lane < length_ref[i // cpages] - (i % cpages) * size)
                    )
                    for i in mine
                ],
                1,
            )

        return len(mine) * size, load, bias

    parts = [part(at) for at in range(0, pages, group)]
    top, total, mixed = softmax_parts(qs, heads, parts, scale2, s_ref)
    mixed_ref[...] = mixed
    lane = lax.broadcasted_iota(jnp.int32, mixed.shape, 2)
    stat_ref[...] = jnp.where(lane < HD // 2, top, total)


def new_kernel(
    heads, block, direct, skip, steps, scale2, start, owner_ref, base_ref, q_ref, fork_ref, tail_ref, mixed_ref, stat_ref, *refs
):
    span_refs, o_ref, s_ref = refs[:-2], refs[-2], refs[-1]
    qs = stacked_heads(q_ref, heads, block, direct, start)
    m = qs.shape[0] // heads
    span = span_refs[0].shape[0]
    prompt = by_row(fork_ref[...], (pl.program_id(0) + start) * block, m, steps)
    at = skip * m if direct else 0
    mine = slice(at, at + m)

    def loaded():
        return jnp.concatenate([ref[...] for ref in span_refs], 0)

    def owned():
        return jnp.concatenate(
            [
                jnp.broadcast_to(
                    shown(prompt == owner_ref[base_ref[0] ^ j].astype(jnp.float32)), (m, span)
                )
                for j in range(len(span_refs))
            ],
            1,
        )

    def causal():
        row = lax.broadcasted_iota(jnp.int32, (m, m), 0)
        col = lax.broadcasted_iota(jnp.int32, (m, m), 1)
        return shown((row // steps == col // steps) & (col <= row))

    parts = (
        (span * len(span_refs), loaded, owned),
        (m, lambda: tail_ref[...], causal),
    )
    top, total, mixed = softmax_parts(qs, heads, parts, scale2, s_ref)
    old_top = stat_ref[:, mine, :1]
    old_total = stat_ref[:, mine, HD // 2 : HD // 2 + 1]
    both = jnp.maximum(top, old_top)
    new_share = jnp.exp2(top - both)
    old_share = jnp.exp2(old_top - both)
    total = total * new_share + old_total * old_share
    mixed = mixed * new_share + mixed_ref[:, mine, :] * old_share
    out = (mixed / total).astype(jnp.bfloat16)
    for h in range(heads):
        o_ref[:, h * HD : (h + 1) * HD] = out[h]


def attend_cached(q, fork_row, page_table, prompt_length, pool, start, count):
    steps, width = q.shape[1:]
    heads = width // HD
    block = min(SET_ROWS, q.shape[0])
    m = block * steps
    cached = pool.shape[0] * pool.shape[1]
    cpages = pool.shape[0] // prompt_length.shape[0]
    direct = count == 1
    return pl.pallas_call(
        functools.partial(cached_kernel, heads, block, direct, cpages, LOG2E / math.sqrt(HD), start),
        grid_spec=pltpu.PrefetchScalarGridSpec(
            num_scalar_prefetch=2,
            grid=(count,),
            in_specs=[ON_CHIP] * 3
            if direct
            else [
                pl.BlockSpec((block, steps, width), lambda i, *_: (i + start, 0, 0)),
                pl.BlockSpec(fork_row.shape, lambda i, *_: (0, 0)),
                pl.BlockSpec(pool.shape, lambda i, *_: (0, 0, 0)),
            ],
            out_specs=[ON_CHIP] * 2
            if direct
            else [pl.BlockSpec((heads, m, HD), lambda i, *_: (0, i, 0))] * 2,
            scratch_shapes=[pltpu.VMEM((heads, m, cached), jnp.float32)],
        ),
        out_shape=[jax.ShapeDtypeStruct((heads, m * count, HD), jnp.float32)] * 2,
        cost_estimate=pl.CostEstimate(
            flops=4 * count * heads * m * cached * HD,
            transcendentals=count * heads * m * cached,
            bytes_accessed=8 * count * heads * m * HD,
        ),
        compiler_params=SMALL,
        name="attend_cached",
    )(page_table, prompt_length, q, fork_row, pool)


def attend_new(q, fork_row, owner, base, span_pairs, tail_pairs, mixed, stat, start, count, skip=0):
    steps, width = q.shape[1:]
    heads = width // HD
    block = min(SET_ROWS, q.shape[0])
    m = block * steps
    span = span_pairs[0].shape[0]
    keys = span * len(span_pairs)
    direct = count == 1
    part = pl.BlockSpec((heads, m, HD), lambda i, *_: (0, i + skip, 0))
    return pl.pallas_call(
        functools.partial(new_kernel, heads, block, direct, skip, steps, LOG2E / math.sqrt(HD), start),
        grid_spec=pltpu.PrefetchScalarGridSpec(
            num_scalar_prefetch=2,
            grid=(count,),
            in_specs=[ON_CHIP] * (5 + len(span_pairs))
            if direct
            else [
                pl.BlockSpec((block, steps, width), lambda i, *_: (i + start, 0, 0)),
                pl.BlockSpec(fork_row.shape, lambda i, *_: (0, 0)),
                pl.BlockSpec((m, 2 * HD), lambda i, *_: (i, 0)),
                part,
                part,
            ]
            + [pl.BlockSpec((span, 2 * HD), lambda i, *_: (0, 0))] * len(span_pairs),
            out_specs=ON_CHIP if direct else pl.BlockSpec((m, width), lambda i, *_: (i, 0)),
            scratch_shapes=[pltpu.VMEM((heads, m, keys + m), jnp.float32)],
        ),
        out_shape=jax.ShapeDtypeStruct((m * count, width), jnp.bfloat16),
        cost_estimate=pl.CostEstimate(
            flops=4 * count * heads * m * (keys + m) * HD,
            transcendentals=count * heads * m * (keys + m),
            bytes_accessed=10 * count * heads * m * HD,
        ),
        compiler_params=SMALL,
        name="attend_new",
    )(owner, base, q, fork_row, tail_pairs, mixed, stat, *span_pairs)


def project_kernel(groups, split, kept, sent, rank_ref, *refs):
    keep_ref, send_ref, acc = refs[-3:]
    s = pl.program_id(0)
    rows = [ref[...].reshape(-1, ref.shape[-1]) for ref in refs[:groups]]
    x = rows[0] if groups == 1 else jnp.concatenate(rows, 0)
    refs = refs[groups:]
    w = jnp.concatenate(
        [jnp.concatenate([refs[2 * i][...], refs[2 * i + 1][...]], 1) for i in range(split)], 0
    )
    one = jnp.dot(x, w, preferred_element_type=jnp.float32)

    @pl.when(s == 0)
    def _():
        acc[...] = one

    @pl.when(s > 0)
    def _():
        acc[...] += one

    @pl.when(s == pl.num_programs(0) - 1)
    def _():
        keys = acc.shape[1] // 2
        for ref, rels in ((send_ref, sent), (keep_ref, kept)):
            for i, rel in enumerate(rels):
                at = pl.multiple_of((rank_ref[0] ^ rel) * HD, HD)
                ref[i, :, :HD] = acc[:, pl.ds(at, HD)].astype(ref.dtype)
                ref[i, :, HD:] = acc[:, pl.ds(pl.multiple_of(at + keys, HD), HD)].astype(ref.dtype)


def project(rank, groups, key_weight, value_weight, kept, sent):
    width, columns = key_weight.shape
    depth, split = width // 2, 2
    in_specs = []
    n = 0
    for x, start, rows in groups:
        lead = (rows,) + x.shape[1:-1]
        n += math.prod(lead)
        in_specs.append(
            pl.BlockSpec(
                tuple(pl.Element(d) for d in lead + (depth,)),
                lambda s, r, start=start, lead=lead: (start,) + (0,) * (len(lead) - 1) + (s * depth,),
            )
        )
    for i in range(split):
        piece = pl.BlockSpec((depth // split, columns), lambda s, r, i=i: (s * split + i, 0))
        in_specs += [piece, piece]
    return pl.pallas_call(
        functools.partial(project_kernel, len(groups), split, kept, sent),
        grid_spec=pltpu.PrefetchScalarGridSpec(
            num_scalar_prefetch=1,
            grid=(width // depth,),
            in_specs=in_specs,
            out_specs=[
                pl.BlockSpec((len(rels), n, 2 * HD), lambda s, r: (0, 0, 0)) for rels in (kept, sent)
            ],
            scratch_shapes=[pltpu.VMEM((n, 2 * columns), jnp.float32)],
        ),
        out_shape=[
            jax.ShapeDtypeStruct((len(kept), n, 2 * HD), jnp.float32),
            jax.ShapeDtypeStruct((len(sent), n, 2 * HD), jnp.bfloat16),
        ],
        cost_estimate=pl.CostEstimate(
            flops=4 * n * width * columns, transcendentals=0, bytes_accessed=4 * width * columns
        ),
        compiler_params=SMALL,
        name="project",
    )(
        rank,
        *[in_hbm(x) for x, _, _ in groups],
        *([in_hbm(key_weight), in_hbm(value_weight)] * split),
    )


def finish_kernel(
    span, steps, start, sizes, owner_ref, length_ref, replica_ref, fork_ref, freq_ref, keep_ref, *refs
):
    outs = refs[-len(sizes) :]
    summed = keep_ref[0]
    for ref in refs[: -len(sizes)]:
        summed = summed + (ref[0] if len(ref.shape) == 3 else ref[...]).astype(jnp.float32)
    n = summed.shape[0]
    fork = fork_ref[...]
    lengths = jnp.zeros_like(fork)
    for p in range(length_ref.shape[0]):
        lengths = jnp.where(fork == p, length_ref[p], lengths)
    lead = max(0, span - start)
    places = []
    if lead:
        own = length_ref[owner_ref[replica_ref[0]]]
        places.append(own + start + lax.broadcasted_iota(jnp.int32, (lead, 1), 0).astype(jnp.int32))
        places[0] = places[0].astype(jnp.float32)
    tail = n - lead
    first = start + lead - span
    step = lax.broadcasted_iota(jnp.int32, (tail, 1), 0) % steps
    places.append(
        by_row(lengths, first // steps, tail, steps) + (span + step).astype(jnp.float32)
    )
    places = places[0] if len(places) == 1 else jnp.concatenate(places, 0)
    angle = places * freq_ref[...]
    lane = lax.broadcasted_iota(jnp.int32, (n, HD), 1)
    sine = jnp.where(lane < HD // 2, -jnp.sin(angle), jnp.sin(angle))
    keys = summed[:, :HD]
    turned = keys * jnp.cos(angle) + pltpu.roll(keys, HD // 2, 1) * sine
    at = 0
    for size, o_ref in zip(sizes, outs):
        o_ref[:, :HD] = turned[at : at + size].astype(jnp.bfloat16)
        o_ref[:, HD:] = summed[at : at + size, HD:].astype(jnp.bfloat16)
        at += size


def finish(keep, others, places, start, sizes):
    span, steps, owner, length, replica, fork_row, freq = places
    return pl.pallas_call(
        functools.partial(finish_kernel, span, steps, start, sizes),
        grid_spec=pltpu.PrefetchScalarGridSpec(
            num_scalar_prefetch=3,
            grid=(1,),
            in_specs=[ON_CHIP] * (3 + len(others)),
            out_specs=[ON_CHIP] * len(sizes),
        ),
        out_shape=[jax.ShapeDtypeStruct((size, 2 * HD), jnp.bfloat16) for size in sizes],
        compiler_params=SMALL,
        name="finish",
    )(owner, length, replica, fork_row, freq, keep, *others)


def swap(x, axis, bit):
    return lax.ppermute(x, axis, [(i, i ^ bit) for i in range(lax.axis_size(axis))])


def swap_sum(keep, send, places, start, sizes):
    got = swap(send, "tensor", 1)
    half = (keep[1] + got[1].astype(jnp.float32)).astype(jnp.bfloat16)
    last = swap(half, "tensor", 2)
    return finish(keep, (got, last), places, start, sizes)


def out_kernel(rels, shapes, cuts, add, held, rank_ref, *refs):
    refs = list(refs)
    pieces = [([refs.pop(0) for _ in range(n)], refs.pop(0) if outer else None) for n, outer in shapes]
    partial = refs.pop(0) if add else None
    w_ref = refs[0]
    o_ref, buf, sem = (refs[-1], None, None) if held else refs[-3:]
    width = pieces[0][0][0].shape[1]
    depth = width // cuts
    rank = rank_ref[0]
    inner = (rank == 1) | (rank == 2)
    copies = []
    for p, rel in enumerate(() if held else rels):
        for c in range(cuts):
            row = pl.multiple_of((rank ^ rel) * width + c * depth, depth)
            slot = p * cuts + c
            copies.append(
                pltpu.make_async_copy(w_ref.at[pl.ds(row, depth), :], buf.at[slot], sem.at[slot])
            )
            copies[-1].start()
    total = partial[...] if add else None
    for p, (groups, outer) in enumerate(pieces):
        a = [ref[...] for ref in groups]
        a = a[0] if len(a) == 1 else jnp.concatenate(a, 0)
        if outer is not None:
            a = jnp.where(inner, a, outer[...])
        for c in range(cuts):
            if held:
                at = held.index(rels[p]) * width + c * depth
                w = w_ref[at : at + depth, :]
            else:
                copies[p * cuts + c].wait()
                w = buf[p * cuts + c]
            one = jnp.dot(
                a[:, c * depth : (c + 1) * depth], w, preferred_element_type=jnp.float32
            )
            total = one if total is None else total + one
    o_ref[...] = total.reshape(o_ref.shape).astype(o_ref.dtype)


def out_project(rank, pieces, weight, shape, start, partial=None, into=None, final=True, held=()):
    width = pieces[0][1][0].shape[1]
    m = sum(x.shape[0] for x in pieces[0][1])
    columns = weight.shape[1]
    steps = shape[1]
    cuts = 1 if held else 4
    flat = lambda x: pl.BlockSpec(x.shape, lambda i, r: (0, 0))
    args = []
    for _, groups, outer in pieces:
        args += list(groups) + ([] if outer is None else [outer])
    if partial is not None:
        args.append(partial)
    in_specs = [flat(x) for x in args]
    args.append(weight if held else in_hbm(weight))
    in_specs.append(pl.BlockSpec(memory_space=pltpu.VMEM if held else pl.ANY))
    aliases = {}
    if into is not None:
        args.append(into)
        in_specs.append(pl.BlockSpec(memory_space=pl.ANY))
        aliases = {len(args): 0}
    if final:
        out_spec = pl.BlockSpec(
            (pl.Element(m // steps), pl.Element(steps), pl.Element(columns)),
            lambda i, r: (start, 0, 0),
        )
        out_shape = jax.ShapeDtypeStruct(shape, jnp.bfloat16)
    else:
        out_spec = pl.BlockSpec((m, columns), lambda i, r: (0, 0))
        out_shape = jax.ShapeDtypeStruct((m, columns), jnp.float32)
    rels = tuple(rel for rel, _, _ in pieces)
    shapes = tuple((len(groups), outer is not None) for _, groups, outer in pieces)
    slots = len(rels) * cuts
    return pl.pallas_call(
        functools.partial(out_kernel, rels, shapes, cuts, partial is not None, held),
        grid_spec=pltpu.PrefetchScalarGridSpec(
            num_scalar_prefetch=1,
            grid=(1,),
            in_specs=in_specs,
            out_specs=out_spec,
            scratch_shapes=[]
            if held
            else [
                pltpu.VMEM((slots, width // cuts, columns), jnp.bfloat16),
                pltpu.SemaphoreType.DMA((slots,)),
            ],
        ),
        out_shape=out_shape,
        input_output_aliases=aliases,
        cost_estimate=pl.CostEstimate(
            flops=2 * m * width * columns * len(rels),
            transcendentals=0,
            bytes_accessed=2 * width * columns * len(rels),
        ),
        compiler_params=LARGE,
        name="out_project",
    )(rank, *args)


def hold_kernel(rels, rank_ref, w_ref, o_ref, sem):
    rows = o_ref.shape[0] // len(rels)
    copies = []
    for i, rel in enumerate(rels):
        at = pl.multiple_of((rank_ref[0] ^ rel) * rows, rows)
        copies.append(
            pltpu.make_async_copy(
                w_ref.at[pl.ds(at, rows), :], o_ref.at[i * rows : (i + 1) * rows, :], sem.at[i]
            )
        )
        copies[-1].start()
    for copy in copies:
        copy.wait()


def hold(rank, rels, weight, rows):
    held = pl.pallas_call(
        functools.partial(hold_kernel, rels),
        grid_spec=pltpu.PrefetchScalarGridSpec(
            num_scalar_prefetch=1,
            grid=(1,),
            in_specs=[pl.BlockSpec(memory_space=pl.ANY)],
            out_specs=pl.BlockSpec(memory_space=pltpu.VMEM),
            scratch_shapes=[pltpu.SemaphoreType.DMA((len(rels),))],
        ),
        out_shape=jax.ShapeDtypeStruct((len(rels) * rows, weight.shape[1]), weight.dtype),
        compiler_params=SMALL,
        name="hold",
    )(rank, in_hbm(weight))
    return pltpu.with_memory_space_constraint(held, pltpu.VMEM)


def near_heads(groups):
    near = []
    for group in groups:
        near.append(swap(group, "tensor", 1))
    return near


def far_heads(own, relay):
    outward = [(1, 0), (2, 3)]
    far = lax.ppermute(own, "tensor", [(0, 2), (3, 1)]) if relay else swap(own, "tensor", 2)
    across = lax.ppermute(own, "tensor", [(1, 2), (2, 1)])
    forward = None
    if relay:
        forward = lax.ppermute(across, "tensor", outward)
    passed = lax.ppermute(far, "tensor", outward)
    return (2, [far], forward), (3, [across], passed)


def on_device(
    prompt_owner,
    fork_map,
    page_table,
    prompt_length,
    span_states,
    decode_states,
    decode_queries,
    key_weight,
    value_weight,
    out_weight,
    page_pool,
):
    replica = lax.axis_index("replica")
    device_rank = lax.axis_index("tensor")
    n_replica = lax.axis_size("replica")
    n_tensor = lax.axis_size("tensor")
    span = span_states.shape[0]
    rows, steps, width = decode_states.shape
    kv_heads = key_weight.shape[1] // HD
    sharing = n_tensor // kv_heads
    prompts = jnp.arange(n_replica, dtype=jnp.int32)
    own_prompt = jnp.sum(jnp.where(prompts == replica, prompt_owner, 0))
    own_length = jnp.sum(jnp.where(prompts == own_prompt, prompt_length, 0))
    row_hits = fork_map[:, None] == prompts[None, :]
    row_length = jnp.sum(jnp.where(row_hits, prompt_length[None, :], 0), 1)
    span_places = own_length + jnp.arange(span, dtype=jnp.int32)
    tail_places = (
        row_length[:, None] + span + jnp.arange(steps, dtype=jnp.int32)[None, :]
    ).reshape(-1)
    pool = page_pool.reshape(page_pool.shape[1:])
    short_line = n_tensor == kv_heads == 4 and n_replica == 4
    first = min(SET_ROWS, rows)
    blocks = rows // first

    if not short_line:
        positions = jnp.concatenate([span_places, tail_places])
        tokens = jnp.concatenate([span_states, decode_states.reshape(rows * steps, width)], 0)
        projected = jnp.dot(
            tokens,
            jnp.concatenate([key_weight, value_weight], 1),
            preferred_element_type=jnp.float32,
        )
        share = lax.psum_scatter(projected, "tensor", scatter_dimension=0, tiled=True)
        number = share.shape[0]
        places = lax.dynamic_slice_in_dim(positions, device_rank * number, number)
        turned = rotate_round(share, places, kv_heads)
        groups = jnp.stack([own_pair(turned, g, kv_heads) for g in range(kv_heads)], 0)
        outgoing = jnp.repeat(groups, sharing, axis=0)
        paired = lax.all_to_all(
            outgoing, "tensor", split_axis=0, concat_axis=1, tiled=True
        ).reshape(-1, 2 * HD)
        arrived = lax.all_gather(paired[:span], "replica", axis=0, tiled=True)
        mixed, stat = attend_cached(
            decode_queries, fork_map[None, :], page_table, prompt_length, pool, 0, blocks
        )
        own = attend_new(
            decode_queries,
            fork_map[None, :],
            prompt_owner,
            jnp.zeros((1,), jnp.int32),
            jnp.split(arrived, n_replica),
            paired[span:],
            mixed,
            stat,
            0,
            blocks,
        )
        decoded = jnp.dot(
            lax.all_gather(own, "tensor", axis=1, tiled=True),
            out_weight,
            preferred_element_type=jnp.float32,
        )
        return decoded.astype(jnp.bfloat16).reshape(rows, steps, out_weight.shape[1])

    rank = device_rank.reshape(1).astype(jnp.int32)
    return line_of_four(
        rank, replica.reshape(1).astype(jnp.int32), prompt_owner, fork_map, page_table,
        prompt_length, span_states, decode_states, decode_queries, key_weight, value_weight,
        out_weight, pool,
    )


def line_of_four(
    rank, replica, prompt_owner, fork_map, page_table, prompt_length, span_states, decode_states,
    decode_queries, key_weight, value_weight, out_weight, pool,
):
    n_replica = lax.axis_size("replica")
    span = span_states.shape[0]
    rows, steps, _ = decode_states.shape
    first = min(SET_ROWS, rows)
    blocks = rows // first
    middle = blocks - 2
    cut = first * steps

    first_units = project(
        rank, ((span_states, 0, span), (decode_states, 0, first)), key_weight, value_weight,
        (0, 2), (1, 3),
    )
    rest_units = project(
        rank, ((decode_states, first, rows - first),), key_weight, value_weight, (0, 2), (1, 3)
    )
    fork_row = fork_map[None, :]
    half = rope_base ** (-(2.0 / HD) * jnp.arange(HD // 2, dtype=jnp.float32))
    freq = jnp.concatenate([half, half])[None, :]
    places = (span, steps, prompt_owner, prompt_length, replica, fork_row, freq)
    own_span, first_tail = swap_sum(*first_units, places, 0, (span, cut))
    arrived = [own_span]
    for j in range(1, n_replica):
        arrived.append(swap(own_span, "replica", j))
    rest_tails = swap_sum(*rest_units, places, span + cut, (cut,) * (blocks - 1))

    def old_part(start, count):
        return attend_cached(
            decode_queries, fork_row, page_table, prompt_length, pool, start, count
        )

    def new_part(tail, old, start, skip=0):
        return attend_new(
            decode_queries, fork_row, prompt_owner, replica, arrived, tail, *old, start, 1, skip
        )

    shape = (rows, steps, out_weight.shape[1])
    first_own = new_part(first_tail, old_part(0, 1), 0)
    middle_old = old_part(1, middle)
    middle_own = [new_part(rest_tails[i], middle_old, 1 + i, i) for i in range(middle)]
    last_own = new_part(rest_tails[-1], old_part(blocks - 1, 1), blocks - 1)
    near = near_heads([first_own])
    two, three = far_heads(first_own, False)
    decoded = out_project(
        rank, ((0, [first_own], None), two, (1, near, None), three), out_weight, shape, 0
    )
    held = (2, 3)
    held_rows = hold(rank, held, out_weight, first_own.shape[1])
    near = near_heads(middle_own)
    two, three = far_heads(jnp.concatenate(middle_own, 0), False)
    pieces = ((0, middle_own, None), (1, near, None), two)
    partial = out_project(rank, pieces, out_weight, shape, 0, final=False)
    decoded = out_project(
        rank, (three,), held_rows, shape, first, partial=partial, into=decoded, held=held
    )
    near = near_heads([last_own])
    two, three = far_heads(last_own, True)
    pieces = ((0, [last_own], None), (1, near, None))
    partial = out_project(rank, pieces, out_weight, shape, 0, final=False)
    return out_project(
        rank, (two, three), held_rows, shape, first * (blocks - 1),
        partial=partial, into=decoded, held=held,
    )


def solution(mesh):
    in_specs = (
        P("parts"),
        P(("parts", "replica")),
        P("parts"),
        P("parts"),
        P(("parts", "replica"), "tensor"),
        P(("parts", "replica"), None, "tensor"),
        P(("parts", "replica"), None, "tensor"),
        P("tensor", None),
        P("tensor", None),
        P(None, "tensor"),
        P("tensor", "parts", None, None),
    )
    out_specs = P(("parts", "replica"), None, "tensor")
    return jax.shard_map(
        on_device, mesh=mesh, in_specs=in_specs, out_specs=out_specs, check_vma=False
    )
```

```python
import functools
import math

import jax
import jax.numpy as jnp
from jax import lax
from jax.experimental import pallas as pl
from jax.experimental.pallas import tpu as pltpu
from jax.sharding import PartitionSpec as P


HD = 128
rope_base = 1000000.0
LOG2E = math.log2(math.e)
HIDDEN = -1e30


def rotary(vectors, places):
    half = vectors.shape[-1] // 2
    freq = rope_base ** (-(2.0 / vectors.shape[-1]) * jnp.arange(half, dtype=jnp.float32))
    angle = places.astype(jnp.float32)[..., None, None] * freq
    cosine = jnp.cos(angle)
    sine = jnp.sin(angle)
    first = vectors[..., :half]
    second = vectors[..., half:]
    return jnp.concatenate([first * cosine - second * sine, second * cosine + first * sine], -1)


def rotate_round(summed, places, kv_heads):
    number = summed.shape[0]
    turned = rotary(summed[:, : kv_heads * HD].reshape(number, kv_heads, HD), places)
    turned = turned.astype(jnp.bfloat16).reshape(number, kv_heads * HD)
    return jnp.concatenate([turned, summed[:, kv_heads * HD :].astype(jnp.bfloat16)], 1)


def own_pair(packed, head_group, kv_heads):
    key_part = lax.dynamic_slice_in_dim(packed, head_group * HD, HD, 1)
    value_part = lax.dynamic_slice_in_dim(packed, (kv_heads + head_group) * HD, HD, 1)
    return jnp.concatenate([key_part, value_part], 1)


NT = (((1,), (1,)), ((), ()))
SMALL = pltpu.CompilerParams(vmem_limit_bytes=24 << 20)
LARGE = pltpu.CompilerParams(vmem_limit_bytes=36 << 20)
SET_ROWS = 32
SPAN_GROUP = 2
PAGE_GROUP = 3


def in_hbm(x):
    return pltpu.with_memory_space_constraint(x, pltpu.HBM)


def lane_tiles(combine, x):
    out = x[..., :HD]
    for i in range(1, x.shape[-1] // HD):
        out = combine(out, x[..., i * HD : (i + 1) * HD])
    return out


ON_CHIP = pl.BlockSpec(memory_space=pltpu.VMEM)


def stacked_heads(q_ref, heads, block, direct, start):
    at = start * block if direct else 0
    m = block * q_ref.shape[1]
    q = q_ref[at : at + block].reshape(m, heads * HD)
    return jnp.concatenate([q[:, h * HD : (h + 1) * HD] for h in range(heads)], 0)


def softmax_parts(qs, heads, parts, scale2, s_ref):
    m = qs.shape[0] // heads
    top = None
    at = 0
    for n, load, bias in parts:
        s = lax.dot_general(qs, load()[:, :HD], NT, preferred_element_type=jnp.float32)
        s = s.reshape(heads, m, n) * scale2 + bias()[None]
        s_ref[:, :, at : at + n] = s
        most = lane_tiles(jnp.maximum, s)
        top = most if top is None else jnp.maximum(top, most)
        at += n
    top = jnp.max(top, -1, keepdims=True)
    total = mixed = None
    at = 0
    for n, load, _ in parts:
        w = jnp.exp2(s_ref[:, :, at : at + n] - top)
        summed = lane_tiles(jnp.add, w)
        one = jnp.dot(
            w.astype(jnp.bfloat16).reshape(heads * m, n),
            load()[:, HD:],
            preferred_element_type=jnp.float32,
        ).reshape(heads, m, HD)
        total = summed if total is None else total + summed
        mixed = one if mixed is None else mixed + one
        at += n
    return top, jnp.sum(total, -1, keepdims=True), mixed


def by_row(values, first, rows, steps):
    lane = lax.broadcasted_iota(jnp.int32, (rows, values.shape[1]), 1)
    row = lax.broadcasted_iota(jnp.int32, (rows, values.shape[1]), 0)
    mine = jnp.where(lane == first + row // steps, values.astype(jnp.float32), 0.0)
    return jnp.sum(mine, 1, keepdims=True)


def shown(allowed):
    return jnp.where(allowed, 0.0, HIDDEN)


def cached_kernel(
    heads, block, direct, cpages, scale2, start, table_ref, length_ref, q_ref, fork_ref, pool_ref, mixed_ref, stat_ref, s_ref
):
    qs = stacked_heads(q_ref, heads, block, direct, start)
    m = qs.shape[0] // heads
    steps = q_ref.shape[1]
    prompt = by_row(fork_ref[...], (pl.program_id(0) + start) * block, m, steps)
    pages, size = pool_ref.shape[:2]
    group = PAGE_GROUP

    def part(at):
        mine = range(at, min(at + group, pages))

        def load():
            return jnp.concatenate([pool_ref[table_ref[i]] for i in mine], 0)

        def bias():
            lane = lax.broadcasted_iota(jnp.int32, (m, size), 1)
            return jnp.concatenate(
                [
                    shown(
                        (prompt == float(i // cpages))
                        & (lane < length_ref[i // cpages] - (i % cpages) * size)
                    )
                    for i in mine
                ],
                1,
            )

        return len(mine) * size, load, bias

    parts = [part(at) for at in range(0, pages, group)]
    top, total, mixed = softmax_parts(qs, heads, parts, scale2, s_ref)
    mixed_ref[...] = mixed
    lane = lax.broadcasted_iota(jnp.int32, mixed.shape, 2)
    stat_ref[...] = jnp.where(lane < HD // 2, top, total)


def new_kernel(
    heads, block, direct, skip, steps, scale2, start, owner_ref, base_ref, q_ref, fork_ref, tail_ref, mixed_ref, stat_ref, *refs
):
    span_refs, o_ref, s_ref = refs[:-2], refs[-2], refs[-1]
    qs = stacked_heads(q_ref, heads, block, direct, start)
    m = qs.shape[0] // heads
    span = span_refs[0].shape[0]
    prompt = by_row(fork_ref[...], (pl.program_id(0) + start) * block, m, steps)
    at = skip * m if direct else 0
    mine = slice(at, at + m)

    def spans(mine):
        def load():
            return jnp.concatenate([span_refs[j][...] for j in mine], 0)

        def bias():
            owners = [owner_ref[base_ref[0] ^ j].astype(jnp.float32) for j in mine]
            return jnp.concatenate(
                [jnp.broadcast_to(shown(prompt == owner), (m, span)) for owner in owners], 1
            )

        return span * len(mine), load, bias

    def causal():
        row = lax.broadcasted_iota(jnp.int32, (m, m), 0)
        col = lax.broadcasted_iota(jnp.int32, (m, m), 1)
        return shown((row // steps == col // steps) & (col <= row))

    count = len(span_refs)
    parts = [
        spans(range(at, min(at + SPAN_GROUP, count))) for at in range(0, count, SPAN_GROUP)
    ]
    parts.append((m, lambda: tail_ref[...], causal))
    top, total, mixed = softmax_parts(qs, heads, parts, scale2, s_ref)
    old_top = stat_ref[:, mine, :1]
    old_total = stat_ref[:, mine, HD // 2 : HD // 2 + 1]
    both = jnp.maximum(top, old_top)
    new_share = jnp.exp2(top - both)
    old_share = jnp.exp2(old_top - both)
    total = total * new_share + old_total * old_share
    mixed = mixed * new_share + mixed_ref[:, mine, :] * old_share
    out = (mixed / total).astype(jnp.bfloat16)
    for h in range(heads):
        o_ref[:, h * HD : (h + 1) * HD] = out[h]


def attend_cached(q, fork_row, page_table, prompt_length, pool, start, count):
    steps, width = q.shape[1:]
    heads = width // HD
    block = min(SET_ROWS, q.shape[0])
    m = block * steps
    cached = pool.shape[0] * pool.shape[1]
    cpages = pool.shape[0] // prompt_length.shape[0]
    direct = count == 1
    return pl.pallas_call(
        functools.partial(cached_kernel, heads, block, direct, cpages, LOG2E / math.sqrt(HD), start),
        grid_spec=pltpu.PrefetchScalarGridSpec(
            num_scalar_prefetch=2,
            grid=(count,),
            in_specs=[ON_CHIP] * 3
            if direct
            else [
                pl.BlockSpec((block, steps, width), lambda i, *_: (i + start, 0, 0)),
                pl.BlockSpec(fork_row.shape, lambda i, *_: (0, 0)),
                pl.BlockSpec(pool.shape, lambda i, *_: (0, 0, 0)),
            ],
            out_specs=[ON_CHIP] * 2
            if direct
            else [pl.BlockSpec((heads, m, HD), lambda i, *_: (0, i, 0))] * 2,
            scratch_shapes=[pltpu.VMEM((heads, m, cached), jnp.float32)],
        ),
        out_shape=[jax.ShapeDtypeStruct((heads, m * count, HD), jnp.float32)] * 2,
        cost_estimate=pl.CostEstimate(
            flops=4 * count * heads * m * cached * HD,
            transcendentals=count * heads * m * cached,
            bytes_accessed=8 * count * heads * m * HD,
        ),
        compiler_params=SMALL,
        name="attend_cached",
    )(page_table, prompt_length, q, fork_row, pool)


def attend_new(q, fork_row, owner, base, span_pairs, tail_pairs, mixed, stat, start, count, skip=0):
    steps, width = q.shape[1:]
    heads = width // HD
    block = min(SET_ROWS, q.shape[0])
    m = block * steps
    span = span_pairs[0].shape[0]
    keys = span * len(span_pairs)
    direct = count == 1
    part = pl.BlockSpec((heads, m, HD), lambda i, *_: (0, i + skip, 0))
    return pl.pallas_call(
        functools.partial(new_kernel, heads, block, direct, skip, steps, LOG2E / math.sqrt(HD), start),
        grid_spec=pltpu.PrefetchScalarGridSpec(
            num_scalar_prefetch=2,
            grid=(count,),
            in_specs=[ON_CHIP] * (5 + len(span_pairs))
            if direct
            else [
                pl.BlockSpec((block, steps, width), lambda i, *_: (i + start, 0, 0)),
                pl.BlockSpec(fork_row.shape, lambda i, *_: (0, 0)),
                pl.BlockSpec((m, 2 * HD), lambda i, *_: (i, 0)),
                part,
                part,
            ]
            + [pl.BlockSpec((span, 2 * HD), lambda i, *_: (0, 0))] * len(span_pairs),
            out_specs=ON_CHIP if direct else pl.BlockSpec((m, width), lambda i, *_: (i, 0)),
            scratch_shapes=[pltpu.VMEM((heads, m, keys + m), jnp.float32)],
        ),
        out_shape=jax.ShapeDtypeStruct((m * count, width), jnp.bfloat16),
        cost_estimate=pl.CostEstimate(
            flops=4 * count * heads * m * (keys + m) * HD,
            transcendentals=count * heads * m * (keys + m),
            bytes_accessed=10 * count * heads * m * HD,
        ),
        compiler_params=SMALL,
        name="attend_new",
    )(owner, base, q, fork_row, tail_pairs, mixed, stat, *span_pairs)


def project_kernel(groups, split, kept, sent, rank_ref, *refs):
    keep_ref, send_ref, acc = refs[-3:]
    s = pl.program_id(0)
    rows = [ref[...].reshape(-1, ref.shape[-1]) for ref in refs[:groups]]
    x = rows[0] if groups == 1 else jnp.concatenate(rows, 0)
    refs = refs[groups:]
    w = jnp.concatenate(
        [jnp.concatenate([refs[2 * i][...], refs[2 * i + 1][...]], 1) for i in range(split)], 0
    )
    one = jnp.dot(x, w, preferred_element_type=jnp.float32)

    @pl.when(s == 0)
    def _():
        acc[...] = one

    @pl.when(s > 0)
    def _():
        acc[...] += one

    @pl.when(s == pl.num_programs(0) - 1)
    def _():
        keys = acc.shape[1] // 2
        for ref, rels in ((send_ref, sent), (keep_ref, kept)):
            for i, rel in enumerate(rels):
                at = pl.multiple_of((rank_ref[0] ^ rel) * HD, HD)
                ref[i, :, :HD] = acc[:, pl.ds(at, HD)].astype(ref.dtype)
                ref[i, :, HD:] = acc[:, pl.ds(pl.multiple_of(at + keys, HD), HD)].astype(ref.dtype)


def project(rank, groups, key_weight, value_weight, kept, sent):
    width, columns = key_weight.shape
    depth, split = width // 2, 2
    in_specs = []
    n = 0
    for x, start, rows in groups:
        lead = (rows,) + x.shape[1:-1]
        n += math.prod(lead)
        in_specs.append(
            pl.BlockSpec(
                tuple(pl.Element(d) for d in lead + (depth,)),
                lambda s, r, start=start, lead=lead: (start,) + (0,) * (len(lead) - 1) + (s * depth,),
            )
        )
    for i in range(split):
        piece = pl.BlockSpec((depth // split, columns), lambda s, r, i=i: (s * split + i, 0))
        in_specs += [piece, piece]
    return pl.pallas_call(
        functools.partial(project_kernel, len(groups), split, kept, sent),
        grid_spec=pltpu.PrefetchScalarGridSpec(
            num_scalar_prefetch=1,
            grid=(width // depth,),
            in_specs=in_specs,
            out_specs=[
                pl.BlockSpec((len(rels), n, 2 * HD), lambda s, r: (0, 0, 0)) for rels in (kept, sent)
            ],
            scratch_shapes=[pltpu.VMEM((n, 2 * columns), jnp.float32)],
        ),
        out_shape=[
            jax.ShapeDtypeStruct((len(kept), n, 2 * HD), jnp.float32),
            jax.ShapeDtypeStruct((len(sent), n, 2 * HD), jnp.bfloat16),
        ],
        cost_estimate=pl.CostEstimate(
            flops=4 * n * width * columns, transcendentals=0, bytes_accessed=4 * width * columns
        ),
        compiler_params=SMALL,
        name="project",
    )(
        rank,
        *[in_hbm(x) for x, _, _ in groups],
        *([in_hbm(key_weight), in_hbm(value_weight)] * split),
    )


def finish_kernel(
    span, steps, start, sizes, owner_ref, length_ref, replica_ref, fork_ref, freq_ref, keep_ref, *refs
):
    outs = refs[-len(sizes) :]
    summed = keep_ref[0]
    for ref in refs[: -len(sizes)]:
        summed = summed + (ref[0] if len(ref.shape) == 3 else ref[...]).astype(jnp.float32)
    n = summed.shape[0]
    fork = fork_ref[...]
    lengths = jnp.zeros_like(fork)
    for p in range(length_ref.shape[0]):
        lengths = jnp.where(fork == p, length_ref[p], lengths)
    lead = max(0, span - start)
    places = []
    if lead:
        own = length_ref[owner_ref[replica_ref[0]]]
        places.append(own + start + lax.broadcasted_iota(jnp.int32, (lead, 1), 0).astype(jnp.int32))
        places[0] = places[0].astype(jnp.float32)
    tail = n - lead
    first = start + lead - span
    step = lax.broadcasted_iota(jnp.int32, (tail, 1), 0) % steps
    places.append(
        by_row(lengths, first // steps, tail, steps) + (span + step).astype(jnp.float32)
    )
    places = places[0] if len(places) == 1 else jnp.concatenate(places, 0)
    angle = places * freq_ref[...]
    lane = lax.broadcasted_iota(jnp.int32, (n, HD), 1)
    sine = jnp.where(lane < HD // 2, -jnp.sin(angle), jnp.sin(angle))
    keys = summed[:, :HD]
    turned = keys * jnp.cos(angle) + pltpu.roll(keys, HD // 2, 1) * sine
    at = 0
    for size, o_ref in zip(sizes, outs):
        o_ref[:, :HD] = turned[at : at + size].astype(jnp.bfloat16)
        o_ref[:, HD:] = summed[at : at + size, HD:].astype(jnp.bfloat16)
        at += size


def finish(keep, others, places, start, sizes):
    span, steps, owner, length, replica, fork_row, freq = places
    return pl.pallas_call(
        functools.partial(finish_kernel, span, steps, start, sizes),
        grid_spec=pltpu.PrefetchScalarGridSpec(
            num_scalar_prefetch=3,
            grid=(1,),
            in_specs=[ON_CHIP] * (3 + len(others)),
            out_specs=[ON_CHIP] * len(sizes),
        ),
        out_shape=[jax.ShapeDtypeStruct((size, 2 * HD), jnp.bfloat16) for size in sizes],
        compiler_params=SMALL,
        name="finish",
    )(owner, length, replica, fork_row, freq, keep, *others)


def swap(x, axis, bit):
    return lax.ppermute(x, axis, [(i, i ^ bit) for i in range(lax.axis_size(axis))])


def swap_sum(keep, send, places, start, sizes):
    got = swap(send, "tensor", 1)
    half = (keep[1] + got[1].astype(jnp.float32)).astype(jnp.bfloat16)
    last = swap(half, "tensor", 2)
    return finish(keep, (got, last), places, start, sizes)


def out_kernel(rels, shapes, cuts, add, held, rank_ref, *refs):
    refs = list(refs)
    pieces = [([refs.pop(0) for _ in range(n)], refs.pop(0) if outer else None) for n, outer in shapes]
    partial = refs.pop(0) if add else None
    w_ref = refs[0]
    o_ref, buf, sem = (refs[-1], None, None) if held else refs[-3:]
    width = pieces[0][0][0].shape[1]
    depth = width // cuts
    rank = rank_ref[0]
    inner = (rank == 1) | (rank == 2)
    copies = []
    for p, rel in enumerate(() if held else rels):
        for c in range(cuts):
            row = pl.multiple_of((rank ^ rel) * width + c * depth, depth)
            slot = p * cuts + c
            copies.append(
                pltpu.make_async_copy(w_ref.at[pl.ds(row, depth), :], buf.at[slot], sem.at[slot])
            )
            copies[-1].start()
    total = partial[...] if add else None
    for p, (groups, outer) in enumerate(pieces):
        a = [ref[...] for ref in groups]
        a = a[0] if len(a) == 1 else jnp.concatenate(a, 0)
        if outer is not None:
            a = jnp.where(inner, a, outer[...])
        for c in range(cuts):
            if held:
                at = held.index(rels[p]) * width + c * depth
                w = w_ref[at : at + depth, :]
            else:
                copies[p * cuts + c].wait()
                w = buf[p * cuts + c]
            one = jnp.dot(
                a[:, c * depth : (c + 1) * depth], w, preferred_element_type=jnp.float32
            )
            total = one if total is None else total + one
    o_ref[...] = total.reshape(o_ref.shape).astype(o_ref.dtype)


def out_project(rank, pieces, weight, shape, start, partial=None, into=None, final=True, held=()):
    width = pieces[0][1][0].shape[1]
    m = sum(x.shape[0] for x in pieces[0][1])
    columns = weight.shape[1]
    steps = shape[1]
    cuts = 1 if held else 4
    flat = lambda x: pl.BlockSpec(x.shape, lambda i, r: (0, 0))
    args = []
    for _, groups, outer in pieces:
        args += list(groups) + ([] if outer is None else [outer])
    if partial is not None:
        args.append(partial)
    in_specs = [flat(x) for x in args]
    args.append(weight if held else in_hbm(weight))
    in_specs.append(pl.BlockSpec(memory_space=pltpu.VMEM if held else pl.ANY))
    aliases = {}
    if into is not None:
        args.append(into)
        in_specs.append(pl.BlockSpec(memory_space=pl.ANY))
        aliases = {len(args): 0}
    if final:
        out_spec = pl.BlockSpec(
            (pl.Element(m // steps), pl.Element(steps), pl.Element(columns)),
            lambda i, r: (start, 0, 0),
        )
        out_shape = jax.ShapeDtypeStruct(shape, jnp.bfloat16)
    else:
        out_spec = pl.BlockSpec((m, columns), lambda i, r: (0, 0))
        out_shape = jax.ShapeDtypeStruct((m, columns), jnp.float32)
    rels = tuple(rel for rel, _, _ in pieces)
    shapes = tuple((len(groups), outer is not None) for _, groups, outer in pieces)
    slots = len(rels) * cuts
    return pl.pallas_call(
        functools.partial(out_kernel, rels, shapes, cuts, partial is not None, held),
        grid_spec=pltpu.PrefetchScalarGridSpec(
            num_scalar_prefetch=1,
            grid=(1,),
            in_specs=in_specs,
            out_specs=out_spec,
            scratch_shapes=[]
            if held
            else [
                pltpu.VMEM((slots, width // cuts, columns), jnp.bfloat16),
                pltpu.SemaphoreType.DMA((slots,)),
            ],
        ),
        out_shape=out_shape,
        input_output_aliases=aliases,
        cost_estimate=pl.CostEstimate(
            flops=2 * m * width * columns * len(rels),
            transcendentals=0,
            bytes_accessed=2 * width * columns * len(rels),
        ),
        compiler_params=LARGE,
        name="out_project",
    )(rank, *args)


def hold_kernel(rels, rank_ref, w_ref, o_ref, sem):
    rows = o_ref.shape[0] // len(rels)
    copies = []
    for i, rel in enumerate(rels):
        at = pl.multiple_of((rank_ref[0] ^ rel) * rows, rows)
        copies.append(
            pltpu.make_async_copy(
                w_ref.at[pl.ds(at, rows), :], o_ref.at[i * rows : (i + 1) * rows, :], sem.at[i]
            )
        )
        copies[-1].start()
    for copy in copies:
        copy.wait()


def hold(rank, rels, weight, rows):
    held = pl.pallas_call(
        functools.partial(hold_kernel, rels),
        grid_spec=pltpu.PrefetchScalarGridSpec(
            num_scalar_prefetch=1,
            grid=(1,),
            in_specs=[pl.BlockSpec(memory_space=pl.ANY)],
            out_specs=pl.BlockSpec(memory_space=pltpu.VMEM),
            scratch_shapes=[pltpu.SemaphoreType.DMA((len(rels),))],
        ),
        out_shape=jax.ShapeDtypeStruct((len(rels) * rows, weight.shape[1]), weight.dtype),
        compiler_params=SMALL,
        name="hold",
    )(rank, in_hbm(weight))
    return pltpu.with_memory_space_constraint(held, pltpu.VMEM)


def near_heads(groups):
    near = []
    for group in groups:
        near.append(swap(group, "tensor", 1))
    return near


def far_heads(own, relay):
    outward = [(1, 0), (2, 3)]
    far = lax.ppermute(own, "tensor", [(0, 2), (3, 1)]) if relay else swap(own, "tensor", 2)
    across = lax.ppermute(own, "tensor", [(1, 2), (2, 1)])
    forward = None
    if relay:
        forward = lax.ppermute(across, "tensor", outward)
    passed = lax.ppermute(far, "tensor", outward)
    return (2, [far], forward), (3, [across], passed)


def on_device(
    prompt_owner,
    fork_map,
    page_table,
    prompt_length,
    span_states,
    decode_states,
    decode_queries,
    key_weight,
    value_weight,
    out_weight,
    page_pool,
):
    replica = lax.axis_index("replica")
    device_rank = lax.axis_index("tensor")
    n_replica = lax.axis_size("replica")
    n_tensor = lax.axis_size("tensor")
    span = span_states.shape[0]
    rows, steps, width = decode_states.shape
    kv_heads = key_weight.shape[1] // HD
    sharing = n_tensor // kv_heads
    prompts = jnp.arange(n_replica, dtype=jnp.int32)
    own_prompt = jnp.sum(jnp.where(prompts == replica, prompt_owner, 0))
    own_length = jnp.sum(jnp.where(prompts == own_prompt, prompt_length, 0))
    row_hits = fork_map[:, None] == prompts[None, :]
    row_length = jnp.sum(jnp.where(row_hits, prompt_length[None, :], 0), 1)
    span_places = own_length + jnp.arange(span, dtype=jnp.int32)
    tail_places = (
        row_length[:, None] + span + jnp.arange(steps, dtype=jnp.int32)[None, :]
    ).reshape(-1)
    pool = page_pool.reshape(page_pool.shape[1:])
    short_line = n_tensor == kv_heads == 4 and n_replica == 4
    first = min(SET_ROWS, rows)
    blocks = rows // first

    if not short_line:
        positions = jnp.concatenate([span_places, tail_places])
        tokens = jnp.concatenate([span_states, decode_states.reshape(rows * steps, width)], 0)
        projected = jnp.dot(
            tokens,
            jnp.concatenate([key_weight, value_weight], 1),
            preferred_element_type=jnp.float32,
        )
        share = lax.psum_scatter(projected, "tensor", scatter_dimension=0, tiled=True)
        number = share.shape[0]
        places = lax.dynamic_slice_in_dim(positions, device_rank * number, number)
        turned = rotate_round(share, places, kv_heads)
        groups = jnp.stack([own_pair(turned, g, kv_heads) for g in range(kv_heads)], 0)
        outgoing = jnp.repeat(groups, sharing, axis=0)
        paired = lax.all_to_all(
            outgoing, "tensor", split_axis=0, concat_axis=1, tiled=True
        ).reshape(-1, 2 * HD)
        arrived = lax.all_gather(paired[:span], "replica", axis=0, tiled=True)
        mixed, stat = attend_cached(
            decode_queries, fork_map[None, :], page_table, prompt_length, pool, 0, blocks
        )
        own = attend_new(
            decode_queries,
            fork_map[None, :],
            prompt_owner,
            jnp.zeros((1,), jnp.int32),
            jnp.split(arrived, n_replica),
            paired[span:],
            mixed,
            stat,
            0,
            blocks,
        )
        decoded = jnp.dot(
            lax.all_gather(own, "tensor", axis=1, tiled=True),
            out_weight,
            preferred_element_type=jnp.float32,
        )
        return decoded.astype(jnp.bfloat16).reshape(rows, steps, out_weight.shape[1])

    rank = device_rank.reshape(1).astype(jnp.int32)
    return line_of_four(
        rank, replica.reshape(1).astype(jnp.int32), prompt_owner, fork_map, page_table,
        prompt_length, span_states, decode_states, decode_queries, key_weight, value_weight,
        out_weight, pool,
    )


def line_of_four(
    rank, replica, prompt_owner, fork_map, page_table, prompt_length, span_states, decode_states,
    decode_queries, key_weight, value_weight, out_weight, pool,
):
    n_replica = lax.axis_size("replica")
    span = span_states.shape[0]
    rows, steps, _ = decode_states.shape
    first = min(SET_ROWS, rows)
    blocks = rows // first
    middle = blocks - 2
    cut = first * steps

    first_units = project(
        rank, ((span_states, 0, span), (decode_states, 0, first)), key_weight, value_weight,
        (0, 2), (1, 3),
    )
    rest_units = project(
        rank, ((decode_states, first, rows - first),), key_weight, value_weight, (0, 2), (1, 3)
    )
    fork_row = fork_map[None, :]
    half = rope_base ** (-(2.0 / HD) * jnp.arange(HD // 2, dtype=jnp.float32))
    freq = jnp.concatenate([half, half])[None, :]
    places = (span, steps, prompt_owner, prompt_length, replica, fork_row, freq)
    own_span, first_tail = swap_sum(*first_units, places, 0, (span, cut))
    arrived = [own_span]
    for j in range(1, n_replica):
        arrived.append(swap(own_span, "replica", j))
    rest_tails = swap_sum(*rest_units, places, span + cut, (cut,) * (blocks - 1))

    def old_part(start, count):
        return attend_cached(
            decode_queries, fork_row, page_table, prompt_length, pool, start, count
        )

    def new_part(tail, old, start, skip=0):
        return attend_new(
            decode_queries, fork_row, prompt_owner, replica, arrived, tail, *old, start, 1, skip
        )

    shape = (rows, steps, out_weight.shape[1])
    first_own = new_part(first_tail, old_part(0, 1), 0)
    middle_old = old_part(1, middle)
    middle_own = [new_part(rest_tails[i], middle_old, 1 + i, i) for i in range(middle)]
    last_own = new_part(rest_tails[-1], old_part(blocks - 1, 1), blocks - 1)
    near = near_heads([first_own])
    two, three = far_heads(first_own, False)
    decoded = out_project(
        rank, ((0, [first_own], None), two, (1, near, None), three), out_weight, shape, 0
    )
    held = (2, 3)
    held_rows = hold(rank, held, out_weight, first_own.shape[1])
    near = near_heads(middle_own)
    two, three = far_heads(jnp.concatenate(middle_own, 0), False)
    pieces = ((0, middle_own, None), (1, near, None), two)
    partial = out_project(rank, pieces, out_weight, shape, 0, final=False)
    decoded = out_project(
        rank, (three,), held_rows, shape, first, partial=partial, into=decoded, held=held
    )
    near = near_heads([last_own])
    two, three = far_heads(last_own, True)
    pieces = ((0, [last_own], None), (1, near, None))
    partial = out_project(rank, pieces, out_weight, shape, 0, final=False)
    partial = out_project(
        rank, (two,), held_rows, shape, 0, partial=partial, final=False, held=held
    )
    return out_project(
        rank, (three,), held_rows, shape, first * (blocks - 1),
        partial=partial, into=decoded, held=held,
    )


def solution(mesh):
    in_specs = (
        P("parts"),
        P(("parts", "replica")),
        P("parts"),
        P("parts"),
        P(("parts", "replica"), "tensor"),
        P(("parts", "replica"), None, "tensor"),
        P(("parts", "replica"), None, "tensor"),
        P("tensor", None),
        P("tensor", None),
        P(None, "tensor"),
        P("tensor", "parts", None, None),
    )
    out_specs = P(("parts", "replica"), None, "tensor")
    return jax.shard_map(
        on_device, mesh=mesh, in_specs=in_specs, out_specs=out_specs, check_vma=False
    )
```

```python
import functools
import math

import jax
import jax.numpy as jnp
from jax import lax
from jax.experimental import pallas as pl
from jax.experimental.pallas import tpu as pltpu
from jax.sharding import PartitionSpec as P


HD = 128
rope_base = 1000000.0
LOG2E = math.log2(math.e)
HIDDEN = -1e30


def rotary(vectors, places):
    half = vectors.shape[-1] // 2
    freq = rope_base ** (-(2.0 / vectors.shape[-1]) * jnp.arange(half, dtype=jnp.float32))
    angle = places.astype(jnp.float32)[..., None, None] * freq
    cosine = jnp.cos(angle)
    sine = jnp.sin(angle)
    first = vectors[..., :half]
    second = vectors[..., half:]
    return jnp.concatenate([first * cosine - second * sine, second * cosine + first * sine], -1)


def rotate_round(summed, places, kv_heads):
    number = summed.shape[0]
    turned = rotary(summed[:, : kv_heads * HD].reshape(number, kv_heads, HD), places)
    turned = turned.astype(jnp.bfloat16).reshape(number, kv_heads * HD)
    return jnp.concatenate([turned, summed[:, kv_heads * HD :].astype(jnp.bfloat16)], 1)


def own_pair(packed, head_group, kv_heads):
    key_part = lax.dynamic_slice_in_dim(packed, head_group * HD, HD, 1)
    value_part = lax.dynamic_slice_in_dim(packed, (kv_heads + head_group) * HD, HD, 1)
    return jnp.concatenate([key_part, value_part], 1)


NT = (((1,), (1,)), ((), ()))
SMALL = pltpu.CompilerParams(vmem_limit_bytes=24 << 20)
LARGE = pltpu.CompilerParams(vmem_limit_bytes=36 << 20)
SET_ROWS = 32
SPAN_GROUP = 2
PAGE_GROUP = 3


def in_hbm(x):
    return pltpu.with_memory_space_constraint(x, pltpu.HBM)


def lane_tiles(combine, x):
    out = x[..., :HD]
    for i in range(1, x.shape[-1] // HD):
        out = combine(out, x[..., i * HD : (i + 1) * HD])
    return out


ON_CHIP = pl.BlockSpec(memory_space=pltpu.VMEM)


def stacked_heads(q_ref, heads, block, direct, start):
    at = start * block if direct else 0
    m = block * q_ref.shape[1]
    q = q_ref[at : at + block].reshape(m, heads * HD)
    return jnp.concatenate([q[:, h * HD : (h + 1) * HD] for h in range(heads)], 0)


def softmax_parts(qs, heads, parts, scale2, s_ref):
    m = qs.shape[0] // heads
    top = None
    at = 0
    for n, load, bias in parts:
        s = lax.dot_general(qs, load()[:, :HD], NT, preferred_element_type=jnp.float32)
        s = s.reshape(heads, m, n) * scale2 + bias()[None]
        s_ref[:, :, at : at + n] = s
        most = lane_tiles(jnp.maximum, s)
        top = most if top is None else jnp.maximum(top, most)
        at += n
    top = jnp.max(top, -1, keepdims=True)
    total = mixed = None
    at = 0
    for n, load, _ in parts:
        w = jnp.exp2(s_ref[:, :, at : at + n] - top)
        summed = lane_tiles(jnp.add, w)
        one = jnp.dot(
            w.astype(jnp.bfloat16).reshape(heads * m, n),
            load()[:, HD:],
            preferred_element_type=jnp.float32,
        ).reshape(heads, m, HD)
        total = summed if total is None else total + summed
        mixed = one if mixed is None else mixed + one
        at += n
    return top, jnp.sum(total, -1, keepdims=True), mixed


def by_row(values, first, rows, steps):
    lane = lax.broadcasted_iota(jnp.int32, (rows, values.shape[1]), 1)
    row = lax.broadcasted_iota(jnp.int32, (rows, values.shape[1]), 0)
    mine = jnp.where(lane == first + row // steps, values.astype(jnp.float32), 0.0)
    return jnp.sum(mine, 1, keepdims=True)


def shown(allowed):
    return jnp.where(allowed, 0.0, HIDDEN)


def cached_kernel(
    heads, block, direct, cpages, scale2, start, table_ref, length_ref, q_ref, fork_ref, pool_ref, mixed_ref, stat_ref, s_ref
):
    qs = stacked_heads(q_ref, heads, block, direct, start)
    m = qs.shape[0] // heads
    steps = q_ref.shape[1]
    prompt = by_row(fork_ref[...], (pl.program_id(0) + start) * block, m, steps)
    pages, size = pool_ref.shape[:2]
    group = PAGE_GROUP

    def part(at):
        mine = range(at, min(at + group, pages))

        def load():
            return jnp.concatenate([pool_ref[table_ref[i]] for i in mine], 0)

        def bias():
            lane = lax.broadcasted_iota(jnp.int32, (m, size), 1)
            return jnp.concatenate(
                [
                    shown(
                        (prompt == float(i // cpages))
                        & (lane < length_ref[i // cpages] - (i % cpages) * size)
                    )
                    for i in mine
                ],
                1,
            )

        return len(mine) * size, load, bias

    parts = [part(at) for at in range(0, pages, group)]
    top, total, mixed = softmax_parts(qs, heads, parts, scale2, s_ref)
    mixed_ref[...] = mixed
    lane = lax.broadcasted_iota(jnp.int32, mixed.shape, 2)
    stat_ref[...] = jnp.where(lane < HD // 2, top, total)


def new_kernel(
    heads, block, direct, skip, steps, scale2, start, owner_ref, base_ref, q_ref, fork_ref, tail_ref, mixed_ref, stat_ref, *refs
):
    span_refs, o_ref, s_ref = refs[:-2], refs[-2], refs[-1]
    qs = stacked_heads(q_ref, heads, block, direct, start)
    m = qs.shape[0] // heads
    span = span_refs[0].shape[0]
    prompt = by_row(fork_ref[...], (pl.program_id(0) + start) * block, m, steps)
    at = skip * m if direct else 0
    mine = slice(at, at + m)

    def spans(mine):
        def load():
            return jnp.concatenate([span_refs[j][...] for j in mine], 0)

        def bias():
            owners = [owner_ref[base_ref[0] ^ j].astype(jnp.float32) for j in mine]
            return jnp.concatenate(
                [jnp.broadcast_to(shown(prompt == owner), (m, span)) for owner in owners], 1
            )

        return span * len(mine), load, bias

    def causal():
        row = lax.broadcasted_iota(jnp.int32, (m, m), 0)
        col = lax.broadcasted_iota(jnp.int32, (m, m), 1)
        return shown((row // steps == col // steps) & (col <= row))

    count = len(span_refs)
    parts = [
        spans(range(at, min(at + SPAN_GROUP, count))) for at in range(0, count, SPAN_GROUP)
    ]
    parts.append((m, lambda: tail_ref[...], causal))
    top, total, mixed = softmax_parts(qs, heads, parts, scale2, s_ref)
    old_top = stat_ref[:, mine, :1]
    old_total = stat_ref[:, mine, HD // 2 : HD // 2 + 1]
    both = jnp.maximum(top, old_top)
    new_share = jnp.exp2(top - both)
    old_share = jnp.exp2(old_top - both)
    total = total * new_share + old_total * old_share
    mixed = mixed * new_share + mixed_ref[:, mine, :] * old_share
    out = (mixed / total).astype(jnp.bfloat16)
    for h in range(heads):
        o_ref[:, h * HD : (h + 1) * HD] = out[h]


def attend_cached(q, fork_row, page_table, prompt_length, pool, start, count):
    steps, width = q.shape[1:]
    heads = width // HD
    block = min(SET_ROWS, q.shape[0])
    m = block * steps
    cached = pool.shape[0] * pool.shape[1]
    cpages = pool.shape[0] // prompt_length.shape[0]
    direct = count == 1
    return pl.pallas_call(
        functools.partial(cached_kernel, heads, block, direct, cpages, LOG2E / math.sqrt(HD), start),
        grid_spec=pltpu.PrefetchScalarGridSpec(
            num_scalar_prefetch=2,
            grid=(count,),
            in_specs=[ON_CHIP] * 3
            if direct
            else [
                pl.BlockSpec((block, steps, width), lambda i, *_: (i + start, 0, 0)),
                pl.BlockSpec(fork_row.shape, lambda i, *_: (0, 0)),
                pl.BlockSpec(pool.shape, lambda i, *_: (0, 0, 0)),
            ],
            out_specs=[ON_CHIP] * 2
            if direct
            else [pl.BlockSpec((heads, m, HD), lambda i, *_: (0, i, 0))] * 2,
            scratch_shapes=[pltpu.VMEM((heads, m, cached), jnp.float32)],
        ),
        out_shape=[jax.ShapeDtypeStruct((heads, m * count, HD), jnp.float32)] * 2,
        cost_estimate=pl.CostEstimate(
            flops=4 * count * heads * m * cached * HD,
            transcendentals=count * heads * m * cached,
            bytes_accessed=8 * count * heads * m * HD,
        ),
        compiler_params=SMALL,
        name="attend_cached",
    )(page_table, prompt_length, q, fork_row, pool)


def attend_new(q, fork_row, owner, base, span_pairs, tail_pairs, mixed, stat, start, count, skip=0):
    steps, width = q.shape[1:]
    heads = width // HD
    block = min(SET_ROWS, q.shape[0])
    m = block * steps
    span = span_pairs[0].shape[0]
    keys = span * len(span_pairs)
    direct = count == 1
    part = pl.BlockSpec((heads, m, HD), lambda i, *_: (0, i + skip, 0))
    return pl.pallas_call(
        functools.partial(new_kernel, heads, block, direct, skip, steps, LOG2E / math.sqrt(HD), start),
        grid_spec=pltpu.PrefetchScalarGridSpec(
            num_scalar_prefetch=2,
            grid=(count,),
            in_specs=[ON_CHIP] * (5 + len(span_pairs))
            if direct
            else [
                pl.BlockSpec((block, steps, width), lambda i, *_: (i + start, 0, 0)),
                pl.BlockSpec(fork_row.shape, lambda i, *_: (0, 0)),
                pl.BlockSpec((m, 2 * HD), lambda i, *_: (i, 0)),
                part,
                part,
            ]
            + [pl.BlockSpec((span, 2 * HD), lambda i, *_: (0, 0))] * len(span_pairs),
            out_specs=ON_CHIP if direct else pl.BlockSpec((m, width), lambda i, *_: (i, 0)),
            scratch_shapes=[pltpu.VMEM((heads, m, keys + m), jnp.float32)],
        ),
        out_shape=jax.ShapeDtypeStruct((m * count, width), jnp.bfloat16),
        cost_estimate=pl.CostEstimate(
            flops=4 * count * heads * m * (keys + m) * HD,
            transcendentals=count * heads * m * (keys + m),
            bytes_accessed=10 * count * heads * m * HD,
        ),
        compiler_params=SMALL,
        name="attend_new",
    )(owner, base, q, fork_row, tail_pairs, mixed, stat, *span_pairs)


def project_kernel(groups, split, kept, sent, rank_ref, *refs):
    keep_ref, send_ref, acc = refs[-3:]
    s = pl.program_id(0)
    rows = [ref[...].reshape(-1, ref.shape[-1]) for ref in refs[:groups]]
    x = rows[0] if groups == 1 else jnp.concatenate(rows, 0)
    refs = refs[groups:]
    w = jnp.concatenate(
        [jnp.concatenate([refs[2 * i][...], refs[2 * i + 1][...]], 1) for i in range(split)], 0
    )
    one = jnp.dot(x, w, preferred_element_type=jnp.float32)

    @pl.when(s == 0)
    def _():
        acc[...] = one

    @pl.when(s > 0)
    def _():
        acc[...] += one

    @pl.when(s == pl.num_programs(0) - 1)
    def _():
        keys = acc.shape[1] // 2
        for ref, rels in ((send_ref, sent), (keep_ref, kept)):
            for i, rel in enumerate(rels):
                at = pl.multiple_of((rank_ref[0] ^ rel) * HD, HD)
                ref[i, :, :HD] = acc[:, pl.ds(at, HD)].astype(ref.dtype)
                ref[i, :, HD:] = acc[:, pl.ds(pl.multiple_of(at + keys, HD), HD)].astype(ref.dtype)


def project(rank, groups, key_weight, value_weight, kept, sent):
    width, columns = key_weight.shape
    depth, split = width // 2, 2
    in_specs = []
    n = 0
    for x, start, rows in groups:
        lead = (rows,) + x.shape[1:-1]
        n += math.prod(lead)
        in_specs.append(
            pl.BlockSpec(
                tuple(pl.Element(d) for d in lead + (depth,)),
                lambda s, r, start=start, lead=lead: (start,) + (0,) * (len(lead) - 1) + (s * depth,),
            )
        )
    for i in range(split):
        piece = pl.BlockSpec((depth // split, columns), lambda s, r, i=i: (s * split + i, 0))
        in_specs += [piece, piece]
    return pl.pallas_call(
        functools.partial(project_kernel, len(groups), split, kept, sent),
        grid_spec=pltpu.PrefetchScalarGridSpec(
            num_scalar_prefetch=1,
            grid=(width // depth,),
            in_specs=in_specs,
            out_specs=[
                pl.BlockSpec((len(rels), n, 2 * HD), lambda s, r: (0, 0, 0)) for rels in (kept, sent)
            ],
            scratch_shapes=[pltpu.VMEM((n, 2 * columns), jnp.float32)],
        ),
        out_shape=[
            jax.ShapeDtypeStruct((len(kept), n, 2 * HD), jnp.float32),
            jax.ShapeDtypeStruct((len(sent), n, 2 * HD), jnp.bfloat16),
        ],
        cost_estimate=pl.CostEstimate(
            flops=4 * n * width * columns, transcendentals=0, bytes_accessed=4 * width * columns
        ),
        compiler_params=SMALL,
        name="project",
    )(
        rank,
        *[in_hbm(x) for x, _, _ in groups],
        *([in_hbm(key_weight), in_hbm(value_weight)] * split),
    )


def finish_kernel(
    span, steps, start, sizes, owner_ref, length_ref, replica_ref, fork_ref, freq_ref, keep_ref, *refs
):
    outs = refs[-len(sizes) :]
    summed = keep_ref[0]
    for ref in refs[: -len(sizes)]:
        summed = summed + (ref[0] if len(ref.shape) == 3 else ref[...]).astype(jnp.float32)
    n = summed.shape[0]
    fork = fork_ref[...]
    lengths = jnp.zeros_like(fork)
    for p in range(length_ref.shape[0]):
        lengths = jnp.where(fork == p, length_ref[p], lengths)
    lead = max(0, span - start)
    places = []
    if lead:
        own = length_ref[owner_ref[replica_ref[0]]]
        places.append(own + start + lax.broadcasted_iota(jnp.int32, (lead, 1), 0).astype(jnp.int32))
        places[0] = places[0].astype(jnp.float32)
    tail = n - lead
    first = start + lead - span
    step = lax.broadcasted_iota(jnp.int32, (tail, 1), 0) % steps
    places.append(
        by_row(lengths, first // steps, tail, steps) + (span + step).astype(jnp.float32)
    )
    places = places[0] if len(places) == 1 else jnp.concatenate(places, 0)
    angle = places * freq_ref[...]
    lane = lax.broadcasted_iota(jnp.int32, (n, HD), 1)
    sine = jnp.where(lane < HD // 2, -jnp.sin(angle), jnp.sin(angle))
    keys = summed[:, :HD]
    turned = keys * jnp.cos(angle) + pltpu.roll(keys, HD // 2, 1) * sine
    at = 0
    for size, o_ref in zip(sizes, outs):
        o_ref[:, :HD] = turned[at : at + size].astype(jnp.bfloat16)
        o_ref[:, HD:] = summed[at : at + size, HD:].astype(jnp.bfloat16)
        at += size


def finish(keep, others, places, start, sizes):
    span, steps, owner, length, replica, fork_row, freq = places
    return pl.pallas_call(
        functools.partial(finish_kernel, span, steps, start, sizes),
        grid_spec=pltpu.PrefetchScalarGridSpec(
            num_scalar_prefetch=3,
            grid=(1,),
            in_specs=[ON_CHIP] * (3 + len(others)),
            out_specs=[ON_CHIP] * len(sizes),
        ),
        out_shape=[jax.ShapeDtypeStruct((size, 2 * HD), jnp.bfloat16) for size in sizes],
        compiler_params=SMALL,
        name="finish",
    )(owner, length, replica, fork_row, freq, keep, *others)


def swap(x, axis, bit):
    return lax.ppermute(x, axis, [(i, i ^ bit) for i in range(lax.axis_size(axis))])


def swap_sum(keep, send, places, start, sizes):
    got = swap(send, "tensor", 1)
    half = (keep[1] + got[1].astype(jnp.float32)).astype(jnp.bfloat16)
    last = swap(half, "tensor", 2)
    return finish(keep, (got, last), places, start, sizes)


def out_kernel(rels, shapes, cuts, add, held, rank_ref, *refs):
    refs = list(refs)
    pieces = [([refs.pop(0) for _ in range(n)], refs.pop(0) if outer else None) for n, outer in shapes]
    partial = refs.pop(0) if add else None
    w_ref = refs[0]
    o_ref, buf, sem = (refs[-1], None, None) if held else refs[-3:]
    width = pieces[0][0][0].shape[1]
    depth = width // cuts
    rank = rank_ref[0]
    inner = (rank == 1) | (rank == 2)
    copies = []
    for p, rel in enumerate(() if held else rels):
        for c in range(cuts):
            row = pl.multiple_of((rank ^ rel) * width + c * depth, depth)
            slot = p * cuts + c
            copies.append(
                pltpu.make_async_copy(w_ref.at[pl.ds(row, depth), :], buf.at[slot], sem.at[slot])
            )
            copies[-1].start()
    total = partial[...] if add else None
    for p, (groups, outer) in enumerate(pieces):
        a = [ref[...] for ref in groups]
        a = a[0] if len(a) == 1 else jnp.concatenate(a, 0)
        if outer is not None:
            a = jnp.where(inner, a, outer[...])
        for c in range(cuts):
            if held:
                at = held.index(rels[p]) * width + c * depth
                w = w_ref[at : at + depth, :]
            else:
                copies[p * cuts + c].wait()
                w = buf[p * cuts + c]
            one = jnp.dot(
                a[:, c * depth : (c + 1) * depth], w, preferred_element_type=jnp.float32
            )
            total = one if total is None else total + one
    o_ref[...] = total.reshape(o_ref.shape).astype(o_ref.dtype)


def out_project(rank, pieces, weight, shape, start, partial=None, into=None, final=True, held=()):
    width = pieces[0][1][0].shape[1]
    m = sum(x.shape[0] for x in pieces[0][1])
    columns = weight.shape[1]
    steps = shape[1]
    cuts = 1 if held else 4
    flat = lambda x: pl.BlockSpec(x.shape, lambda i, r: (0, 0))
    args = []
    for _, groups, outer in pieces:
        args += list(groups) + ([] if outer is None else [outer])
    if partial is not None:
        args.append(partial)
    in_specs = [flat(x) for x in args]
    args.append(weight if held else in_hbm(weight))
    in_specs.append(pl.BlockSpec(memory_space=pltpu.VMEM if held else pl.ANY))
    aliases = {}
    if into is not None:
        args.append(into)
        in_specs.append(pl.BlockSpec(memory_space=pl.ANY))
        aliases = {len(args): 0}
    if final:
        out_spec = pl.BlockSpec(
            (pl.Element(m // steps), pl.Element(steps), pl.Element(columns)),
            lambda i, r: (start, 0, 0),
        )
        out_shape = jax.ShapeDtypeStruct(shape, jnp.bfloat16)
    else:
        out_spec = pl.BlockSpec((m, columns), lambda i, r: (0, 0))
        out_shape = jax.ShapeDtypeStruct((m, columns), jnp.float32)
    rels = tuple(rel for rel, _, _ in pieces)
    shapes = tuple((len(groups), outer is not None) for _, groups, outer in pieces)
    slots = len(rels) * cuts
    return pl.pallas_call(
        functools.partial(out_kernel, rels, shapes, cuts, partial is not None, held),
        grid_spec=pltpu.PrefetchScalarGridSpec(
            num_scalar_prefetch=1,
            grid=(1,),
            in_specs=in_specs,
            out_specs=out_spec,
            scratch_shapes=[]
            if held
            else [
                pltpu.VMEM((slots, width // cuts, columns), jnp.bfloat16),
                pltpu.SemaphoreType.DMA((slots,)),
            ],
        ),
        out_shape=out_shape,
        input_output_aliases=aliases,
        cost_estimate=pl.CostEstimate(
            flops=2 * m * width * columns * len(rels),
            transcendentals=0,
            bytes_accessed=2 * width * columns * len(rels),
        ),
        compiler_params=LARGE,
        name="out_project",
    )(rank, *args)


def hold_kernel(rels, rank_ref, w_ref, o_ref, sem):
    rows = o_ref.shape[0] // len(rels)
    copies = []
    for i, rel in enumerate(rels):
        at = pl.multiple_of((rank_ref[0] ^ rel) * rows, rows)
        copies.append(
            pltpu.make_async_copy(
                w_ref.at[pl.ds(at, rows), :], o_ref.at[i * rows : (i + 1) * rows, :], sem.at[i]
            )
        )
        copies[-1].start()
    for copy in copies:
        copy.wait()


def hold(rank, rels, weight, rows):
    held = pl.pallas_call(
        functools.partial(hold_kernel, rels),
        grid_spec=pltpu.PrefetchScalarGridSpec(
            num_scalar_prefetch=1,
            grid=(1,),
            in_specs=[pl.BlockSpec(memory_space=pl.ANY)],
            out_specs=pl.BlockSpec(memory_space=pltpu.VMEM),
            scratch_shapes=[pltpu.SemaphoreType.DMA((len(rels),))],
        ),
        out_shape=jax.ShapeDtypeStruct((len(rels) * rows, weight.shape[1]), weight.dtype),
        compiler_params=SMALL,
        name="hold",
    )(rank, in_hbm(weight))
    return pltpu.with_memory_space_constraint(held, pltpu.VMEM)


def near_heads(groups):
    near = []
    for group in groups:
        near.append(swap(group, "tensor", 1))
    return near


def far_heads(own, relay):
    outward = [(1, 0), (2, 3)]
    far = lax.ppermute(own, "tensor", [(0, 2), (3, 1)]) if relay else swap(own, "tensor", 2)
    across = lax.ppermute(own, "tensor", [(1, 2), (2, 1)])
    forward = None
    if relay:
        forward = lax.ppermute(across, "tensor", outward)
    passed = lax.ppermute(far, "tensor", outward)
    return (2, [far], forward), (3, [across], passed)


def on_device(
    prompt_owner,
    fork_map,
    page_table,
    prompt_length,
    span_states,
    decode_states,
    decode_queries,
    key_weight,
    value_weight,
    out_weight,
    page_pool,
):
    replica = lax.axis_index("replica")
    device_rank = lax.axis_index("tensor")
    n_replica = lax.axis_size("replica")
    n_tensor = lax.axis_size("tensor")
    span = span_states.shape[0]
    rows, steps, width = decode_states.shape
    kv_heads = key_weight.shape[1] // HD
    sharing = n_tensor // kv_heads
    prompts = jnp.arange(n_replica, dtype=jnp.int32)
    own_prompt = jnp.sum(jnp.where(prompts == replica, prompt_owner, 0))
    own_length = jnp.sum(jnp.where(prompts == own_prompt, prompt_length, 0))
    row_hits = fork_map[:, None] == prompts[None, :]
    row_length = jnp.sum(jnp.where(row_hits, prompt_length[None, :], 0), 1)
    span_places = own_length + jnp.arange(span, dtype=jnp.int32)
    tail_places = (
        row_length[:, None] + span + jnp.arange(steps, dtype=jnp.int32)[None, :]
    ).reshape(-1)
    pool = page_pool.reshape(page_pool.shape[1:])
    short_line = n_tensor == kv_heads == 4 and n_replica == 4
    first = min(SET_ROWS, rows)
    blocks = rows // first

    if not short_line:
        positions = jnp.concatenate([span_places, tail_places])
        tokens = jnp.concatenate([span_states, decode_states.reshape(rows * steps, width)], 0)
        projected = jnp.dot(
            tokens,
            jnp.concatenate([key_weight, value_weight], 1),
            preferred_element_type=jnp.float32,
        )
        share = lax.psum_scatter(projected, "tensor", scatter_dimension=0, tiled=True)
        number = share.shape[0]
        places = lax.dynamic_slice_in_dim(positions, device_rank * number, number)
        turned = rotate_round(share, places, kv_heads)
        groups = jnp.stack([own_pair(turned, g, kv_heads) for g in range(kv_heads)], 0)
        outgoing = jnp.repeat(groups, sharing, axis=0)
        paired = lax.all_to_all(
            outgoing, "tensor", split_axis=0, concat_axis=1, tiled=True
        ).reshape(-1, 2 * HD)
        arrived = lax.all_gather(paired[:span], "replica", axis=0, tiled=True)
        mixed, stat = attend_cached(
            decode_queries, fork_map[None, :], page_table, prompt_length, pool, 0, blocks
        )
        own = attend_new(
            decode_queries,
            fork_map[None, :],
            prompt_owner,
            jnp.zeros((1,), jnp.int32),
            jnp.split(arrived, n_replica),
            paired[span:],
            mixed,
            stat,
            0,
            blocks,
        )
        decoded = jnp.dot(
            lax.all_gather(own, "tensor", axis=1, tiled=True),
            out_weight,
            preferred_element_type=jnp.float32,
        )
        return decoded.astype(jnp.bfloat16).reshape(rows, steps, out_weight.shape[1])

    rank = device_rank.reshape(1).astype(jnp.int32)
    return line_of_four(
        rank, replica.reshape(1).astype(jnp.int32), prompt_owner, fork_map, page_table,
        prompt_length, span_states, decode_states, decode_queries, key_weight, value_weight,
        out_weight, pool,
    )


def line_of_four(
    rank, replica, prompt_owner, fork_map, page_table, prompt_length, span_states, decode_states,
    decode_queries, key_weight, value_weight, out_weight, pool,
):
    n_replica = lax.axis_size("replica")
    span = span_states.shape[0]
    rows, steps, _ = decode_states.shape
    first = min(SET_ROWS, rows)
    blocks = rows // first
    cut = first * steps

    first_units = project(
        rank, ((span_states, 0, span), (decode_states, 0, first)), key_weight, value_weight,
        (0, 2), (1, 3),
    )
    rest_units = project(
        rank, ((decode_states, first, rows - first),), key_weight, value_weight, (0, 2), (1, 3)
    )
    fork_row = fork_map[None, :]
    half = rope_base ** (-(2.0 / HD) * jnp.arange(HD // 2, dtype=jnp.float32))
    freq = jnp.concatenate([half, half])[None, :]
    places = (span, steps, prompt_owner, prompt_length, replica, fork_row, freq)
    own_span, first_tail = swap_sum(*first_units, places, 0, (span, cut))
    arrived = [own_span]
    for j in range(1, n_replica):
        arrived.append(swap(own_span, "replica", j))
    rest_tails = swap_sum(*rest_units, places, span + cut, (cut,) * (blocks - 1))

    def old_part(start, count):
        return attend_cached(
            decode_queries, fork_row, page_table, prompt_length, pool, start, count
        )

    def new_part(tail, old, start, skip=0):
        return attend_new(
            decode_queries, fork_row, prompt_owner, replica, arrived, tail, *old, start, 1, skip
        )

    shape = (rows, steps, out_weight.shape[1])
    first_own = new_part(first_tail, old_part(0, 1), 0)
    later_old = old_part(2, blocks - 2)
    middle_own = [new_part(rest_tails[0], old_part(1, 1), 1)] + [
        new_part(rest_tails[i - 1], later_old, i, i - 2) for i in range(2, blocks - 1)
    ]
    last_own = new_part(rest_tails[-1], later_old, blocks - 1, blocks - 3)
    near = near_heads([first_own])
    two, three = far_heads(first_own, False)
    decoded = out_project(
        rank, ((0, [first_own], None), two, (1, near, None), three), out_weight, shape, 0
    )
    held = (2, 3)
    held_rows = hold(rank, held, out_weight, first_own.shape[1])
    near = near_heads(middle_own)
    two, three = far_heads(jnp.concatenate(middle_own, 0), False)
    pieces = ((0, middle_own, None), (1, near, None), two)
    partial = out_project(rank, pieces, out_weight, shape, 0, final=False)
    decoded = out_project(
        rank, (three,), held_rows, shape, first, partial=partial, into=decoded, held=held
    )
    near = near_heads([last_own])
    two, three = far_heads(last_own, True)
    pieces = ((0, [last_own], None), (1, near, None))
    partial = out_project(rank, pieces, out_weight, shape, 0, final=False)
    partial = out_project(
        rank, (two,), held_rows, shape, 0, partial=partial, final=False, held=held
    )
    return out_project(
        rank, (three,), held_rows, shape, first * (blocks - 1),
        partial=partial, into=decoded, held=held,
    )


def solution(mesh):
    in_specs = (
        P("parts"),
        P(("parts", "replica")),
        P("parts"),
        P("parts"),
        P(("parts", "replica"), "tensor"),
        P(("parts", "replica"), None, "tensor"),
        P(("parts", "replica"), None, "tensor"),
        P("tensor", None),
        P("tensor", None),
        P(None, "tensor"),
        P("tensor", "parts", None, None),
    )
    out_specs = P(("parts", "replica"), None, "tensor")
    return jax.shard_map(
        on_device, mesh=mesh, in_specs=in_specs, out_specs=out_specs, check_vma=False
    )
```
